256 devices in a mesh: bx: 8 (over z), by: 16 (over y, x), bz: 2 (over core).
Axes of the slice: x: 4, y: 4, z: 8, core: 2. Of those that a mesh axis runs over, the one named last changes fastest.
Arguments:
- velocity: float32 [2048, 3, 39304], P(('bx', 'by', 'bz')), may hold values from -5 to 5, as said below
- fraction: int32 [2048, 39304], P(('bx', 'by', 'bz')), may hold values from 0 to 256, as said below
- placement: int32 [8, 16, 2, 4], P('bx', None, 'bz'), may hold values from 0 to 15, as said below
Outputs:
- velocity_out: float32 [2048, 3, 32768], P(('bx', 'by', 'bz'))
- pressure: float32 [256, 512, 256], P('bx', 'by', 'bz')
The draws below stay inside these ranges and needn't reach their ends.
Inputs may be any that keep to these rules, and one draw needn't show every extreme that they name: placement[x, b, z, k] is the owner code c of box k of the brick (x, b, z): that box lives on the device (x, c, z). The 4 codes of one brick are distinct. Each device holds at most 8 boxes, and in every line of fixed (x, z) some device holds exactly 8. `velocity`: slot s of the device (x, y, z) holds that device's s-th box in the order of (its brick's y index, k); ghost cells equal the neighbouring cells of the grid and are zero outside it; slots beyond the device's count of boxes are zero. `fraction`: same slots and ghost layers as velocity; 256 in regular cells, 32 to 255 in cut cells, zero outside the grid and in unused slots.
All inputs are finite; a program needn't handle non-finite values.
Results may differ from the reference program's by a relative error of at most 0.0003.
Values sent between devices are 32-bit elements; how exact they have to be, the bound alone decides.
No kernel may reach another device: no remote copies, remote signals or barrier semaphores. Data moves between devices by JAX's collectives and lax.ppermute only.
A program may use at most 128 MiB of HBM per device.

```python
import jax
import jax.numpy as jnp
from jax import lax

BOX = 32
KB = 4
ITERS = 4
PAIR = 1
BOX_CAP = 8
PAD = 34
SLOTS = 2048
NX = 256
NY = 512
NZ = 256
N_BX = 8
N_BY = 16
N_BZ = 2


def line_table(key):
    lanes = N_BY
    virtual = lanes * PAIR
    crowded = 2 * KB // PAIR
    key_start, key_order = jax.random.split(key)
    start = PAIR * jax.random.randint(key_start, (), 0, lanes)
    order = jax.random.permutation(key_order, lanes)
    ranking = jnp.argsort(order).astype(jnp.int32)
    rank_col = ranking[:, None]
    number = jnp.arange(KB, dtype=jnp.int32)[None, :]
    busy_code = (start + number) % virtual
    other_code = (start + KB + ((rank_col - crowded) * KB + number) % (virtual - KB)) % virtual
    return jnp.where(rank_col < crowded, busy_code, other_code).astype(jnp.int32)


def placement_table(key):
    base = jax.random.fold_in(key, 7301)
    tables = jax.vmap(lambda line_id: line_table(jax.random.fold_in(base, line_id)))(jnp.arange(N_BX * N_BZ, dtype=jnp.int32))
    return tables.reshape(N_BX, N_BZ, N_BY, KB).transpose(0, 2, 1, 3)


def slot_starts(table):
    entries = N_BY * KB
    total_slots = N_BX * N_BY * N_BZ * BOX_CAP
    lines = (table // PAIR).transpose(0, 2, 1, 3).reshape(N_BX, N_BZ, entries)
    onehot = (lines[..., None] == jnp.arange(N_BY, dtype=jnp.int32)).astype(jnp.int32)
    ranks = jnp.sum((jnp.cumsum(onehot, axis=2) - onehot) * onehot, axis=-1)
    along_x = jnp.arange(N_BX, dtype=jnp.int32)[:, None, None]
    along_z = jnp.arange(N_BZ, dtype=jnp.int32)[None, :, None]
    slots = (((along_x * N_BY + lines) * N_BZ + along_z) * BOX_CAP + ranks).reshape(-1)
    entry_ids = jnp.arange(N_BX * N_BZ * entries, dtype=jnp.int32)
    start_x = entry_ids // (N_BZ * entries)
    start_zline = entry_ids // entries % N_BZ
    inner_id = entry_ids % entries
    starts = jnp.stack([start_x * BOX, inner_id // KB * BOX, (start_zline * KB + inner_id % KB) * BOX], axis=-1)
    slot_start = jnp.zeros((total_slots, 3), jnp.int32).at[slots].set(starts)
    live = jnp.zeros((total_slots,), jnp.bool_).at[slots].set(True)
    return (slot_start, live)


def draw_placement(key, part):
    return placement_table(key)


def draw_velocity(key, part):
    slot_start, live = slot_starts(placement_table(key))
    field_key = jax.random.fold_in(key, 4409)
    field = jax.random.truncated_normal(field_key, -5.0, 5.0, (3, NX, NY, NZ), jnp.float32)
    padded_field = jnp.pad(field, ((0, 0), (1, 1), (1, 1), (1, 1)))
    boxes = jax.vmap(lambda start: lax.dynamic_slice(padded_field, (0, start[0], start[1], start[2]), (3, PAD, PAD, PAD)))(slot_start)
    boxes = boxes.reshape(slot_start.shape[0], 3, PAD * PAD * PAD)
    return jnp.where(live[:, None, None], boxes, 0.0).astype(jnp.float32)


def draw_fraction(key, part):
    slot_start, live = slot_starts(placement_table(key))
    key_cut, key_value = jax.random.split(jax.random.fold_in(key, 5501))
    cut = jax.random.randint(key_cut, (NX, NY, NZ), 0, 10) < 4
    values = jax.random.randint(key_value, (NX, NY, NZ), 32, 256)
    field = jnp.where(cut, values, 256).astype(jnp.int32)
    padded_field = jnp.pad(field, 1)
    boxes = jax.vmap(lambda start: lax.dynamic_slice(padded_field, (start[0], start[1], start[2]), (PAD, PAD, PAD)))(slot_start)
    boxes = boxes.reshape(slot_start.shape[0], PAD * PAD * PAD)
    return jnp.where(live[:, None], boxes, 0).astype(jnp.int32)


def setup_inputs(seed: int = 0) -> dict:
    keys = jax.random.split(jax.random.key(seed), 4)
    velocity = draw_velocity(jax.random.fold_in(keys[3], 71), 0)
    fraction = draw_fraction(jax.random.fold_in(keys[3], 71), 0)
    placement = draw_placement(jax.random.fold_in(keys[3], 71), 0)
    return {"velocity": velocity, "fraction": fraction, "placement": placement}


STEP_DT = 0.25
SHIFT_WEIGHT = 0.5
LOWER_BOUND = 0.5 / 6.5
UPPER_BOUND = 2.0


def shift_up(values, heading, edge):
    offset = edge ** (2 - heading)
    widths = [(0, 0)] * (values.ndim - 1) + [(0, offset)]
    return jnp.pad(values[..., offset:], widths)


def shift_down(values, heading, edge):
    offset = edge ** (2 - heading)
    widths = [(0, 0)] * (values.ndim - 1) + [(offset, 0)]
    return jnp.pad(values[..., :values.shape[-1] - offset], widths)


def interior(values, padded):
    inner = padded - 2
    leading = values.shape[:-1]
    cube = values.reshape(leading + (padded, padded, padded))
    cube = cube[..., 1:padded - 1, 1:padded - 1, 1:padded - 1]
    return cube.reshape(leading + (inner * inner * inner,))


def inside_mask(padded):
    flat_pos = lax.broadcasted_iota(jnp.int32, (padded * padded * padded,), 0)
    along_x = flat_pos // (padded * padded)
    along_y = (flat_pos // padded) % padded
    along_z = flat_pos % padded
    return ((along_x >= 1) & (along_x <= padded - 2) & (along_y >= 1) & (along_y <= padded - 2)
            & (along_z >= 1) & (along_z <= padded - 2))


def box_update(velocity_box, fraction_box, padded):
    volume = fraction_box.astype(jnp.float32) / 256.0
    inside = inside_mask(padded)
    tendency = jnp.zeros_like(velocity_box)
    divergence = jnp.zeros_like(volume)
    for heading in range(3):
        aperture = jnp.minimum(volume, shift_up(volume, heading, padded))
        ahead = shift_up(velocity_box, heading, padded)
        face_speed = 0.5 * (velocity_box[heading] + ahead[heading])
        face_flow = aperture * face_speed
        fluxes = face_flow * jnp.where(face_speed > 0.0, velocity_box, ahead)
        tendency = tendency + fluxes - shift_down(fluxes, heading, padded)
        divergence = divergence + face_flow - shift_down(face_flow, heading, padded)
    masses = jnp.where(inside, volume * velocity_box - STEP_DT * tendency, 0.0)
    weights = jnp.where(inside, volume, 0.0)
    numerator = masses
    denominator = weights
    for heading in range(3):
        numerator = numerator + shift_up(masses, heading, padded) + shift_down(masses, heading, padded)
        denominator = denominator + shift_up(weights, heading, padded) + shift_down(weights, heading, padded)
    denominator = jnp.where(inside, denominator, 1.0)
    regular = masses / jnp.where(inside, volume, 1.0)
    updated = jnp.where(fraction_box < 256, numerator / denominator, regular)
    return interior(updated, padded), interior(-divergence, padded)


def box_correction(updated, pressure_box, fraction_box, padded):
    volume = fraction_box.astype(jnp.float32) / 256.0
    slopes = []
    for heading in range(3):
        aperture = jnp.minimum(volume, shift_up(volume, heading, padded))
        behind = shift_down(aperture, heading, padded)
        slope = 0.5 * (aperture * (shift_up(pressure_box, heading, padded) - pressure_box)
                       + behind * (pressure_box - shift_down(pressure_box, heading, padded)))
        slopes.append(slope)
    return updated - interior(jnp.stack(slopes), padded)


def sides(rimmed):
    return [(rimmed[2:, 1:-1, 1:-1], rimmed[:-2, 1:-1, 1:-1]),
            (rimmed[1:-1, 2:, 1:-1], rimmed[1:-1, :-2, 1:-1]),
            (rimmed[1:-1, 1:-1, 2:], rimmed[1:-1, 1:-1, :-2])]


def operator_parts(volume, volume_rimmed):
    apertures = []
    diagonal = SHIFT_WEIGHT * volume
    for upper_side, lower_side in sides(volume_rimmed):
        upper_ap = jnp.minimum(volume, upper_side)
        lower_ap = jnp.minimum(lower_side, volume)
        apertures.append((upper_ap, lower_ap))
        diagonal = diagonal + upper_ap + lower_ap
    return apertures, diagonal


def apply_operator(search, search_rimmed, apertures, diagonal):
    total = jnp.zeros_like(search)
    for (upper_side, lower_side), (upper_ap, lower_ap) in zip(sides(search_rimmed), apertures):
        total = total + upper_ap * upper_side + lower_ap * lower_side
    return diagonal * search - total


def reference(velocity, fraction, placement):
    updated, rhs_boxes = lax.map(lambda items: box_update(items[0], items[1], PAD), (velocity, fraction))
    volume_boxes = interior(fraction.astype(jnp.float32) / 256.0, PAD)
    entries = N_BY * KB
    owners = placement // PAIR
    lines = owners.transpose(0, 2, 1, 3).reshape(N_BX, N_BZ, entries)
    onehot = (lines[..., None] == jnp.arange(N_BY, dtype=jnp.int32)).astype(jnp.int32)
    ranks = jnp.sum((jnp.cumsum(onehot, axis=2) - onehot) * onehot, axis=-1)
    along_x = jnp.arange(N_BX, dtype=jnp.int32)[:, None, None]
    along_z = jnp.arange(N_BZ, dtype=jnp.int32)[None, :, None]
    slots = (((along_x * N_BY + lines) * N_BZ + along_z) * BOX_CAP + ranks).astype(jnp.int32)
    slots_brick = slots.reshape(N_BX, N_BZ, N_BY, KB).transpose(0, 2, 1, 3)

    def to_grid(boxes):
        picked = boxes[slots_brick]
        cube = picked.reshape(N_BX, N_BY, N_BZ, KB, BOX, BOX, BOX)
        return cube.transpose(0, 4, 1, 5, 2, 3, 6).reshape(NX, NY, NZ)

    source = to_grid(rhs_boxes)
    volume_grid = to_grid(volume_boxes)
    apertures, diagonal = operator_parts(volume_grid, jnp.pad(volume_grid, 1))
    center = 0.5 * (UPPER_BOUND + LOWER_BOUND)
    halfwidth = 0.5 * (UPPER_BOUND - LOWER_BOUND)
    spread = center / halfwidth
    damping = 1.0 / spread
    pressure = jnp.zeros_like(source)
    residual = source
    search = (residual / diagonal) * (1.0 / center)
    for iteration in range(ITERS):
        pressure = pressure + search
        if iteration < ITERS - 1:
            residual = residual - apply_operator(search, jnp.pad(search, 1), apertures, diagonal)
            damping_next = 1.0 / (2.0 * spread - damping)
            search = (damping_next * damping) * search + (2.0 * damping_next / halfwidth) * (residual / diagonal)
            damping = damping_next

    entry_ids = jnp.arange(N_BX * N_BZ * entries, dtype=jnp.int32)
    start_x = entry_ids // (N_BZ * entries)
    start_zline = (entry_ids // entries) % N_BZ
    inner_id = entry_ids % entries
    brick_y = inner_id // KB
    box_k = inner_id % KB
    starts = jnp.stack([start_x * BOX, brick_y * BOX, (start_zline * KB + box_k) * BOX], axis=-1).astype(jnp.int32)
    flat_slots = slots.reshape(-1)
    slot_start = jnp.zeros((SLOTS, 3), jnp.int32).at[flat_slots].set(starts)
    live = jnp.zeros((SLOTS,), jnp.bool_).at[flat_slots].set(True)
    rimmed_pressure = jnp.pad(pressure, 1)

    def finish(items):
        update_box, fraction_box, start, alive = items
        pressure_box = lax.dynamic_slice(rimmed_pressure, (start[0], start[1], start[2]), (PAD, PAD, PAD))
        corrected = box_correction(update_box, pressure_box.reshape(PAD * PAD * PAD), fraction_box, PAD)
        return jnp.where(alive, corrected, 0.0)

    velocity_out = lax.map(finish, (updated, fraction, slot_start, live))
    return velocity_out, pressure
```

```python
import functools

import jax
import jax.numpy as jnp
from jax import lax
from jax.experimental import pallas as pl
from jax.experimental.pallas import tpu as pltpu
from jax.sharding import PartitionSpec as P

BOX = 32
ITERS = 4
PADDED = BOX + 2
PLANE = PADDED * PADDED
TILE = 128
WIDE = 10 * TILE
INNER = BOX * BOX
TILES = INNER // TILE
PER_TILE = TILE // BOX
ROWS = BOX * TILES
RETURN_ROWS = PADDED * TILES + 4 * TILES
STEP_DT = 0.25
SHIFT_WEIGHT = 0.5
LOWER_BOUND = 0.5 / 6.5
UPPER_BOUND = 2.0

VMEM_SPEC = pl.BlockSpec(memory_space=pltpu.VMEM)
SMEM_SPEC = pl.BlockSpec(memory_space=pltpu.SMEM)
ANY_SPEC = pl.BlockSpec(memory_space=pl.ANY)


def lane_index():
    return lax.broadcasted_iota(jnp.int32, (8, TILE), 1)


def inside_plane():
    flat = lax.broadcasted_iota(jnp.int32, (8, WIDE), 1)
    row = flat // PADDED
    col = flat % PADDED
    return (row >= 1) & (row <= BOX) & (col >= 1) & (col <= BOX)


def ahead(values, offset):
    return pltpu.roll(values, WIDE - offset, 1)


def behind(values, offset):
    return pltpu.roll(values, offset, 1)


def compact(values, offset, lanes):
    tiles = [values[:, t * TILE : (t + 1) * TILE] for t in range(WIDE // TILE)]
    out = []
    for q in range(TILES):
        pieces = []
        for r in range(PER_TILE):
            start = (q * PER_TILE + r + 1) * PADDED + 1 + offset
            index, lane = divmod(start, TILE)
            shift = (BOX * r - lane) % TILE
            piece = pltpu.roll(tiles[index], shift, 1) if shift else tiles[index]
            if lane + BOX > TILE:
                rest = pltpu.roll(tiles[index + 1], shift, 1) if shift else tiles[index + 1]
                piece = jnp.where(lanes < BOX * r + TILE - lane, piece, rest)
            pieces.append(piece)
        value = pieces[-1]
        for r in reversed(range(PER_TILE - 1)):
            value = jnp.where(lanes < BOX * (r + 1), pieces[r], value)
        out.append(value)
    return out


def aligned_plane(load, x, lanes):
    start = x * (PLANE // TILE) + (x * (PLANE % TILE)) // TILE
    amount = (x * (PLANE % TILE)) % TILE
    block = load(pl.multiple_of(start * TILE, TILE))
    tiles = [
        pltpu.roll(block[:, t * TILE : (t + 1) * TILE], TILE - amount, 1)
        for t in range(WIDE // TILE)
    ]
    keep = lanes < TILE - amount
    return [
        jnp.where(keep, tiles[t], tiles[t + 1]) if t + 1 < len(tiles) else tiles[t]
        for t in range(len(tiles))
    ]


def store_plane(ref, index, tiles):
    for t, tile in enumerate(tiles):
        ref[index + (slice(None), slice(t * TILE, (t + 1) * TILE))] = tile


def last_plane(ref_tail, out_ref, index):
    tail = ref_tail
    start = (PADDED - 1) * PLANE
    first = start // TILE * TILE
    span = PADDED * PLANE - first
    tail_block = jnp.concatenate([tail, jnp.zeros((8, WIDE - span), jnp.float32)], axis=1)
    out_ref[index] = pltpu.roll(tail_block, WIDE - (start - first), 1)


def put_rows(ref, x, tiles):
    for q, tile in enumerate(tiles):
        ref[pl.ds(x * TILES + q, 8, stride=ROWS), :] = tile


def send_rows(slots, rows_ref, out_ref, sem, count):
    copies = [
        pltpu.make_async_copy(
            rows_ref.at[pl.ds(pl.multiple_of(slots[d] * ROWS, ROWS), ROWS)],
            out_ref.at[d],
            sem.at[d],
        )
        for d in range(count)
    ]
    for copy in copies:
        copy.start()
    for copy in copies:
        copy.wait()


def volume_kernel(slots, fraction, planes, rows, packed, tail, sem, *, lanes_by):
    lanes = lane_index()

    def align(x):
        tiles = aligned_plane(
            lambda s: fraction[:, pl.ds(s, WIDE)].astype(jnp.float32) * (1.0 / 256.0), x, lanes
        )
        store_plane(planes, (x,), tiles)

    def body(x, carry):
        align(x)
        return carry

    lax.fori_loop(0, PADDED - 1, body, 0)
    start = (PADDED - 1) * PLANE
    first = start // TILE * TILE
    span = PADDED * PLANE - first
    tail[...] = jnp.zeros_like(tail)
    tail[:, 0:span] = fraction[:, first : PADDED * PLANE].astype(jnp.float32) * (1.0 / 256.0)
    planes[PADDED - 1] = ahead(tail[...], start - first)

    def pack(x, carry):
        put_rows(packed, x, compact(planes[x + 1], 0, lanes))
        return carry

    lax.fori_loop(0, BOX, pack, 0)
    send_rows(slots, packed, rows, sem, lanes_by)


def flux_kernel(slots, velocity, planes, masses, rows, field, tail, carry_ref, packed, sem, *, lanes_by):
    lanes = lane_index()
    inside = inside_plane()

    def align(x):
        for c in range(3):
            store_plane(field, (x, c), aligned_plane(lambda s: velocity[c, :, pl.ds(s, WIDE)], x, lanes))

    def align_body(x, carry):
        align(x)
        return carry

    lax.fori_loop(0, PADDED - 1, align_body, 0)
    start = (PADDED - 1) * PLANE
    first = start // TILE * TILE
    span = PADDED * PLANE - first
    tail[...] = jnp.zeros_like(tail)
    for c in range(3):
        tail[:, 0:span] = velocity[c, :, first : PADDED * PLANE]
        field[PADDED - 1, c] = ahead(tail[...], start - first)

    def face(volume, volume_ahead, here, there, heading):
        speed = 0.5 * (here[heading] + there[heading])
        flow = jnp.minimum(volume, volume_ahead) * speed
        upwind = speed > 0.0
        return [flow * jnp.where(upwind, here[c], there[c]) for c in range(3)] + [flow]

    def x_face(x):
        return face(
            planes[x], planes[x + 1], [field[x, c] for c in range(3)], [field[x + 1, c] for c in range(3)], 0
        )

    for c, value in enumerate(x_face(0)):
        carry_ref[c] = value
    for c in range(3):
        masses[0, c] = jnp.zeros((8, WIDE), jnp.float32)
        masses[PADDED - 1, c] = jnp.zeros((8, WIDE), jnp.float32)

    def step(x, carry):
        volume = planes[x]
        here = [field[x, c] for c in range(3)]
        upper = x_face(x)
        total = [upper[c] - carry_ref[c] for c in range(4)]
        for c in range(4):
            carry_ref[c] = upper[c]
        for heading, offset in ((1, PADDED), (2, 1)):
            faces = face(volume, ahead(volume, offset), here, [ahead(v, offset) for v in here], heading)
            total = [total[c] + faces[c] - behind(faces[c], offset) for c in range(4)]
        for c in range(3):
            masses[x, c] = jnp.where(inside, volume * here[c] - STEP_DT * total[c], 0.0)
        put_rows(packed, x - 1, compact(-total[3], 0, lanes))
        return carry

    lax.fori_loop(1, PADDED - 1, step, 0)
    send_rows(slots, packed, rows, sem, lanes_by)


def update_kernel(masses, planes, updated, apertures):
    lanes = lane_index()
    inside = inside_plane()

    def put(ref, index, tiles):
        for q, tile in enumerate(tiles):
            ref[index + (slice(None), slice(q * TILE, (q + 1) * TILE))] = tile

    def neighbours(here, below, above):
        total = here + below + above
        for offset in (PADDED, 1):
            total = total + ahead(here, offset) + behind(here, offset)
        return total

    def step(x, carry):
        volume = planes[x]
        weight = jnp.where(inside, volume, 0.0)
        below = jnp.where(inside & (x > 1), planes[x - 1], 0.0)
        above = jnp.where(inside & (x < BOX), planes[x + 1], 0.0)
        weights = neighbours(weight, below, above)
        inverse = 1.0 / jnp.where(weights > 0.0, weights, 1.0)
        cut = volume < 1.0
        for c in range(3):
            here = masses[x, c]
            spread = neighbours(here, masses[x - 1, c], masses[x + 1, c]) * inverse
            put(updated, (x - 1, c), compact(jnp.where(cut, spread, here), 0, lanes))
        put(apertures, (x - 1, 0), compact(jnp.minimum(volume, planes[x - 1]), 0, lanes))
        put(apertures, (x - 1, 1), compact(jnp.minimum(volume, planes[x + 1]), 0, lanes))
        for axis, offset in ((1, PADDED), (2, 1)):
            aperture = jnp.minimum(volume, ahead(volume, offset))
            put(apertures, (x - 1, 2 * axis), compact(aperture, -offset, lanes))
            put(apertures, (x - 1, 2 * axis + 1), compact(aperture, 0, lanes))
        return carry

    lax.fori_loop(1, PADDED - 1, step, 0)


STEP_X = 4


def correct_kernel(rows, updated, apertures, returned, out, boxes, sem):
    step = pl.program_id(0)
    lanes = lane_index()

    @pl.when(step == 0)
    def _():
        copies = [
            pltpu.make_async_copy(
                returned.at[rows[s]], boxes.at[pl.ds(s * RETURN_ROWS, RETURN_ROWS)], sem.at[s]
            )
            for s in range(8)
        ]
        for copy in copies:
            copy.start()
        for copy in copies:
            copy.wait()

    def tile_of(row):
        return boxes[pl.ds(row, 8, stride=RETURN_ROWS), :]

    base = step * STEP_X
    faces = [
        tile_of(PADDED * TILES + f * TILES + step) for f in range(4)
    ]

    for i in range(STEP_X):
        x = base + i
        below = [tile_of(x * TILES + q) for q in range(TILES)]
        here = [tile_of((x + 1) * TILES + q) for q in range(TILES)]
        above = [tile_of((x + 2) * TILES + q) for q in range(TILES)]
        y_low, y_high = [
            pltpu.roll(faces[f], (TILE - BOX * i) % TILE, 1) if i else faces[f] for f in (0, 1)
        ]
        z_low, z_high = faces[2], faces[3]
        quarter = [pltpu.roll(t, BOX, 1) for t in here]
        reverse = [pltpu.roll(t, TILE - BOX, 1) for t in here]
        for q in range(TILES):
            p = here[q]
            before = quarter[q - 1] if q else pltpu.roll(y_low, 0, 1)
            y_behind = jnp.where(lanes < BOX, before, quarter[q])
            after = reverse[q + 1] if q + 1 < TILES else pltpu.roll(y_high, TILE - BOX, 1)
            y_ahead = jnp.where(lanes < TILE - BOX, reverse[q], after)
            z_behind = pltpu.roll(p, 1, 1)
            z_ahead = pltpu.roll(p, TILE - 1, 1)
            for r in range(PER_TILE):
                source = BOX * i + PER_TILE * q + r
                low = pltpu.roll(z_low, (BOX * r - source) % TILE, 1)
                high = pltpu.roll(z_high, (BOX * r + BOX - 1 - source) % TILE, 1)
                z_behind = jnp.where(lanes == BOX * r, low, z_behind)
                z_ahead = jnp.where(lanes == BOX * r + BOX - 1, high, z_ahead)
            cut = slice(q * TILE, (q + 1) * TILE)
            around = ((below[q], above[q]), (y_behind, y_ahead), (z_behind, z_ahead))
            for c, (lower, upper) in enumerate(around):
                slope = 0.5 * (
                    apertures[i, 2 * c + 1, :, cut] * (upper - p)
                    + apertures[i, 2 * c, :, cut] * (p - lower)
                )
                out[c, :, i * INNER + q * TILE : i * INNER + (q + 1) * TILE] = updated[i, c, :, cut] - slope


def struct(*shape):
    return jax.ShapeDtypeStruct(shape, jnp.float32)


def volume_call(send_slot, fraction):
    lanes_by = send_slot.shape[0]
    return pl.pallas_call(
        functools.partial(volume_kernel, lanes_by=lanes_by),
        in_specs=[SMEM_SPEC, VMEM_SPEC],
        out_specs=[VMEM_SPEC, ANY_SPEC],
        out_shape=[struct(PADDED, 8, WIDE), struct(lanes_by, ROWS, TILE)],
        scratch_shapes=[
            pltpu.VMEM((8 * ROWS, TILE), jnp.float32),
            pltpu.VMEM((8, WIDE), jnp.float32),
            pltpu.SemaphoreType.DMA((lanes_by,)),
        ],
        name="volume_rows",
    )(send_slot, fraction)


def flux_call(send_slot, velocity, planes):
    lanes_by = send_slot.shape[0]
    return pl.pallas_call(
        functools.partial(flux_kernel, lanes_by=lanes_by),
        in_specs=[SMEM_SPEC, VMEM_SPEC, VMEM_SPEC],
        out_specs=[VMEM_SPEC, ANY_SPEC],
        out_shape=[struct(PADDED, 3, 8, WIDE), struct(lanes_by, ROWS, TILE)],
        scratch_shapes=[
            pltpu.VMEM((PADDED, 3, 8, WIDE), jnp.float32),
            pltpu.VMEM((8, WIDE), jnp.float32),
            pltpu.VMEM((4, 8, WIDE), jnp.float32),
            pltpu.VMEM((8 * ROWS, TILE), jnp.float32),
            pltpu.SemaphoreType.DMA((lanes_by,)),
        ],
        name="flux_rows",
    )(send_slot, velocity, planes)


def update_call(masses, planes):
    return pl.pallas_call(
        update_kernel,
        in_specs=[VMEM_SPEC, VMEM_SPEC],
        out_specs=[VMEM_SPEC, VMEM_SPEC],
        out_shape=[struct(BOX, 3, 8, INNER), struct(BOX, 6, 8, INNER)],
        name="updated",
    )(masses, planes)


def correct_call(slot_row, updated, apertures, returned):
    return pl.pallas_call(
        correct_kernel,
        grid=(BOX // STEP_X,),
        in_specs=[
            SMEM_SPEC,
            pl.BlockSpec((STEP_X, 3, 8, INNER), lambda i: (i, 0, 0, 0)),
            pl.BlockSpec((STEP_X, 6, 8, INNER), lambda i: (i, 0, 0, 0)),
            ANY_SPEC,
        ],
        out_specs=pl.BlockSpec((3, 8, STEP_X * INNER), lambda i: (0, 0, i)),
        out_shape=struct(3, 8, BOX * INNER),
        scratch_shapes=[
            pltpu.VMEM((8 * RETURN_ROWS, TILE), jnp.float32),
            pltpu.SemaphoreType.DMA((8,)),
        ],
        name="corrected",
    )(slot_row, updated, apertures, returned)


def extended(cells, sides, width):
    for axis, dim in sides:
        count = lax.axis_size(axis)
        ends = count - 1
        head = lax.slice_in_dim(cells, 0, width, axis=dim)
        tail = lax.slice_in_dim(cells, cells.shape[dim] - width, cells.shape[dim], axis=dim)
        cells = jnp.concatenate(
            [
                lax.ppermute(tail, axis, [(i, (i + 1) % count) for i in range(ends)]),
                cells,
                lax.ppermute(head, axis, [((i + 1) % count, i) for i in range(ends)]),
            ],
            axis=dim,
        )
    return cells


def sides(rimmed):
    return [
        (rimmed[2:, 1:-1, 1:-1], rimmed[:-2, 1:-1, 1:-1]),
        (rimmed[1:-1, 2:, 1:-1], rimmed[1:-1, :-2, 1:-1]),
        (rimmed[1:-1, 1:-1, 2:], rimmed[1:-1, 1:-1, :-2]),
    ]


def operator_parts(volume, volume_rimmed):
    apertures = []
    diagonal = SHIFT_WEIGHT * volume
    for upper_side, lower_side in sides(volume_rimmed):
        upper_ap = jnp.minimum(volume, upper_side)
        lower_ap = jnp.minimum(lower_side, volume)
        apertures.append((upper_ap, lower_ap))
        diagonal = diagonal + upper_ap + lower_ap
    return (apertures, diagonal)


def apply_operator(search, search_rimmed, apertures, diagonal):
    total = jnp.zeros_like(search)
    for (upper_side, lower_side), (upper_ap, lower_ap) in zip(sides(search_rimmed), apertures):
        total = total + upper_ap * upper_side + lower_ap * lower_side
    return diagonal * search - total


def to_brick(rows):
    count = rows.shape[0]
    cube = rows.reshape(count, BOX, TILES, PER_TILE, BOX)
    return cube.transpose(1, 2, 3, 0, 4).reshape(BOX, BOX, count * BOX)


def return_box(rimmed, k):
    low = k * BOX
    core = rimmed[:, 1:-1, low + 1 : low + 1 + BOX].reshape(PADDED * TILES, TILE)
    y_faces = [rimmed[1:-1, y, low + 1 : low + 1 + BOX] for y in (0, BOX + 1)]
    z_faces = [rimmed[1:-1, 1:-1, z] for z in (low, low + BOX + 1)]
    return jnp.concatenate([core] + [f.reshape(TILES, TILE) for f in y_faces + z_faces], axis=0)


def solve(source, volume):
    axes = (("bx", 0), ("by", 1), ("bz", 2))
    volume_rimmed = extended(volume, axes, 1)
    apertures, diagonal = operator_parts(volume, volume_rimmed)
    center = 0.5 * (UPPER_BOUND + LOWER_BOUND)
    halfwidth = 0.5 * (UPPER_BOUND - LOWER_BOUND)
    spread = center / halfwidth
    damping = 1.0 / spread
    pressure = jnp.zeros_like(source)
    residual = source
    search = residual / diagonal * (1.0 / center)
    for iteration in range(ITERS):
        pressure = pressure + search
        if iteration < ITERS - 1:
            residual = residual - apply_operator(search, extended(search, axes, 1), apertures, diagonal)
            damping_next = 1.0 / (2.0 * spread - damping)
            search = damping_next * damping * search + 2.0 * damping_next / halfwidth * (
                residual / diagonal
            )
            damping = damping_next
    return pressure, extended(pressure, axes, 1)


def routing(placement, capacity):
    lanes = lax.axis_size("by")
    own_index = lax.axis_index("by")
    table = placement[0, :, 0, :]
    per_brick = table.shape[1]
    entries = lanes * per_brick
    owners = table.reshape(entries)
    onehot = (owners[:, None] == jnp.arange(lanes, dtype=jnp.int32)[None, :]).astype(jnp.int32)
    ranks = jnp.sum((jnp.cumsum(onehot, axis=0) - onehot) * onehot, axis=1)
    matches = (table == own_index).astype(jnp.int32)
    send_slot = jnp.sum(matches * ranks.reshape(lanes, per_brick), axis=1)
    slot_match = (
        (owners == own_index)[:, None]
        & (ranks[:, None] == jnp.arange(capacity, dtype=jnp.int32)[None, :])
    ).astype(jnp.int32)
    row_value = jnp.arange(entries, dtype=jnp.int32) // per_brick
    slot_row = jnp.sum(slot_match * row_value[:, None], axis=0)
    brick_table = lax.dynamic_index_in_dim(table, own_index, 0, keepdims=False)
    all_rows = jnp.arange(lanes, dtype=jnp.int32)
    box_of_row = jnp.sum(
        (brick_table[None, :] == all_rows[:, None]).astype(jnp.int32)
        * jnp.arange(per_brick, dtype=jnp.int32)[None, :],
        axis=1,
    )
    return send_slot, slot_row, brick_table, box_of_row


def exchange(rows):
    return lax.all_to_all(rows, "by", split_axis=0, concat_axis=0, tiled=True)


def local(velocity, fraction, placement):
    send_slot, slot_row, brick_table, box_of_row = routing(placement, velocity.shape[0])
    planes, volume_rows = volume_call(send_slot, fraction)
    volume_recv = exchange(volume_rows)
    masses, source_rows = flux_call(send_slot, jnp.swapaxes(velocity, 0, 1), planes)
    source_recv = exchange(source_rows)
    updated, apertures = update_call(masses, planes)
    volume = to_brick(jnp.take(volume_recv, brick_table, axis=0))
    source = to_brick(jnp.take(source_recv, brick_table, axis=0))
    pressure, rimmed = solve(source, volume)
    boxes = jnp.stack([return_box(rimmed, k) for k in range(placement.shape[3])])
    returned = exchange(jnp.take(boxes, box_of_row, axis=0))
    corrected = correct_call(slot_row, updated, apertures, returned)
    return (jnp.swapaxes(corrected, 0, 1), pressure)


def solution(mesh):
    in_specs = (
        P(("bx", "by", "bz"), None, None),
        P(("bx", "by", "bz"), None),
        P("bx", None, "bz", None),
    )
    out_specs = (P(("bx", "by", "bz"), None, None), P("bx", "by", "bz"))
    return jax.shard_map(local, mesh=mesh, in_specs=in_specs, out_specs=out_specs, check_vma=False)
```

```python
import functools

import jax
import jax.numpy as jnp
from jax import lax
from jax.experimental import pallas as pl
from jax.experimental.pallas import tpu as pltpu
from jax.sharding import PartitionSpec as P

BOX = 32
ITERS = 4
PADDED = BOX + 2
PLANE = PADDED * PADDED
TILE = 128
WIDE = 10 * TILE
INNER = BOX * BOX
TILES = INNER // TILE
PER_TILE = TILE // BOX
ROWS = BOX * TILES
RETURN_ROWS = PADDED * TILES + 4 * TILES
STEP_DT = 0.25
SHIFT_WEIGHT = 0.5
LOWER_BOUND = 0.5 / 6.5
UPPER_BOUND = 2.0

VMEM_SPEC = pl.BlockSpec(memory_space=pltpu.VMEM)
SMEM_SPEC = pl.BlockSpec(memory_space=pltpu.SMEM)
ANY_SPEC = pl.BlockSpec(memory_space=pl.ANY)


def lane_index():
    return lax.broadcasted_iota(jnp.int32, (8, TILE), 1)


def inside_plane():
    flat = lax.broadcasted_iota(jnp.int32, (8, WIDE), 1)
    row = flat // PADDED
    col = flat % PADDED
    return (row >= 1) & (row <= BOX) & (col >= 1) & (col <= BOX)


def ahead(values, offset):
    return pltpu.roll(values, WIDE - offset, 1)


def behind(values, offset):
    return pltpu.roll(values, offset, 1)


def compact(values, offset, lanes):
    tiles = [values[:, t * TILE : (t + 1) * TILE] for t in range(WIDE // TILE)]
    out = []
    for q in range(TILES):
        pieces = []
        for r in range(PER_TILE):
            start = (q * PER_TILE + r + 1) * PADDED + 1 + offset
            index, lane = divmod(start, TILE)
            shift = (BOX * r - lane) % TILE
            piece = pltpu.roll(tiles[index], shift, 1) if shift else tiles[index]
            if lane + BOX > TILE:
                rest = pltpu.roll(tiles[index + 1], shift, 1) if shift else tiles[index + 1]
                piece = jnp.where(lanes < BOX * r + TILE - lane, piece, rest)
            pieces.append(piece)
        value = pieces[-1]
        for r in reversed(range(PER_TILE - 1)):
            value = jnp.where(lanes < BOX * (r + 1), pieces[r], value)
        out.append(value)
    return out


def aligned_plane(load, x, lanes):
    start = x * (PLANE // TILE) + (x * (PLANE % TILE)) // TILE
    amount = (x * (PLANE % TILE)) % TILE
    block = load(pl.multiple_of(start * TILE, TILE))
    tiles = [
        pltpu.roll(block[:, t * TILE : (t + 1) * TILE], TILE - amount, 1)
        for t in range(WIDE // TILE)
    ]
    keep = lanes < TILE - amount
    return [
        jnp.where(keep, tiles[t], tiles[t + 1]) if t + 1 < len(tiles) else tiles[t]
        for t in range(len(tiles))
    ]


def store_plane(ref, index, tiles):
    for t, tile in enumerate(tiles):
        ref[index + (slice(None), slice(t * TILE, (t + 1) * TILE))] = tile


def last_plane(ref_tail, out_ref, index):
    tail = ref_tail
    start = (PADDED - 1) * PLANE
    first = start // TILE * TILE
    span = PADDED * PLANE - first
    tail_block = jnp.concatenate([tail, jnp.zeros((8, WIDE - span), jnp.float32)], axis=1)
    out_ref[index] = pltpu.roll(tail_block, WIDE - (start - first), 1)


def put_rows(ref, x, tiles):
    for q, tile in enumerate(tiles):
        ref[pl.ds(x * TILES + q, 8, stride=ROWS), :] = tile


def send_rows(slots, rows_ref, out_ref, sem, count):
    copies = [
        pltpu.make_async_copy(
            rows_ref.at[pl.ds(pl.multiple_of(slots[d] * ROWS, ROWS), ROWS)],
            out_ref.at[d],
            sem.at[d],
        )
        for d in range(count)
    ]
    for copy in copies:
        copy.start()
    for copy in copies:
        copy.wait()


def volume_kernel(slots, fraction, planes, rows, packed, tail, sem, *, lanes_by):
    lanes = lane_index()

    def align(x):
        tiles = aligned_plane(
            lambda s: fraction[:, pl.ds(s, WIDE)].astype(jnp.float32) * (1.0 / 256.0), x, lanes
        )
        store_plane(planes, (x,), tiles)

    def body(x, carry):
        align(x)
        return carry

    lax.fori_loop(0, PADDED - 1, body, 0)
    start = (PADDED - 1) * PLANE
    first = start // TILE * TILE
    span = PADDED * PLANE - first
    tail[...] = jnp.zeros_like(tail)
    tail[:, 0:span] = fraction[:, first : PADDED * PLANE].astype(jnp.float32) * (1.0 / 256.0)
    planes[PADDED - 1] = ahead(tail[...], start - first)

    def pack(x, carry):
        put_rows(packed, x, compact(planes[x + 1], 0, lanes))
        return carry

    lax.fori_loop(0, BOX, pack, 0)
    send_rows(slots, packed, rows, sem, lanes_by)


def flux_kernel(slots, velocity, planes, masses, rows, field, tail, carry_ref, packed, sem, *, lanes_by):
    lanes = lane_index()
    inside = inside_plane()

    def align(x):
        for c in range(3):
            store_plane(field, (x, c), aligned_plane(lambda s: velocity[c, :, pl.ds(s, WIDE)], x, lanes))

    def align_body(x, carry):
        align(x)
        return carry

    lax.fori_loop(0, PADDED - 1, align_body, 0)
    start = (PADDED - 1) * PLANE
    first = start // TILE * TILE
    span = PADDED * PLANE - first
    tail[...] = jnp.zeros_like(tail)
    for c in range(3):
        tail[:, 0:span] = velocity[c, :, first : PADDED * PLANE]
        field[PADDED - 1, c] = ahead(tail[...], start - first)

    def face(volume, volume_ahead, here, there, heading):
        speed = 0.5 * (here[heading] + there[heading])
        flow = jnp.minimum(volume, volume_ahead) * speed
        upwind = speed > 0.0
        return [flow * jnp.where(upwind, here[c], there[c]) for c in range(3)] + [flow]

    def x_face(x):
        return face(
            planes[x], planes[x + 1], [field[x, c] for c in range(3)], [field[x + 1, c] for c in range(3)], 0
        )

    for c, value in enumerate(x_face(0)):
        carry_ref[c] = value
    for c in range(3):
        masses[0, c] = jnp.zeros((8, WIDE), jnp.float32)
        masses[PADDED - 1, c] = jnp.zeros((8, WIDE), jnp.float32)

    def step(x, carry):
        volume = planes[x]
        here = [field[x, c] for c in range(3)]
        upper = x_face(x)
        total = [upper[c] - carry_ref[c] for c in range(4)]
        for c in range(4):
            carry_ref[c] = upper[c]
        for heading, offset in ((1, PADDED), (2, 1)):
            faces = face(volume, ahead(volume, offset), here, [ahead(v, offset) for v in here], heading)
            total = [total[c] + faces[c] - behind(faces[c], offset) for c in range(4)]
        for c in range(3):
            masses[x, c] = jnp.where(inside, volume * here[c] - STEP_DT * total[c], 0.0)
        put_rows(packed, x - 1, compact(-total[3], 0, lanes))
        return carry

    lax.fori_loop(1, PADDED - 1, step, 0)
    send_rows(slots, packed, rows, sem, lanes_by)


def update_kernel(masses, planes, updated, apertures):
    lanes = lane_index()
    inside = inside_plane()

    def put(ref, index, tiles):
        for q, tile in enumerate(tiles):
            ref[index + (slice(None), slice(q * TILE, (q + 1) * TILE))] = tile

    def neighbours(here, below, above):
        total = here + below + above
        for offset in (PADDED, 1):
            total = total + ahead(here, offset) + behind(here, offset)
        return total

    def step(x, carry):
        volume = planes[x]
        weight = jnp.where(inside, volume, 0.0)
        below = jnp.where(inside & (x > 1), planes[x - 1], 0.0)
        above = jnp.where(inside & (x < BOX), planes[x + 1], 0.0)
        weights = neighbours(weight, below, above)
        inverse = 1.0 / jnp.where(weights > 0.0, weights, 1.0)
        cut = volume < 1.0
        for c in range(3):
            here = masses[x, c]
            spread = neighbours(here, masses[x - 1, c], masses[x + 1, c]) * inverse
            put(updated, (x - 1, c), compact(jnp.where(cut, spread, here), 0, lanes))
        put(apertures, (x - 1, 0), compact(jnp.minimum(volume, planes[x - 1]), 0, lanes))
        put(apertures, (x - 1, 1), compact(jnp.minimum(volume, planes[x + 1]), 0, lanes))
        for axis, offset in ((1, PADDED), (2, 1)):
            aperture = jnp.minimum(volume, ahead(volume, offset))
            put(apertures, (x - 1, 2 * axis), compact(aperture, -offset, lanes))
            put(apertures, (x - 1, 2 * axis + 1), compact(aperture, 0, lanes))
        return carry

    lax.fori_loop(1, PADDED - 1, step, 0)


STEP_X = 4


def correct_kernel(rows, updated, apertures, returned, out, boxes, sem):
    step = pl.program_id(0)
    lanes = lane_index()

    @pl.when(step == 0)
    def _():
        copies = [
            pltpu.make_async_copy(
                returned.at[rows[s]], boxes.at[pl.ds(s * RETURN_ROWS, RETURN_ROWS)], sem.at[s]
            )
            for s in range(8)
        ]
        for copy in copies:
            copy.start()
        for copy in copies:
            copy.wait()

    def tile_of(row):
        return boxes[pl.ds(row, 8, stride=RETURN_ROWS), :]

    base = step * STEP_X
    faces = [
        tile_of(PADDED * TILES + f * TILES + step) for f in range(4)
    ]

    for i in range(STEP_X):
        x = base + i
        below = [tile_of(x * TILES + q) for q in range(TILES)]
        here = [tile_of((x + 1) * TILES + q) for q in range(TILES)]
        above = [tile_of((x + 2) * TILES + q) for q in range(TILES)]
        y_low, y_high = [
            pltpu.roll(faces[f], (TILE - BOX * i) % TILE, 1) if i else faces[f] for f in (0, 1)
        ]
        z_low, z_high = faces[2], faces[3]
        quarter = [pltpu.roll(t, BOX, 1) for t in here]
        reverse = [pltpu.roll(t, TILE - BOX, 1) for t in here]
        for q in range(TILES):
            p = here[q]
            before = quarter[q - 1] if q else pltpu.roll(y_low, 0, 1)
            y_behind = jnp.where(lanes < BOX, before, quarter[q])
            after = reverse[q + 1] if q + 1 < TILES else pltpu.roll(y_high, TILE - BOX, 1)
            y_ahead = jnp.where(lanes < TILE - BOX, reverse[q], after)
            z_behind = pltpu.roll(p, 1, 1)
            z_ahead = pltpu.roll(p, TILE - 1, 1)
            for r in range(PER_TILE):
                source = BOX * i + PER_TILE * q + r
                low = pltpu.roll(z_low, (BOX * r - source) % TILE, 1)
                high = pltpu.roll(z_high, (BOX * r + BOX - 1 - source) % TILE, 1)
                z_behind = jnp.where(lanes == BOX * r, low, z_behind)
                z_ahead = jnp.where(lanes == BOX * r + BOX - 1, high, z_ahead)
            cut = slice(q * TILE, (q + 1) * TILE)
            around = ((below[q], above[q]), (y_behind, y_ahead), (z_behind, z_ahead))
            for c, (lower, upper) in enumerate(around):
                slope = 0.5 * (
                    apertures[i, 2 * c + 1, :, cut] * (upper - p)
                    + apertures[i, 2 * c, :, cut] * (p - lower)
                )
                out[c, :, i * INNER + q * TILE : i * INNER + (q + 1) * TILE] = updated[i, c, :, cut] - slope


def struct(*shape):
    return jax.ShapeDtypeStruct(shape, jnp.float32)


def volume_call(send_slot, fraction):
    lanes_by = send_slot.shape[0]
    return pl.pallas_call(
        functools.partial(volume_kernel, lanes_by=lanes_by),
        in_specs=[SMEM_SPEC, VMEM_SPEC],
        out_specs=[VMEM_SPEC, ANY_SPEC],
        out_shape=[struct(PADDED, 8, WIDE), struct(lanes_by, ROWS, TILE)],
        scratch_shapes=[
            pltpu.VMEM((8 * ROWS, TILE), jnp.float32),
            pltpu.VMEM((8, WIDE), jnp.float32),
            pltpu.SemaphoreType.DMA((lanes_by,)),
        ],
        name="volume_rows",
    )(send_slot, fraction)


def flux_call(send_slot, velocity, planes):
    lanes_by = send_slot.shape[0]
    return pl.pallas_call(
        functools.partial(flux_kernel, lanes_by=lanes_by),
        in_specs=[SMEM_SPEC, VMEM_SPEC, VMEM_SPEC],
        out_specs=[VMEM_SPEC, ANY_SPEC],
        out_shape=[struct(PADDED, 3, 8, WIDE), struct(lanes_by, ROWS, TILE)],
        scratch_shapes=[
            pltpu.VMEM((PADDED, 3, 8, WIDE), jnp.float32),
            pltpu.VMEM((8, WIDE), jnp.float32),
            pltpu.VMEM((4, 8, WIDE), jnp.float32),
            pltpu.VMEM((8 * ROWS, TILE), jnp.float32),
            pltpu.SemaphoreType.DMA((lanes_by,)),
        ],
        name="flux_rows",
    )(send_slot, velocity, planes)


def update_call(masses, planes):
    return pl.pallas_call(
        update_kernel,
        in_specs=[VMEM_SPEC, VMEM_SPEC],
        out_specs=[VMEM_SPEC, VMEM_SPEC],
        out_shape=[struct(BOX, 3, 8, INNER), struct(BOX, 6, 8, INNER)],
        name="updated",
    )(masses, planes)


def correct_call(slot_row, updated, apertures, returned):
    return pl.pallas_call(
        correct_kernel,
        grid=(BOX // STEP_X,),
        in_specs=[
            SMEM_SPEC,
            pl.BlockSpec((STEP_X, 3, 8, INNER), lambda i: (i, 0, 0, 0)),
            pl.BlockSpec((STEP_X, 6, 8, INNER), lambda i: (i, 0, 0, 0)),
            ANY_SPEC,
        ],
        out_specs=pl.BlockSpec((3, 8, STEP_X * INNER), lambda i: (0, 0, i)),
        out_shape=struct(3, 8, BOX * INNER),
        scratch_shapes=[
            pltpu.VMEM((8 * RETURN_ROWS, TILE), jnp.float32),
            pltpu.SemaphoreType.DMA((8,)),
        ],
        name="corrected",
    )(slot_row, updated, apertures, returned)


HALO = 5
SIDE = 8
EXT = BOX + 2 * HALO
ROWS_Y = BOX + 2 * SIDE
SLOT = 8
GROUP = TILE // SLOT
GROUPS = BOX // GROUP + 2


def wide_lane():
    return lax.broadcasted_iota(jnp.int32, (ROWS_Y, TILE), 1)


def assemble_kernel(table, side, recv, brick, first, last, strip, strip_first, strip_last, boxes, sem, *, count):
    lanes = lane_index()
    copies = [
        pltpu.make_async_copy(recv.at[table[k]], boxes.at[k], sem.at[k]) for k in range(count)
    ]
    for copy in copies:
        copy.start()
    for copy in copies:
        copy.wait()
    strip[...] = jnp.zeros_like(strip)
    lanes_brick = lax.broadcasted_iota(jnp.int32, (BOX, TILE), 1)
    source_lane = jnp.where(side[0] == 0, TILE - SLOT, 0)

    def step(x, carry):
        rows = [boxes[k, pl.ds(x * TILES, TILES), :] for k in range(count)]
        for r in range(PER_TILE):
            value = None
            for k in reversed(range(count)):
                shift = (BOX * (k - r)) % TILE
                piece = pltpu.roll(rows[k], shift, 1) if shift else rows[k]
                value = piece if value is None else jnp.where(lanes < BOX * (k + 1), piece, value)
            brick[pl.ds(x * BOX + r, TILES, stride=PER_TILE), :] = value
        plane = brick[pl.ds(x * BOX, BOX), :]
        group = x // GROUP
        lane = (x % GROUP) * SLOT
        moved = pltpu.roll(plane, (lane - source_lane + TILE) % TILE, 1)
        strip[group] = jnp.where(lanes_brick // SLOT == x % GROUP, moved, strip[group])
        return carry

    lax.fori_loop(0, BOX, step, 0)
    first[...] = brick[0 : HALO * BOX, :]
    last[...] = brick[(BOX - HALO) * BOX : BOX * BOX, :]
    strip_first[...] = strip[0]
    strip_last[...] = strip[BOX // GROUP - 1]


def solve_kernel(box_of_row, side, *refs, count, lanes_by):
    volume_in, source_in = refs[0:8], refs[8:16]
    pressure, rows = refs[16:18]
    scratch = refs[18:]
    (vol, ax, ayu, ayl, azu, azl, diag, inv, res, sa, sb, total) = scratch[0:12]
    (hvol, hres, hsa, hsb, htotal, hcoef, edge, turned, packed, sem) = scratch[12:]
    lane = wide_lane()
    at_top = side[0] == 0
    edge_lane = jnp.where(at_top, TILE - 1, 0)
    slot_lane = jnp.where(at_top, 0, SLOT - 1)
    up_lane = jnp.where(at_top, TILE - 1, -1)
    low_lane = jnp.where(at_top, -1, 0)
    open_up = (lane % SLOT == SLOT - 1) & (low_lane == 0)
    open_low = (lane % SLOT == 0) & (up_lane >= 0)

    def main(ref, x):
        return ref[pl.ds(pl.multiple_of(x * ROWS_Y, 8), ROWS_Y), :]

    def put(ref, x, value):
        ref[pl.ds(pl.multiple_of(x * ROWS_Y, 8), ROWS_Y), :] = value

    def fill(ext, strips, parts):
        brick, x_lo, x_hi, middle, z_lo, z_hi, y_lo, y_hi = parts

        def rows_of(x):
            ext[pl.ds(pl.multiple_of(x * ROWS_Y, 8), SIDE), :] = y_lo[x]
            ext[pl.ds(pl.multiple_of(x * ROWS_Y + SIDE + BOX, 8), SIDE), :] = y_hi[x]

        def body(i, carry):
            ext[pl.ds(pl.multiple_of((i + HALO) * ROWS_Y + SIDE, 8), BOX), :] = brick[
                pl.ds(pl.multiple_of(i * BOX, 8), BOX), :
            ]
            rows_of(i + HALO)
            return carry

        lax.fori_loop(0, BOX, body, 0)
        for i in range(HALO):
            for x, part in ((i, x_lo), (HALO + BOX + i, x_hi)):
                ext[x * ROWS_Y + SIDE : x * ROWS_Y + SIDE + BOX, :] = part[i * BOX : (i + 1) * BOX, :]
                rows_of(x)
        pieces = [z_lo[...]] + [middle[g] for g in range(GROUPS - 2)] + [z_hi[...]]
        for g, piece in enumerate(pieces):
            strips[g, 0:SIDE] = y_lo[EXT + g]
            strips[g, SIDE : SIDE + BOX] = piece
            strips[g, SIDE + BOX : ROWS_Y] = y_hi[EXT + g]

    fill(vol, hvol, volume_in)
    fill(res, hres, source_in)

    def place(x):
        return (x + GROUP - HALO) // GROUP, (x + GROUP - HALO) % GROUP * SLOT + slot_lane

    def strip_value(strips, x):
        group, where = place(x)
        return pltpu.roll(strips[group], (edge_lane - where + TILE) % TILE, 1)

    def gather_edge(ref):
        def body(x, carry):
            group, where = place(x)
            moved = pltpu.roll(main(ref, x), (where - edge_lane + TILE) % TILE, 1)
            edge[group] = jnp.where(lane == where, moved, edge[group])
            return carry

        lax.fori_loop(1, EXT - 1, body, 0)

    def y_up(value):
        return pltpu.roll(value, ROWS_Y - 1, 0)

    def y_down(value):
        return pltpu.roll(value, 1, 0)

    def z_sides(value, outside):
        up = jnp.where(lane == up_lane, outside, pltpu.roll(value, TILE - 1, 1))
        down = jnp.where(lane == low_lane, outside, pltpu.roll(value, 1, 1))
        return up, down

    def strip_sides(strips, g):
        here = strips[g]
        following = strips[min(g + 1, GROUPS - 1)]
        previous = strips[max(g - 1, 0)]
        x_up = jnp.where(
            lane >= TILE - SLOT, pltpu.roll(following, TILE - SLOT, 1), pltpu.roll(here, TILE - SLOT, 1)
        )
        x_down = jnp.where(lane < SLOT, pltpu.roll(previous, SLOT, 1), pltpu.roll(here, SLOT, 1))
        z_up = jnp.where(open_up, edge[g], pltpu.roll(here, TILE - 1, 1))
        z_down = jnp.where(open_low, edge[g], pltpu.roll(here, 1, 1))
        return x_up, x_down, y_up(here), y_down(here), z_up, z_down

    edge[...] = jnp.zeros_like(edge)
    gather_edge(vol)
    zero = jnp.zeros((ROWS_Y, TILE), jnp.float32)
    center = 0.5 * (UPPER_BOUND + LOWER_BOUND)
    halfwidth = 0.5 * (UPPER_BOUND - LOWER_BOUND)
    spread = center / halfwidth
    damping = 1.0 / spread
    for ref in (sa, sb):
        put(ref, 0, zero)
        put(ref, EXT - 1, zero)
    put(ax, 0, jnp.minimum(main(vol, 0), main(vol, 1)))

    def inverse_of(value):
        return jnp.where(value > 0.0, 1.0 / jnp.where(value > 0.0, value, 1.0), 0.0)

    def prepare(x, carry):
        v = main(vol, x)
        upper = jnp.minimum(v, main(vol, x + 1))
        z_up, z_down = z_sides(v, strip_value(hvol, x))
        z_up = jnp.where((lane == TILE - 1) & (lane != up_lane), 0.0, z_up)
        z_down = jnp.where((lane == 0) & (lane != low_lane), 0.0, z_down)
        parts = [jnp.minimum(v, n) for n in (y_up(v), y_down(v), z_up, z_down)]
        whole = SHIFT_WEIGHT * v + upper + main(ax, x - 1) + parts[0] + parts[1] + parts[2] + parts[3]
        scale = inverse_of(whole)
        put(ax, x, upper)
        for ref, value in zip((ayu, ayl, azu, azl, diag, inv), parts + [whole, scale]):
            put(ref, x, value)
        search = (main(res, x) * scale) * (1.0 / center)
        put(sa, x, search)
        put(total, x, search)
        return carry

    lax.fori_loop(1, EXT - 1, prepare, 0)
    for g in range(GROUPS):
        v = hvol[g]
        parts = [jnp.minimum(v, n) for n in strip_sides(hvol, g)]
        whole = SHIFT_WEIGHT * v
        for value in parts:
            whole = whole + value
        scale = inverse_of(whole)
        for i, value in enumerate(parts + [whole, scale]):
            hcoef[i, g] = value
        search = (hres[g] * scale) * (1.0 / center)
        hsa[g] = search
        htotal[g] = search

    now, then, hnow, hthen = sa, sb, hsa, hsb
    for iteration in range(ITERS - 1):
        damping_next = 1.0 / (2.0 * spread - damping)
        keep = damping_next * damping
        push = 2.0 * damping_next / halfwidth
        damping = damping_next
        gather_edge(now)

        def iterate(x, carry, now=now, then=then, hnow=hnow, keep=keep, push=push):
            s = main(now, x)
            z_up, z_down = z_sides(s, strip_value(hnow, x))
            flow = main(ax, x) * main(now, x + 1) + main(ax, x - 1) * main(now, x - 1)
            flow = flow + (main(ayu, x) * y_up(s) + main(ayl, x) * y_down(s))
            flow = flow + (main(azu, x) * z_up + main(azl, x) * z_down)
            residual = main(res, x) - (main(diag, x) * s - flow)
            put(res, x, residual)
            search = keep * s + push * (residual * main(inv, x))
            put(then, x, search)
            put(total, x, main(total, x) + search)
            return carry

        lax.fori_loop(1, EXT - 1, iterate, 0)
        for g in range(GROUPS):
            s = hnow[g]
            flow = zero
            for i, value in enumerate(strip_sides(hnow, g)):
                flow = flow + hcoef[i, g] * value
            residual = hres[g] - (hcoef[6, g] * s - flow)
            hres[g] = residual
            search = keep * s + push * (residual * hcoef[7, g])
            hthen[g] = search
            htotal[g] = htotal[g] + search
        now, then, hnow, hthen = then, now, hthen, hnow

    lanes = lane_index()

    def spread_boxes(pieces, row):
        for k in range(count):
            value = None
            for r in reversed(range(PER_TILE)):
                shift = (BOX * (r - k)) % TILE
                piece = pltpu.roll(pieces[r], shift, 1) if shift else pieces[r]
                value = piece if value is None else jnp.where(lanes < BOX * (r + 1), piece, value)
            packed[pl.ds(pl.multiple_of(k * RETURN_ROWS + row, 8), TILES), :] = value

    def core(i, carry):
        base = (i + HALO - 1) * ROWS_Y + SIDE
        pieces = [total[pl.ds(base + r, TILES, stride=PER_TILE), :] for r in range(PER_TILE)]
        spread_boxes(pieces, i * TILES)
        return carry

    lax.fori_loop(0, PADDED, core, 0)

    def output(i, carry):
        pressure[i] = total[pl.ds(pl.multiple_of((i + HALO) * ROWS_Y + SIDE, 8), BOX), :]
        return carry

    lax.fori_loop(0, BOX, output, 0)
    for f, y in enumerate((SIDE - 1, SIDE + BOX)):
        pieces = [
            total[pl.ds((HALO + r) * ROWS_Y + y, TILES, stride=PER_TILE * ROWS_Y), :]
            for r in range(PER_TILE)
        ]
        spread_boxes(pieces, PADDED * TILES + f * TILES)
    z_row = PADDED * TILES + 2 * TILES
    for k in (0, count - 1):
        packed[k * RETURN_ROWS + z_row : k * RETURN_ROWS + z_row + 2 * TILES, :] = jnp.zeros(
            (2 * TILES, TILE), jnp.float32
        )
    for block in range(TILES):
        for r in range(PER_TILE):
            start = (HALO + PER_TILE * block + r) * ROWS_Y + SIDE
            turned[r * BOX : (r + 1) * BOX, :] = total[start : start + BOX, :]
        flat = turned[...].T
        for k in range(count):
            low = k * RETURN_ROWS + z_row + block
            if k:
                packed[low : low + 1, :] = flat[BOX * k - 1 : BOX * k, :]
            if k < count - 1:
                packed[low + TILES : low + TILES + 1, :] = flat[BOX * k + BOX : BOX * k + BOX + 1, :]
    half = GROUP // PER_TILE
    row4 = lax.broadcasted_iota(jnp.int32, (half, TILE), 1)
    box = jnp.where(at_top, count - 1, 0)
    target = box * RETURN_ROWS + z_row + jnp.where(at_top, TILES, 0)
    for g in range(1, GROUPS - 1):
        turned[0:BOX, :] = htotal[g, SIDE : SIDE + BOX]
        turned[BOX:TILE, :] = jnp.zeros((TILE - BOX, TILE), jnp.float32)
        flat = turned[...].T
        turned[...] = flat
        value = None
        for r in range(PER_TILE):
            piece = turned[pl.ds(SLOT * r + slot_lane, half, stride=SLOT * PER_TILE), :]
            piece = pltpu.roll(piece, BOX * r, 1) if r else piece
            value = piece if value is None else jnp.where(row4 // BOX == r, piece, value)
        packed[pl.ds(target + (g - 1) * half, half), :] = value
    copies = [
        pltpu.make_async_copy(
            packed.at[pl.ds(pl.multiple_of(box_of_row[d] * RETURN_ROWS, 8), RETURN_ROWS)],
            rows.at[d],
            sem.at[d],
        )
        for d in range(lanes_by)
    ]
    for copy in copies:
        copy.start()
    for copy in copies:
        copy.wait()


def assemble_call(table, side, recv):
    count = table.shape[0]
    return pl.pallas_call(
        functools.partial(assemble_kernel, count=count),
        in_specs=[SMEM_SPEC, SMEM_SPEC, ANY_SPEC],
        out_specs=[VMEM_SPEC] * 6,
        out_shape=[
            struct(BOX * BOX, TILE),
            struct(HALO * BOX, TILE),
            struct(HALO * BOX, TILE),
            struct(BOX // GROUP, BOX, TILE),
            struct(BOX, TILE),
            struct(BOX, TILE),
        ],
        scratch_shapes=[
            pltpu.VMEM((count, ROWS, TILE), jnp.float32),
            pltpu.SemaphoreType.DMA((count,)),
        ],
        name="brick",
    )(table, side, recv)


def halo(parts):
    brick, first, last, strip, strip_first, strip_last = parts
    nx, ny = lax.axis_size("bx"), lax.axis_size("by")
    nz = lax.axis_size("bz")
    middle = lax.ppermute(strip, "bz", [(i, nz - 1 - i) for i in range(nz)])
    up = [(i, i + 1) for i in range(nx - 1)]
    down = [(j, i) for i, j in up]
    cross_up = [(i * nz + z, j * nz + nz - 1 - z) for i, j in up for z in range(nz)]
    cross_down = [(i * nz + z, j * nz + nz - 1 - z) for i, j in down for z in range(nz)]
    x_lo = lax.ppermute(last, "bx", up)
    x_hi = lax.ppermute(first, "bx", down)
    z_lo = lax.ppermute(strip_last, ("bx", "bz"), cross_up)
    z_hi = lax.ppermute(strip_first, ("bx", "bz"), cross_down)
    cubes = [v.reshape(-1, BOX, TILE) for v in (x_lo, brick, x_hi, z_lo, middle, z_hi)]

    def edge(start):
        return jnp.concatenate([v[:, start : start + SIDE] for v in cubes], axis=0)

    y_up = [(i, i + 1) for i in range(ny - 1)]
    y_lo = lax.ppermute(edge(BOX - SIDE), "by", y_up)
    y_hi = lax.ppermute(edge(0), "by", [(j, i) for i, j in y_up])
    return brick, x_lo, x_hi, middle, z_lo, z_hi, y_lo, y_hi


def solve_call(box_of_row, side, count, volume, source):
    lanes_by = box_of_row.shape[0]
    wide = pltpu.VMEM((EXT * ROWS_Y, TILE), jnp.float32)
    narrow = pltpu.VMEM((GROUPS, ROWS_Y, TILE), jnp.float32)
    return pl.pallas_call(
        functools.partial(solve_kernel, count=count, lanes_by=lanes_by),
        in_specs=[SMEM_SPEC, SMEM_SPEC] + [VMEM_SPEC] * 16,
        out_specs=[VMEM_SPEC, ANY_SPEC],
        out_shape=[struct(BOX, BOX, count * BOX), struct(lanes_by, RETURN_ROWS, TILE)],
        scratch_shapes=[wide] * 12
        + [narrow] * 5
        + [
            pltpu.VMEM((8, GROUPS, ROWS_Y, TILE), jnp.float32),
            narrow,
            pltpu.VMEM((TILE, TILE), jnp.float32),
            pltpu.VMEM((count * RETURN_ROWS, TILE), jnp.float32),
            pltpu.SemaphoreType.DMA((lanes_by,)),
        ],
        name="solve",
    )(box_of_row, side, *volume, *source)


def routing(placement, capacity):
    lanes = lax.axis_size("by")
    own_index = lax.axis_index("by")
    table = placement[0, :, 0, :]
    per_brick = table.shape[1]
    entries = lanes * per_brick
    owners = table.reshape(entries)
    onehot = (owners[:, None] == jnp.arange(lanes, dtype=jnp.int32)[None, :]).astype(jnp.int32)
    ranks = jnp.sum((jnp.cumsum(onehot, axis=0) - onehot) * onehot, axis=1)
    matches = (table == own_index).astype(jnp.int32)
    send_slot = jnp.sum(matches * ranks.reshape(lanes, per_brick), axis=1)
    slot_match = (
        (owners == own_index)[:, None]
        & (ranks[:, None] == jnp.arange(capacity, dtype=jnp.int32)[None, :])
    ).astype(jnp.int32)
    row_value = jnp.arange(entries, dtype=jnp.int32) // per_brick
    slot_row = jnp.sum(slot_match * row_value[:, None], axis=0)
    brick_table = lax.dynamic_index_in_dim(table, own_index, 0, keepdims=False)
    all_rows = jnp.arange(lanes, dtype=jnp.int32)
    box_of_row = jnp.sum(
        (brick_table[None, :] == all_rows[:, None]).astype(jnp.int32)
        * jnp.arange(per_brick, dtype=jnp.int32)[None, :],
        axis=1,
    )
    return send_slot, slot_row, brick_table, box_of_row


def exchange(rows):
    return lax.all_to_all(rows, "by", split_axis=0, concat_axis=0, tiled=True)


def local(velocity, fraction, placement):
    send_slot, slot_row, brick_table, box_of_row = routing(placement, velocity.shape[0])
    planes, volume_rows = volume_call(send_slot, fraction)
    volume_recv = exchange(volume_rows)
    masses, source_rows = flux_call(send_slot, jnp.swapaxes(velocity, 0, 1), planes)
    source_recv = exchange(source_rows)
    updated, apertures = update_call(masses, planes)
    side = lax.axis_index("bz").reshape(1)
    volume = halo(assemble_call(brick_table, side, volume_recv))
    source = halo(assemble_call(brick_table, side, source_recv))
    pressure, rows = solve_call(box_of_row, side, placement.shape[3], volume, source)
    returned = exchange(rows)
    corrected = correct_call(slot_row, updated, apertures, returned)
    return (jnp.swapaxes(corrected, 0, 1), pressure)


def solution(mesh):
    in_specs = (
        P(("bx", "by", "bz"), None, None),
        P(("bx", "by", "bz"), None),
        P("bx", None, "bz", None),
    )
    out_specs = (P(("bx", "by", "bz"), None, None), P("bx", "by", "bz"))
    return jax.shard_map(local, mesh=mesh, in_specs=in_specs, out_specs=out_specs, check_vma=False)
```

```python
import functools

import jax
import jax.numpy as jnp
from jax import lax
from jax.experimental import pallas as pl
from jax.experimental.pallas import tpu as pltpu
from jax.sharding import PartitionSpec as P

BOX = 32
ITERS = 4
PADDED = BOX + 2
PLANE = PADDED * PADDED
TILE = 128
WIDE = 10 * TILE
INNER = BOX * BOX
TILES = INNER // TILE
PER_TILE = TILE // BOX
ROWS = BOX * TILES
RETURN_ROWS = PADDED * TILES + 4 * TILES
STEP_DT = 0.25
SHIFT_WEIGHT = 0.5
LOWER_BOUND = 0.5 / 6.5
UPPER_BOUND = 2.0

VMEM_SPEC = pl.BlockSpec(memory_space=pltpu.VMEM)
SMEM_SPEC = pl.BlockSpec(memory_space=pltpu.SMEM)
ANY_SPEC = pl.BlockSpec(memory_space=pl.ANY)
HBM_SPEC = pl.BlockSpec(memory_space=pltpu.HBM)


def lane_index():
    return lax.broadcasted_iota(jnp.int32, (8, TILE), 1)


def inside_plane():
    flat = lax.broadcasted_iota(jnp.int32, (8, WIDE), 1)
    row = flat // PADDED
    col = flat % PADDED
    return (row >= 1) & (row <= BOX) & (col >= 1) & (col <= BOX)


def ahead(values, offset):
    return pltpu.roll(values, WIDE - offset, 1)


def behind(values, offset):
    return pltpu.roll(values, offset, 1)


def compact(values, offset, lanes):
    tiles = [values[:, t * TILE : (t + 1) * TILE] for t in range(WIDE // TILE)]
    out = []
    for q in range(TILES):
        pieces = []
        for r in range(PER_TILE):
            start = (q * PER_TILE + r + 1) * PADDED + 1 + offset
            index, lane = divmod(start, TILE)
            shift = (BOX * r - lane) % TILE
            piece = pltpu.roll(tiles[index], shift, 1) if shift else tiles[index]
            if lane + BOX > TILE:
                rest = pltpu.roll(tiles[index + 1], shift, 1) if shift else tiles[index + 1]
                piece = jnp.where(lanes < BOX * r + TILE - lane, piece, rest)
            pieces.append(piece)
        value = pieces[-1]
        for r in reversed(range(PER_TILE - 1)):
            value = jnp.where(lanes < BOX * (r + 1), pieces[r], value)
        out.append(value)
    return out


def aligned_plane(load, x, lanes):
    start = x * (PLANE // TILE) + (x * (PLANE % TILE)) // TILE
    amount = (x * (PLANE % TILE)) % TILE
    block = load(pl.multiple_of(start * TILE, TILE))
    tiles = [
        pltpu.roll(block[:, t * TILE : (t + 1) * TILE], TILE - amount, 1)
        for t in range(WIDE // TILE)
    ]
    keep = lanes < TILE - amount
    return [
        jnp.where(keep, tiles[t], tiles[t + 1]) if t + 1 < len(tiles) else tiles[t]
        for t in range(len(tiles))
    ]


def store_plane(ref, index, tiles):
    for t, tile in enumerate(tiles):
        ref[index + (slice(None), slice(t * TILE, (t + 1) * TILE))] = tile


def last_plane(ref_tail, out_ref, index):
    tail = ref_tail
    start = (PADDED - 1) * PLANE
    first = start // TILE * TILE
    span = PADDED * PLANE - first
    tail_block = jnp.concatenate([tail, jnp.zeros((8, WIDE - span), jnp.float32)], axis=1)
    out_ref[index] = pltpu.roll(tail_block, WIDE - (start - first), 1)


def put_rows(ref, x, tiles):
    for q, tile in enumerate(tiles):
        ref[pl.ds(x * TILES + q, 8, stride=ROWS), :] = tile


def send_rows(slots, rows_ref, out_ref, sem, count):
    copies = [
        pltpu.make_async_copy(
            rows_ref.at[pl.ds(pl.multiple_of(slots[d] * ROWS, ROWS), ROWS)],
            out_ref.at[d],
            sem.at[d],
        )
        for d in range(count)
    ]
    for copy in copies:
        copy.start()
    for copy in copies:
        copy.wait()


def volume_kernel(slots, fraction, planes, rows, packed, tail, sem, *, lanes_by):
    lanes = lane_index()

    def align(x):
        tiles = aligned_plane(
            lambda s: fraction[:, pl.ds(s, WIDE)].astype(jnp.float32) * (1.0 / 256.0), x, lanes
        )
        store_plane(planes, (x,), tiles)

    def body(x, carry):
        align(x)
        return carry

    lax.fori_loop(0, PADDED - 1, body, 0)
    start = (PADDED - 1) * PLANE
    first = start // TILE * TILE
    span = PADDED * PLANE - first
    tail[...] = jnp.zeros_like(tail)
    tail[:, 0:span] = fraction[:, first : PADDED * PLANE].astype(jnp.float32) * (1.0 / 256.0)
    planes[PADDED - 1] = ahead(tail[...], start - first)

    def pack(x, carry):
        put_rows(packed, x, compact(planes[x + 1], 0, lanes))
        return carry

    lax.fori_loop(0, BOX, pack, 0)
    send_rows(slots, packed, rows, sem, lanes_by)


def flux_kernel(slots, velocity, planes, masses, rows, field, tail, carry_ref, packed, sem, *, lanes_by):
    lanes = lane_index()
    inside = inside_plane()

    def align(x):
        for c in range(3):
            store_plane(field, (x, c), aligned_plane(lambda s: velocity[c, :, pl.ds(s, WIDE)], x, lanes))

    def align_body(x, carry):
        align(x)
        return carry

    lax.fori_loop(0, PADDED - 1, align_body, 0)
    start = (PADDED - 1) * PLANE
    first = start // TILE * TILE
    span = PADDED * PLANE - first
    tail[...] = jnp.zeros_like(tail)
    for c in range(3):
        tail[:, 0:span] = velocity[c, :, first : PADDED * PLANE]
        field[PADDED - 1, c] = ahead(tail[...], start - first)

    def face(volume, volume_ahead, here, there, heading):
        speed = 0.5 * (here[heading] + there[heading])
        flow = jnp.minimum(volume, volume_ahead) * speed
        upwind = speed > 0.0
        return [flow * jnp.where(upwind, here[c], there[c]) for c in range(3)] + [flow]

    def x_face(x):
        return face(
            planes[x], planes[x + 1], [field[x, c] for c in range(3)], [field[x + 1, c] for c in range(3)], 0
        )

    for c, value in enumerate(x_face(0)):
        carry_ref[c] = value
    for c in range(3):
        masses[0, c] = jnp.zeros((8, WIDE), jnp.float32)
        masses[PADDED - 1, c] = jnp.zeros((8, WIDE), jnp.float32)

    def step(x, carry):
        volume = planes[x]
        here = [field[x, c] for c in range(3)]
        upper = x_face(x)
        total = [upper[c] - carry_ref[c] for c in range(4)]
        for c in range(4):
            carry_ref[c] = upper[c]
        for heading, offset in ((1, PADDED), (2, 1)):
            faces = face(volume, ahead(volume, offset), here, [ahead(v, offset) for v in here], heading)
            total = [total[c] + faces[c] - behind(faces[c], offset) for c in range(4)]
        for c in range(3):
            masses[x, c] = jnp.where(inside, volume * here[c] - STEP_DT * total[c], 0.0)
        put_rows(packed, x - 1, compact(-total[3], 0, lanes))
        return carry

    lax.fori_loop(1, PADDED - 1, step, 0)
    send_rows(slots, packed, rows, sem, lanes_by)


def update_kernel(masses, planes, updated, apertures):
    lanes = lane_index()
    inside = inside_plane()

    def put(ref, index, tiles):
        for q, tile in enumerate(tiles):
            ref[index + (slice(None), slice(q * TILE, (q + 1) * TILE))] = tile

    def neighbours(here, below, above):
        total = here + below + above
        for offset in (PADDED, 1):
            total = total + ahead(here, offset) + behind(here, offset)
        return total

    def step(x, carry):
        volume = planes[x]
        weight = jnp.where(inside, volume, 0.0)
        below = jnp.where(inside & (x > 1), planes[x - 1], 0.0)
        above = jnp.where(inside & (x < BOX), planes[x + 1], 0.0)
        weights = neighbours(weight, below, above)
        inverse = 1.0 / jnp.where(weights > 0.0, weights, 1.0)
        cut = volume < 1.0
        for c in range(3):
            here = masses[x, c]
            spread = neighbours(here, masses[x - 1, c], masses[x + 1, c]) * inverse
            put(updated, (x - 1, c), compact(jnp.where(cut, spread, here), 0, lanes))
        put(apertures, (x - 1, 0), compact(jnp.minimum(volume, planes[x - 1]), 0, lanes))
        put(apertures, (x - 1, 1), compact(jnp.minimum(volume, planes[x + 1]), 0, lanes))
        for axis, offset in ((1, PADDED), (2, 1)):
            aperture = jnp.minimum(volume, ahead(volume, offset))
            put(apertures, (x - 1, 2 * axis), compact(aperture, -offset, lanes))
            put(apertures, (x - 1, 2 * axis + 1), compact(aperture, 0, lanes))
        return carry

    lax.fori_loop(1, PADDED - 1, step, 0)


STEP_X = 4


def correct_kernel(rows, updated, apertures, returned, out, boxes, sem):
    step = pl.program_id(0)
    lanes = lane_index()

    @pl.when(step == 0)
    def _():
        copies = [
            pltpu.make_async_copy(
                returned.at[rows[s]], boxes.at[pl.ds(s * RETURN_ROWS, RETURN_ROWS)], sem.at[s]
            )
            for s in range(8)
        ]
        for copy in copies:
            copy.start()
        for copy in copies:
            copy.wait()

    def tile_of(row):
        return boxes[pl.ds(row, 8, stride=RETURN_ROWS), :]

    base = step * STEP_X
    faces = [
        tile_of(PADDED * TILES + f * TILES + step) for f in range(4)
    ]

    for i in range(STEP_X):
        x = base + i
        below = [tile_of(x * TILES + q) for q in range(TILES)]
        here = [tile_of((x + 1) * TILES + q) for q in range(TILES)]
        above = [tile_of((x + 2) * TILES + q) for q in range(TILES)]
        y_low, y_high = [
            pltpu.roll(faces[f], (TILE - BOX * i) % TILE, 1) if i else faces[f] for f in (0, 1)
        ]
        z_low, z_high = faces[2], faces[3]
        quarter = [pltpu.roll(t, BOX, 1) for t in here]
        reverse = [pltpu.roll(t, TILE - BOX, 1) for t in here]
        for q in range(TILES):
            p = here[q]
            before = quarter[q - 1] if q else pltpu.roll(y_low, 0, 1)
            y_behind = jnp.where(lanes < BOX, before, quarter[q])
            after = reverse[q + 1] if q + 1 < TILES else pltpu.roll(y_high, TILE - BOX, 1)
            y_ahead = jnp.where(lanes < TILE - BOX, reverse[q], after)
            z_behind = pltpu.roll(p, 1, 1)
            z_ahead = pltpu.roll(p, TILE - 1, 1)
            low = pltpu.roll(z_low, (TILE - TILES * i - q) % TILE, 1) if i + q else z_low
            high = pltpu.roll(z_high, (BOX - 1 - TILES * i - q) % TILE, 1)
            z_behind = jnp.where(lanes % BOX == 0, low, z_behind)
            z_ahead = jnp.where(lanes % BOX == BOX - 1, high, z_ahead)
            cut = slice(q * TILE, (q + 1) * TILE)
            around = ((below[q], above[q]), (y_behind, y_ahead), (z_behind, z_ahead))
            for c, (lower, upper) in enumerate(around):
                slope = 0.5 * (
                    apertures[i, 2 * c + 1, :, cut] * (upper - p)
                    + apertures[i, 2 * c, :, cut] * (p - lower)
                )
                out[c, :, i * INNER + q * TILE : i * INNER + (q + 1) * TILE] = updated[i, c, :, cut] - slope


def struct(*shape):
    return jax.ShapeDtypeStruct(shape, jnp.float32)


def volume_call(send_slot, fraction):
    lanes_by = send_slot.shape[0]
    return pl.pallas_call(
        functools.partial(volume_kernel, lanes_by=lanes_by),
        in_specs=[SMEM_SPEC, VMEM_SPEC],
        out_specs=[VMEM_SPEC, HBM_SPEC],
        out_shape=[struct(PADDED, 8, WIDE), struct(lanes_by, ROWS, TILE)],
        scratch_shapes=[
            pltpu.VMEM((8 * ROWS, TILE), jnp.float32),
            pltpu.VMEM((8, WIDE), jnp.float32),
            pltpu.SemaphoreType.DMA((lanes_by,)),
        ],
        name="volume_rows",
    )(send_slot, fraction)


def flux_call(send_slot, velocity, planes):
    lanes_by = send_slot.shape[0]
    return pl.pallas_call(
        functools.partial(flux_kernel, lanes_by=lanes_by),
        in_specs=[SMEM_SPEC, VMEM_SPEC, VMEM_SPEC],
        out_specs=[VMEM_SPEC, HBM_SPEC],
        out_shape=[struct(PADDED, 3, 8, WIDE), struct(lanes_by, ROWS, TILE)],
        scratch_shapes=[
            pltpu.VMEM((PADDED, 3, 8, WIDE), jnp.float32),
            pltpu.VMEM((8, WIDE), jnp.float32),
            pltpu.VMEM((4, 8, WIDE), jnp.float32),
            pltpu.VMEM((8 * ROWS, TILE), jnp.float32),
            pltpu.SemaphoreType.DMA((lanes_by,)),
        ],
        name="flux_rows",
    )(send_slot, velocity, planes)


def update_call(masses, planes):
    return pl.pallas_call(
        update_kernel,
        in_specs=[VMEM_SPEC, VMEM_SPEC],
        out_specs=[VMEM_SPEC, VMEM_SPEC],
        out_shape=[struct(BOX, 3, 8, INNER), struct(BOX, 6, 8, INNER)],
        name="updated",
    )(masses, planes)


def correct_call(slot_row, updated, apertures, returned):
    return pl.pallas_call(
        correct_kernel,
        grid=(BOX // STEP_X,),
        in_specs=[
            SMEM_SPEC,
            pl.BlockSpec((STEP_X, 3, 8, INNER), lambda i: (i, 0, 0, 0)),
            pl.BlockSpec((STEP_X, 6, 8, INNER), lambda i: (i, 0, 0, 0)),
            ANY_SPEC,
        ],
        out_specs=pl.BlockSpec((3, 8, STEP_X * INNER), lambda i: (0, 0, i)),
        out_shape=struct(3, 8, BOX * INNER),
        scratch_shapes=[
            pltpu.VMEM((8 * RETURN_ROWS, TILE), jnp.float32),
            pltpu.SemaphoreType.DMA((8,)),
        ],
        compiler_params=pltpu.CompilerParams(vmem_limit_bytes=14 << 20),
        name="corrected",
    )(
        slot_row,
        pltpu.with_memory_space_constraint(updated, pltpu.HBM),
        pltpu.with_memory_space_constraint(apertures, pltpu.HBM),
        returned,
    )


HALO = 5
SIDE = 8
EXT = BOX + 2 * HALO
ROWS_Y = BOX + 2 * SIDE
SLOT = 8
GROUP = TILE // SLOT
GROUPS = BOX // GROUP + 2


def loop(start, stop, body, unroll):
    def several(i, carry):
        for j in range(unroll):
            body(start + i * unroll + j)
        return carry

    lax.fori_loop(0, (stop - start) // unroll, several, 0)


STEP_BRICK = 8


def assemble_kernel(table, side, *refs, count):
    boxes = refs[:count]
    brick, first, last, strip, strip_first, strip_last = refs[count:]
    step = pl.program_id(0)
    steps = BOX // STEP_BRICK
    lanes = lane_index()
    lanes_brick = lax.broadcasted_iota(jnp.int32, (BOX, TILE), 1)
    source_lane = jnp.where(side[0] == 0, TILE - SLOT, 0)
    half = step % (GROUP // STEP_BRICK) * STEP_BRICK

    for x in range(STEP_BRICK):
        rows = [boxes[k][0, x * TILES : (x + 1) * TILES, :] for k in range(count)]
        for r in range(PER_TILE):
            value = None
            for k in reversed(range(count)):
                shift = (BOX * (k - r)) % TILE
                piece = pltpu.roll(rows[k], shift, 1) if shift else rows[k]
                value = piece if value is None else jnp.where(lanes < BOX * (k + 1), piece, value)
            brick[pl.ds(x * BOX + r, TILES, stride=PER_TILE), :] = value
    group = step // (GROUP // STEP_BRICK)
    value = jnp.zeros((BOX, TILE), jnp.float32)
    for x in range(STEP_BRICK):
        lane = (half + x) * SLOT
        plane = brick[x * BOX : (x + 1) * BOX, :]
        moved = pltpu.roll(plane, (lane - source_lane + TILE) % TILE, 1)
        value = jnp.where(lanes_brick // SLOT == half + x, moved, value)

    @pl.when(half == 0)
    def _():
        strip[group] = value

    @pl.when(half != 0)
    def _():
        strip[group] = jnp.where(lanes_brick // SLOT >= half, value, strip[group])

    @pl.when(step == 0)
    def _():
        first[...] = brick[0 : HALO * BOX, :]

    @pl.when(step == steps - 1)
    def _():
        last[...] = brick[(STEP_BRICK - HALO) * BOX : STEP_BRICK * BOX, :]
        strip_first[...] = strip[0]
        strip_last[...] = strip[BOX // GROUP - 1]


def solve_kernel(box_of_row, side, *refs, count, lanes_by):
    volume_in, source_in = refs[0:8], refs[8:16]
    pressure, rows = refs[16:18]
    scratch = refs[18:]
    (vol, ax, ay, azu, azl, diag, inv, res, sa, sb, total) = scratch[0:11]
    (hvol, hres, hsa, hsb, htotal, edge_a, edge_b, hcoef, turned, packed, sem) = scratch[11:]
    lane = lane_index()
    at_top = side[0] == 0
    edge_lane = jnp.where(at_top, TILE - 1, 0)
    slot_lane = jnp.where(at_top, 0, SLOT - 1)
    up_lane = jnp.where(at_top, TILE - 1, -1)
    low_lane = jnp.where(at_top, -1, 0)
    open_up = (lane % SLOT == SLOT - 1) & (low_lane == 0)
    open_low = (lane % SLOT == 0) & (up_lane >= 0)
    row_tiles = range(ROWS_Y // 8)

    def base(x):
        return pl.multiple_of(x * ROWS_Y, 8)

    def tile(ref, start, t, offset=0):
        return ref[pl.ds(start + 8 * t + offset, 8), :]

    def put(ref, start, t, value):
        ref[pl.ds(start + 8 * t, 8), :] = value

    def strip_base(g):
        return g * ROWS_Y + 8

    def fill(ext, strips, parts):
        brick, x_lo, x_hi, middle, z_lo, z_hi, y_lo, y_hi = parts

        def rows_of(x):
            ext[pl.ds(base(x), SIDE), :] = y_lo[x]
            ext[pl.ds(base(x) + SIDE + BOX, SIDE), :] = y_hi[x]

        def body(i):
            ext[pl.ds(base(i + HALO) + SIDE, BOX), :] = brick[pl.ds(pl.multiple_of(i * BOX, 8), BOX), :]
            rows_of(i + HALO)

        loop(0, BOX, body, 4)
        for i in range(HALO):
            for x, part in ((i, x_lo), (HALO + BOX + i, x_hi)):
                ext[x * ROWS_Y + SIDE : x * ROWS_Y + SIDE + BOX, :] = part[i * BOX : (i + 1) * BOX, :]
                rows_of(x)
        pieces = [z_lo[...]] + [middle[g] for g in range(GROUPS - 2)] + [z_hi[...]]
        for g, piece in enumerate(pieces):
            start = strip_base(g)
            strips[start : start + SIDE, :] = y_lo[EXT + g]
            strips[start + SIDE : start + SIDE + BOX, :] = piece
            strips[start + SIDE + BOX : start + ROWS_Y, :] = y_hi[EXT + g]

    fill(vol, hvol, volume_in)
    fill(res, hres, source_in)
    guard = jnp.zeros((8, TILE), jnp.float32)
    for ref in (hvol, hsa, hsb):
        ref[0:8, :] = guard
        ref[GROUPS * ROWS_Y + 8 : GROUPS * ROWS_Y + 16, :] = guard
    for ref in (edge_a, edge_b):
        ref[...] = jnp.zeros_like(ref)

    def place(x):
        group = (x + GROUP - HALO) // GROUP
        where = (x + GROUP - HALO) % GROUP * SLOT + slot_lane
        return pl.multiple_of(group * ROWS_Y + 8, 8), where

    def to_edge(edge, start, t, where, value):
        moved = pltpu.roll(value, (where - edge_lane + TILE) % TILE, 1)
        pltpu.store(edge.at[pl.ds(start + 8 * t, 8), :], moved, mask=lane == where)

    def z_sides(value, strips, start, t, where):
        outside = pltpu.roll(tile(strips, start, t), (edge_lane - where + TILE) % TILE, 1)
        up = jnp.where(lane == up_lane, outside, pltpu.roll(value, TILE - 1, 1))
        down = jnp.where(lane == low_lane, outside, pltpu.roll(value, 1, 1))
        return up, down

    def strip_sides(strips, edge, g, t):
        here = tile(strips, strip_base(g), t)
        following = tile(strips, strip_base(min(g + 1, GROUPS - 1)), t)
        previous = tile(strips, strip_base(max(g - 1, 0)), t)
        x_up = pltpu.roll(jnp.where(lane < SLOT, following, here), TILE - SLOT, 1)
        x_down = pltpu.roll(jnp.where(lane >= TILE - SLOT, previous, here), SLOT, 1)
        beyond = tile(edge, strip_base(g), t)
        z_up = jnp.where(open_up, beyond, pltpu.roll(here, TILE - 1, 1))
        z_down = jnp.where(open_low, beyond, pltpu.roll(here, 1, 1))
        y_up = tile(strips, strip_base(g), t, 1)
        y_down = tile(strips, strip_base(g), t, -1)
        return x_up, x_down, y_up, y_down, z_up, z_down

    def volume_edge(x):
        start, where = place(x)
        for t in row_tiles:
            to_edge(edge_a, start, t, where, tile(vol, base(x), t))

    loop(1, EXT - 1, volume_edge, 4)
    center = 0.5 * (UPPER_BOUND + LOWER_BOUND)
    halfwidth = 0.5 * (UPPER_BOUND - LOWER_BOUND)
    spread = center / halfwidth
    damping = 1.0 / spread
    for t in row_tiles:
        for ref in (sa, sb):
            put(ref, 0, t, guard)
            put(ref, (EXT - 1) * ROWS_Y, t, guard)
        put(ax, 0, t, jnp.minimum(tile(vol, 0, t), tile(vol, ROWS_Y, t)))
    put(ay, ROWS_Y - 8, 0, guard)

    def inverse_of(value):
        return jnp.where(value > 0.0, 1.0 / jnp.where(value > 0.0, value, 1.0), 0.0)

    closed_up = (lane == TILE - 1) & (lane != up_lane)
    closed_low = (lane == 0) & (lane != low_lane)

    def prepare(x):
        here = base(x)
        start, where = place(x)
        for t in row_tiles:
            v = tile(vol, here, t)
            upper = jnp.minimum(v, tile(vol, here + ROWS_Y, t))
            lower = jnp.minimum(v, tile(vol, here - ROWS_Y, t))
            z_up, z_down = z_sides(v, hvol, start, t, where)
            z_up = jnp.minimum(v, jnp.where(closed_up, 0.0, z_up))
            z_down = jnp.minimum(v, jnp.where(closed_low, 0.0, z_down))
            y_up = jnp.minimum(v, tile(vol, here, t, 1))
            y_down = jnp.minimum(v, tile(vol, here, t, -1))
            whole = SHIFT_WEIGHT * v + (upper + lower) + (y_up + y_down) + (z_up + z_down)
            scale = inverse_of(whole)
            for ref, value in ((ax, upper), (ay, y_up), (azu, z_up), (azl, z_down), (diag, whole), (inv, scale)):
                put(ref, here, t, value)
            search = (tile(res, here, t) * scale) * (1.0 / center)
            put(sa, here, t, search)
            put(total, here, t, search)
            to_edge(edge_b, start, t, where, search)

    loop(1, EXT - 1, prepare, 2)
    for g in range(GROUPS):
        for t in row_tiles:
            v = tile(hvol, strip_base(g), t)
            parts = [jnp.minimum(v, n) for n in strip_sides(hvol, edge_a, g, t)]
            whole = SHIFT_WEIGHT * v
            for value in parts:
                whole = whole + value
            scale = inverse_of(whole)
            for i, value in enumerate(parts + [whole, scale]):
                hcoef[i, g * ROWS_Y + 8 * t : g * ROWS_Y + 8 * t + 8, :] = value
            search = (tile(hres, strip_base(g), t) * scale) * (1.0 / center)
            put(hsa, strip_base(g), t, search)
            put(htotal, strip_base(g), t, search)

    now, then, hnow, hthen = sa, sb, hsa, hsb
    edge, edge_next = edge_b, edge_a
    for iteration in range(ITERS - 1):
        damping_next = 1.0 / (2.0 * spread - damping)
        keep = damping_next * damping
        push = 2.0 * damping_next / halfwidth
        damping = damping_next

        def iterate(x, now=now, then=then, hnow=hnow, edge_next=edge_next, keep=keep, push=push):
            here = base(x)
            start, where = place(x)
            for t in row_tiles:
                s = tile(now, here, t)
                z_up, z_down = z_sides(s, hnow, start, t, where)
                along_x = tile(ax, here, t) * tile(now, here + ROWS_Y, t)
                along_x = along_x + tile(ax, here - ROWS_Y, t) * tile(now, here - ROWS_Y, t)
                along_y = tile(ay, here, t) * tile(now, here, t, 1)
                along_y = along_y + tile(ay, here, t, -1) * tile(now, here, t, -1)
                along_z = tile(azu, here, t) * z_up + tile(azl, here, t) * z_down
                flow = along_x + along_y + along_z
                residual = tile(res, here, t) - (tile(diag, here, t) * s - flow)
                put(res, here, t, residual)
                search = keep * s + push * (residual * tile(inv, here, t))
                put(then, here, t, search)
                put(total, here, t, tile(total, here, t) + search)
                if edge_next is not None:
                    to_edge(edge_next, start, t, where, search)

        if iteration == ITERS - 2:
            iterate = functools.partial(iterate, edge_next=None)
        loop(1, EXT - 1, iterate, 2)
        for g in range(GROUPS):
            for t in row_tiles:
                rows_here = slice(g * ROWS_Y + 8 * t, g * ROWS_Y + 8 * t + 8)
                s = tile(hnow, strip_base(g), t)
                parts = [hcoef[i, rows_here, :] * v for i, v in enumerate(strip_sides(hnow, edge, g, t))]
                flow = (parts[0] + parts[1]) + (parts[2] + parts[3]) + (parts[4] + parts[5])
                residual = tile(hres, strip_base(g), t) - (hcoef[6, rows_here, :] * s - flow)
                put(hres, strip_base(g), t, residual)
                search = keep * s + push * (residual * hcoef[7, rows_here, :])
                put(hthen, strip_base(g), t, search)
                put(htotal, strip_base(g), t, tile(htotal, strip_base(g), t) + search)
        now, then, hnow, hthen = then, now, hthen, hnow
        edge, edge_next = edge_next, edge

    lanes = lane_index()

    def spread_boxes(pieces, row):
        for k in range(count):
            value = None
            for r in reversed(range(PER_TILE)):
                shift = (BOX * (r - k)) % TILE
                piece = pltpu.roll(pieces[r], shift, 1) if shift else pieces[r]
                value = piece if value is None else jnp.where(lanes < BOX * (r + 1), piece, value)
            packed[pl.ds(pl.multiple_of(k * RETURN_ROWS + row, 8), TILES), :] = value

    def core(i):
        start = (i + HALO - 1) * ROWS_Y + SIDE
        pieces = [total[pl.ds(start + r, TILES, stride=PER_TILE), :] for r in range(PER_TILE)]
        spread_boxes(pieces, i * TILES)

    loop(0, PADDED, core, 2)

    def output(i):
        pressure[i] = total[pl.ds(base(i + HALO) + SIDE, BOX), :]

    loop(0, BOX, output, 4)
    for f, y in enumerate((SIDE - 1, SIDE + BOX)):
        pieces = [
            total[pl.ds((HALO + r) * ROWS_Y + y, TILES, stride=PER_TILE * ROWS_Y), :]
            for r in range(PER_TILE)
        ]
        spread_boxes(pieces, PADDED * TILES + f * TILES)
    z_row = PADDED * TILES + 2 * TILES
    for k in (0, count - 1):
        packed[k * RETURN_ROWS + z_row : k * RETURN_ROWS + z_row + 2 * TILES, :] = jnp.zeros(
            (2 * TILES, TILE), jnp.float32
        )
    for block in range(TILES):
        for i in range(PER_TILE):
            for r in range(PER_TILE):
                start = (HALO + PER_TILE * block + i) * ROWS_Y + SIDE + r
                turned[BOX * r + TILES * i : BOX * r + TILES * (i + 1), :] = total[
                    pl.ds(start, TILES, stride=PER_TILE), :
                ]
        flat = turned[...].T
        for k in range(count):
            low = k * RETURN_ROWS + z_row + block
            if k:
                packed[low : low + 1, :] = flat[BOX * k - 1 : BOX * k, :]
            if k < count - 1:
                packed[low + TILES : low + TILES + 1, :] = flat[BOX * k + BOX : BOX * k + BOX + 1, :]
    half = GROUP // PER_TILE
    row4 = lax.broadcasted_iota(jnp.int32, (half, TILE), 1)
    box = jnp.where(at_top, count - 1, 0)
    target = box * RETURN_ROWS + z_row + jnp.where(at_top, TILES, 0)
    for g in range(1, GROUPS - 1):
        turned[...] = jnp.zeros_like(turned)
        for r in range(PER_TILE):
            turned[BOX * r : BOX * r + TILES, :] = htotal[
                pl.ds(strip_base(g) + SIDE + r, TILES, stride=PER_TILE), :
            ]
        turned[...] = turned[...].T
        value = None
        for i in range(PER_TILE):
            piece = turned[pl.ds(SLOT * i + slot_lane, half, stride=SLOT * PER_TILE), :]
            piece = pltpu.roll(piece, TILES * i, 1) if i else piece
            value = piece if value is None else jnp.where(row4 % BOX // TILES == i, piece, value)
        packed[pl.ds(target + (g - 1) * half, half), :] = value
    copies = [
        pltpu.make_async_copy(
            packed.at[pl.ds(pl.multiple_of(box_of_row[d] * RETURN_ROWS, 8), RETURN_ROWS)],
            rows.at[d],
            sem.at[d],
        )
        for d in range(lanes_by)
    ]
    for copy in copies:
        copy.start()
    for copy in copies:
        copy.wait()


def assemble_call(table, side, recv):
    count = table.shape[0]
    fixed = [
        (HALO * BOX, TILE),
        (HALO * BOX, TILE),
        (BOX // GROUP, BOX, TILE),
        (BOX, TILE),
        (BOX, TILE),
    ]

    def box_spec(k):
        return pl.BlockSpec((1, STEP_BRICK * TILES, TILE), lambda i, table, side: (table[k], i, 0))

    def fixed_spec(shape):
        return pl.BlockSpec(shape, lambda i, table, side: (0,) * len(shape))

    return pl.pallas_call(
        functools.partial(assemble_kernel, count=count),
        grid_spec=pltpu.PrefetchScalarGridSpec(
            num_scalar_prefetch=2,
            grid=(BOX // STEP_BRICK,),
            in_specs=[box_spec(k) for k in range(count)],
            out_specs=[pl.BlockSpec((STEP_BRICK * BOX, TILE), lambda i, table, side: (i, 0))]
            + [fixed_spec(shape) for shape in fixed],
        ),
        out_shape=[struct(BOX * BOX, TILE)] + [struct(*shape) for shape in fixed],
        compiler_params=pltpu.CompilerParams(vmem_limit_bytes=6 << 20),
        name="brick",
    )(table, side, *([recv] * count))


def halo(parts):
    brick, first, last, strip, strip_first, strip_last = parts
    nx, ny = lax.axis_size("bx"), lax.axis_size("by")
    nz = lax.axis_size("bz")
    middle = lax.ppermute(strip, "bz", [(i, nz - 1 - i) for i in range(nz)])
    up = [(i, i + 1) for i in range(nx - 1)]
    down = [(j, i) for i, j in up]
    cross_up = [(i * nz + z, j * nz + nz - 1 - z) for i, j in up for z in range(nz)]
    cross_down = [(i * nz + z, j * nz + nz - 1 - z) for i, j in down for z in range(nz)]
    x_lo = lax.ppermute(last, "bx", up)
    x_hi = lax.ppermute(first, "bx", down)
    z_lo = lax.ppermute(strip_last, ("bx", "bz"), cross_up)
    z_hi = lax.ppermute(strip_first, ("bx", "bz"), cross_down)
    cubes = [v.reshape(-1, BOX, TILE) for v in (x_lo, brick, x_hi, z_lo, middle, z_hi)]

    def edge(start):
        return jnp.concatenate([v[:, start : start + SIDE] for v in cubes], axis=0)

    y_up = [(i, i + 1) for i in range(ny - 1)]
    y_lo = lax.ppermute(edge(BOX - SIDE), "by", y_up)
    y_hi = lax.ppermute(edge(0), "by", [(j, i) for i, j in y_up])
    return brick, x_lo, x_hi, middle, z_lo, z_hi, y_lo, y_hi


def solve_call(box_of_row, side, count, volume, source):
    lanes_by = box_of_row.shape[0]
    wide = pltpu.VMEM((EXT * ROWS_Y, TILE), jnp.float32)
    narrow = pltpu.VMEM((GROUPS * ROWS_Y + 16, TILE), jnp.float32)
    return pl.pallas_call(
        functools.partial(solve_kernel, count=count, lanes_by=lanes_by),
        in_specs=[SMEM_SPEC, SMEM_SPEC] + [VMEM_SPEC] * 16,
        out_specs=[VMEM_SPEC, HBM_SPEC],
        out_shape=[struct(BOX, BOX, count * BOX), struct(lanes_by, RETURN_ROWS, TILE)],
        scratch_shapes=[wide] * 11
        + [narrow] * 7
        + [
            pltpu.VMEM((8, GROUPS * ROWS_Y, TILE), jnp.float32),
            pltpu.VMEM((TILE, TILE), jnp.float32),
            pltpu.VMEM((count * RETURN_ROWS, TILE), jnp.float32),
            pltpu.SemaphoreType.DMA((lanes_by,)),
        ],
        compiler_params=pltpu.CompilerParams(vmem_limit_bytes=26 << 20),
        name="solve",
    )(box_of_row, side, *volume, *source)


def routing(placement, capacity):
    lanes = lax.axis_size("by")
    own_index = lax.axis_index("by")
    table = placement[0, :, 0, :]
    per_brick = table.shape[1]
    entries = lanes * per_brick
    owners = table.reshape(entries)
    onehot = (owners[:, None] == jnp.arange(lanes, dtype=jnp.int32)[None, :]).astype(jnp.int32)
    ranks = jnp.sum((jnp.cumsum(onehot, axis=0) - onehot) * onehot, axis=1)
    matches = (table == own_index).astype(jnp.int32)
    send_slot = jnp.sum(matches * ranks.reshape(lanes, per_brick), axis=1)
    slot_match = (
        (owners == own_index)[:, None]
        & (ranks[:, None] == jnp.arange(capacity, dtype=jnp.int32)[None, :])
    ).astype(jnp.int32)
    row_value = jnp.arange(entries, dtype=jnp.int32) // per_brick
    slot_row = jnp.sum(slot_match * row_value[:, None], axis=0)
    brick_table = lax.dynamic_index_in_dim(table, own_index, 0, keepdims=False)
    all_rows = jnp.arange(lanes, dtype=jnp.int32)
    box_of_row = jnp.sum(
        (brick_table[None, :] == all_rows[:, None]).astype(jnp.int32)
        * jnp.arange(per_brick, dtype=jnp.int32)[None, :],
        axis=1,
    )
    return send_slot, slot_row, brick_table, box_of_row


def exchange(rows):
    return lax.all_to_all(rows, "by", split_axis=0, concat_axis=0, tiled=True)


def local(velocity, fraction, placement):
    send_slot, slot_row, brick_table, box_of_row = routing(placement, velocity.shape[0])
    planes, volume_rows = volume_call(send_slot, fraction)
    volume_recv = exchange(volume_rows)
    masses, source_rows = flux_call(send_slot, jnp.swapaxes(velocity, 0, 1), planes)
    source_recv = exchange(source_rows)
    updated, apertures = update_call(masses, planes)
    side = lax.axis_index("bz").reshape(1)
    volume = halo(assemble_call(brick_table, side, volume_recv))
    source_recv, volume = lax.optimization_barrier((source_recv, volume))
    source = halo(assemble_call(brick_table, side, source_recv))
    pressure, rows = solve_call(box_of_row, side, placement.shape[3], volume, source)
    returned = exchange(pltpu.with_memory_space_constraint(rows, pltpu.HBM))
    corrected = correct_call(slot_row, updated, apertures, returned)
    return (jnp.swapaxes(corrected, 0, 1), pressure)


def solution(mesh):
    in_specs = (
        P(("bx", "by", "bz"), None, None),
        P(("bx", "by", "bz"), None),
        P("bx", None, "bz", None),
    )
    out_specs = (P(("bx", "by", "bz"), None, None), P("bx", "by", "bz"))
    return jax.shard_map(local, mesh=mesh, in_specs=in_specs, out_specs=out_specs, check_vma=False)
```

```python
import functools

import jax
import jax.numpy as jnp
from jax import lax
from jax.experimental import pallas as pl
from jax.experimental.pallas import tpu as pltpu
from jax.sharding import PartitionSpec as P

BOX = 32
ITERS = 4
PADDED = BOX + 2
PLANE = PADDED * PADDED
TILE = 128
WIDE = 10 * TILE
INNER = BOX * BOX
TILES = INNER // TILE
PER_TILE = TILE // BOX
ROWS = BOX * TILES
PITCH = ROWS + 8
RETURN_ROWS = PADDED * TILES + 4 * TILES
STEP_DT = 0.25
SHIFT_WEIGHT = 0.5
LOWER_BOUND = 0.5 / 6.5
UPPER_BOUND = 2.0

VMEM_SPEC = pl.BlockSpec(memory_space=pltpu.VMEM)
SMEM_SPEC = pl.BlockSpec(memory_space=pltpu.SMEM)
ANY_SPEC = pl.BlockSpec(memory_space=pl.ANY)
HBM_SPEC = pl.BlockSpec(memory_space=pltpu.HBM)


def lane_index():
    return lax.broadcasted_iota(jnp.int32, (8, TILE), 1)


def inside_plane():
    flat = lax.broadcasted_iota(jnp.int32, (8, WIDE), 1)
    row = flat // PADDED
    col = flat % PADDED
    return (row >= 1) & (row <= BOX) & (col >= 1) & (col <= BOX)


def ahead(values, offset):
    return pltpu.roll(values, WIDE - offset, 1)


def behind(values, offset):
    return pltpu.roll(values, offset, 1)


def compact(values, offset, lanes):
    tiles = [values[:, t * TILE : (t + 1) * TILE] for t in range(WIDE // TILE)]
    out = []
    for q in range(TILES):
        pieces = []
        for r in range(PER_TILE):
            start = (q * PER_TILE + r + 1) * PADDED + 1 + offset
            index, lane = divmod(start, TILE)
            shift = (BOX * r - lane) % TILE
            piece = pltpu.roll(tiles[index], shift, 1) if shift else tiles[index]
            if lane + BOX > TILE:
                rest = pltpu.roll(tiles[index + 1], shift, 1) if shift else tiles[index + 1]
                piece = jnp.where(lanes < BOX * r + TILE - lane, piece, rest)
            pieces.append(piece)
        value = pieces[-1]
        for r in reversed(range(PER_TILE - 1)):
            value = jnp.where(lanes < BOX * (r + 1), pieces[r], value)
        out.append(value)
    return out


def aligned_plane(load, x, lanes):
    start = x * (PLANE // TILE) + (x * (PLANE % TILE)) // TILE
    amount = (x * (PLANE % TILE)) % TILE
    block = load(pl.multiple_of(start * TILE, TILE))
    tiles = [
        pltpu.roll(block[:, t * TILE : (t + 1) * TILE], TILE - amount, 1)
        for t in range(WIDE // TILE)
    ]
    keep = lanes < TILE - amount
    return [
        jnp.where(keep, tiles[t], tiles[t + 1]) if t + 1 < len(tiles) else tiles[t]
        for t in range(len(tiles))
    ]


def store_plane(ref, index, tiles):
    for t, tile in enumerate(tiles):
        ref[index + (slice(None), slice(t * TILE, (t + 1) * TILE))] = tile


def last_plane(ref_tail, out_ref, index):
    tail = ref_tail
    start = (PADDED - 1) * PLANE
    first = start // TILE * TILE
    span = PADDED * PLANE - first
    tail_block = jnp.concatenate([tail, jnp.zeros((8, WIDE - span), jnp.float32)], axis=1)
    out_ref[index] = pltpu.roll(tail_block, WIDE - (start - first), 1)


def put_rows(ref, x, tiles):
    for q, tile in enumerate(tiles):
        ref[pl.ds(x * TILES + q, 8, stride=PITCH), :] = tile


def send_rows(slots, rows_ref, out_ref, sem, count):
    copies = [
        pltpu.make_async_copy(
            rows_ref.at[pl.ds(pl.multiple_of(slots[d] * PITCH, 8), ROWS)],
            out_ref.at[d],
            sem.at[d],
        )
        for d in range(count)
    ]
    for copy in copies:
        copy.start()
    for copy in copies:
        copy.wait()


def own_slots(table, own, lanes_by):
    per_brick = table.shape[0] // lanes_by
    count = jnp.int32(0)
    slots = []
    for d in range(lanes_by):
        slot = jnp.int32(0)
        for k in range(per_brick):
            hit = jnp.where(table[d * per_brick + k] == own[0], 1, 0)
            slot = slot + hit * count
            count = count + hit
        slots.append(slot)
    return slots


CHUNK = 8


def fetched_until(x):
    return x * PLANE // TILE * TILE + WIDE


def volume_kernel(table, own, fraction, rows, cells, packed, sem_in, sem, *, lanes_by):
    lanes = lane_index()
    fetches = []
    begin = 0
    for chunk in range(BOX // CHUNK):
        end = fetched_until((chunk + 1) * CHUNK)
        fetches.append(
            pltpu.make_async_copy(
                fraction.at[:, pl.ds(begin, end - begin)],
                cells.at[:, pl.ds(begin, end - begin)],
                sem_in.at[chunk],
            )
        )
        begin = end
    for fetch in fetches:
        fetch.start()
    slots = own_slots(table, own, lanes_by)

    def send(chunk):
        span = CHUNK * TILES
        copies = [
            pltpu.make_async_copy(
                packed.at[pl.ds(pl.multiple_of(slots[d] * PITCH + chunk * span, 8), span)],
                rows.at[d, pl.ds(chunk * span, span)],
                sem.at[chunk, d],
            )
            for d in range(lanes_by)
        ]
        for copy in copies:
            copy.start()
        return copies

    def body(x, carry):
        tiles = aligned_plane(
            lambda s: cells[:, pl.ds(s, WIDE)].astype(jnp.float32) * (1.0 / 256.0), x, lanes
        )
        put_rows(packed, x - 1, compact(jnp.concatenate(tiles, axis=1), 0, lanes))
        return carry

    copies = []
    for chunk in range(BOX // CHUNK):
        fetches[chunk].wait()
        loop(chunk * CHUNK + 1, (chunk + 1) * CHUNK + 1, lambda x: body(x, 0), 4)
        copies += send(chunk)
    for copy in copies:
        copy.wait()


def flux_kernel(slots, velocity, fraction, planes, masses, rows, field, tail, carry_ref, packed, sem, *, lanes_by):
    lanes = lane_index()
    inside = inside_plane()

    def align(x):
        tiles = aligned_plane(
            lambda s: fraction[:, pl.ds(s, WIDE)].astype(jnp.float32) * (1.0 / 256.0), x, lanes
        )
        store_plane(planes, (x,), tiles)
        for c in range(3):
            store_plane(field, (x, c), aligned_plane(lambda s: velocity[c, :, pl.ds(s, WIDE)], x, lanes))

    def align_body(x, carry):
        align(x)
        return carry

    loop(0, PADDED - 1, align, 3)
    start = (PADDED - 1) * PLANE
    first = start // TILE * TILE
    span = PADDED * PLANE - first
    tail[...] = jnp.zeros_like(tail)
    tail[:, 0:span] = fraction[:, first : PADDED * PLANE].astype(jnp.float32) * (1.0 / 256.0)
    planes[PADDED - 1] = ahead(tail[...], start - first)
    for c in range(3):
        tail[:, 0:span] = velocity[c, :, first : PADDED * PLANE]
        field[PADDED - 1, c] = ahead(tail[...], start - first)

    def face(volume, volume_ahead, here, there, heading):
        speed = 0.5 * (here[heading] + there[heading])
        flow = jnp.minimum(volume, volume_ahead) * speed
        upwind = speed > 0.0
        return [flow * jnp.where(upwind, here[c], there[c]) for c in range(3)] + [flow]

    def x_face(x):
        return face(
            planes[x], planes[x + 1], [field[x, c] for c in range(3)], [field[x + 1, c] for c in range(3)], 0
        )

    for c, value in enumerate(x_face(0)):
        carry_ref[c] = value
    for c in range(3):
        masses[0, c] = jnp.zeros((8, WIDE), jnp.float32)
        masses[PADDED - 1, c] = jnp.zeros((8, WIDE), jnp.float32)

    def step(x, carry):
        volume = planes[x]
        here = [field[x, c] for c in range(3)]
        upper = x_face(x)
        total = [upper[c] - carry_ref[c] for c in range(4)]
        for c in range(4):
            carry_ref[c] = upper[c]
        for heading, offset in ((1, PADDED), (2, 1)):
            faces = face(volume, ahead(volume, offset), here, [ahead(v, offset) for v in here], heading)
            total = [total[c] + faces[c] - behind(faces[c], offset) for c in range(4)]
        for c in range(3):
            masses[x, c] = jnp.where(inside, volume * here[c] - STEP_DT * total[c], 0.0)
        put_rows(packed, x - 1, compact(-total[3], 0, lanes))
        return carry

    lax.fori_loop(1, PADDED - 1, step, 0)
    send_rows(slots, packed, rows, sem, lanes_by)


def update_kernel(masses, planes, updated, apertures):
    lanes = lane_index()
    inside = inside_plane()

    def put(ref, index, tiles):
        for q, tile in enumerate(tiles):
            ref[index + (slice(None), slice(q * TILE, (q + 1) * TILE))] = tile

    def neighbours(here, below, above):
        total = here + below + above
        for offset in (PADDED, 1):
            total = total + ahead(here, offset) + behind(here, offset)
        return total

    def step(i, carry):
        x = pl.program_id(0) * STEP_X + i + 1
        volume = planes[x]
        weight = jnp.where(inside, volume, 0.0)
        below = jnp.where(inside & (x > 1), planes[x - 1], 0.0)
        above = jnp.where(inside & (x < BOX), planes[x + 1], 0.0)
        weights = neighbours(weight, below, above)
        inverse = 1.0 / jnp.where(weights > 0.0, weights, 1.0)
        cut = volume < 1.0
        for c in range(3):
            here = masses[x, c]
            spread = neighbours(here, masses[x - 1, c], masses[x + 1, c]) * inverse
            put(updated, (i, c), compact(jnp.where(cut, spread, here), 0, lanes))
        put(apertures, (i, 0), compact(jnp.minimum(volume, planes[x - 1]), 0, lanes))
        put(apertures, (i, 1), compact(jnp.minimum(volume, planes[x + 1]), 0, lanes))
        for axis, offset in ((1, PADDED), (2, 1)):
            aperture = jnp.minimum(volume, ahead(volume, offset))
            put(apertures, (i, 2 * axis), compact(aperture, -offset, lanes))
            put(apertures, (i, 2 * axis + 1), compact(aperture, 0, lanes))
        return carry

    loop(0, STEP_X, lambda i: step(i, 0), 4)


STEP_X = 4


def correct_kernel(rows, updated, apertures, returned, out, boxes, sem):
    step = pl.program_id(0)
    lanes = lane_index()

    @pl.when(step == 0)
    def _():
        copies = [
            pltpu.make_async_copy(
                returned.at[rows[s]], boxes.at[pl.ds(s * RETURN_ROWS, RETURN_ROWS)], sem.at[s]
            )
            for s in range(8)
        ]
        for copy in copies:
            copy.start()
        for copy in copies:
            copy.wait()

    def tile_of(row):
        return boxes[pl.ds(row, 8, stride=RETURN_ROWS), :]

    base = step * STEP_X
    faces = [
        tile_of(PADDED * TILES + f * TILES + step) for f in range(4)
    ]

    for i in range(STEP_X):
        x = base + i
        below = [tile_of(x * TILES + q) for q in range(TILES)]
        here = [tile_of((x + 1) * TILES + q) for q in range(TILES)]
        above = [tile_of((x + 2) * TILES + q) for q in range(TILES)]
        y_low, y_high = [
            pltpu.roll(faces[f], (TILE - BOX * i) % TILE, 1) if i else faces[f] for f in (0, 1)
        ]
        z_low, z_high = faces[2], faces[3]
        quarter = [pltpu.roll(t, BOX, 1) for t in here]
        reverse = [pltpu.roll(t, TILE - BOX, 1) for t in here]
        for q in range(TILES):
            p = here[q]
            before = quarter[q - 1] if q else pltpu.roll(y_low, 0, 1)
            y_behind = jnp.where(lanes < BOX, before, quarter[q])
            after = reverse[q + 1] if q + 1 < TILES else pltpu.roll(y_high, TILE - BOX, 1)
            y_ahead = jnp.where(lanes < TILE - BOX, reverse[q], after)
            z_behind = pltpu.roll(p, 1, 1)
            z_ahead = pltpu.roll(p, TILE - 1, 1)
            low = pltpu.roll(z_low, (TILE - TILES * i - q) % TILE, 1) if i + q else z_low
            high = pltpu.roll(z_high, (BOX - 1 - TILES * i - q) % TILE, 1)
            z_behind = jnp.where(lanes % BOX == 0, low, z_behind)
            z_ahead = jnp.where(lanes % BOX == BOX - 1, high, z_ahead)
            cut = slice(q * TILE, (q + 1) * TILE)
            around = ((below[q], above[q]), (y_behind, y_ahead), (z_behind, z_ahead))
            for c, (lower, upper) in enumerate(around):
                slope = 0.5 * (
                    apertures[i, 2 * c + 1, :, cut] * (upper - p)
                    + apertures[i, 2 * c, :, cut] * (p - lower)
                )
                out[c, :, i * INNER + q * TILE : i * INNER + (q + 1) * TILE] = updated[i, c, :, cut] - slope


def struct(*shape):
    return jax.ShapeDtypeStruct(shape, jnp.float32)


def volume_call(table, own, fraction, lanes_by):
    return pl.pallas_call(
        functools.partial(volume_kernel, lanes_by=lanes_by),
        in_specs=[SMEM_SPEC, SMEM_SPEC, ANY_SPEC],
        out_specs=HBM_SPEC,
        out_shape=struct(lanes_by, ROWS, TILE),
        scratch_shapes=[
            pltpu.VMEM((8, fetched_until(BOX)), jnp.int32),
            pltpu.VMEM((8 * PITCH, TILE), jnp.float32),
            pltpu.SemaphoreType.DMA((BOX // CHUNK,)),
            pltpu.SemaphoreType.DMA((BOX // CHUNK, lanes_by)),
        ],
        name="volume_rows",
    )(table, own, fraction)


def flux_call(send_slot, velocity, fraction):
    lanes_by = send_slot.shape[0]
    return pl.pallas_call(
        functools.partial(flux_kernel, lanes_by=lanes_by),
        in_specs=[SMEM_SPEC, VMEM_SPEC, VMEM_SPEC],
        out_specs=[VMEM_SPEC, VMEM_SPEC, HBM_SPEC],
        out_shape=[
            struct(PADDED, 8, WIDE),
            struct(PADDED, 3, 8, WIDE),
            struct(lanes_by, ROWS, TILE),
        ],
        scratch_shapes=[
            pltpu.VMEM((PADDED, 3, 8, WIDE), jnp.float32),
            pltpu.VMEM((8, WIDE), jnp.float32),
            pltpu.VMEM((4, 8, WIDE), jnp.float32),
            pltpu.VMEM((8 * PITCH, TILE), jnp.float32),
            pltpu.SemaphoreType.DMA((lanes_by,)),
        ],
        name="flux_rows",
    )(send_slot, velocity, fraction)


def update_call(masses, planes):
    return pl.pallas_call(
        update_kernel,
        grid=(BOX // STEP_X,),
        in_specs=[VMEM_SPEC, VMEM_SPEC],
        out_specs=[
            pl.BlockSpec((STEP_X, 3, 8, INNER), lambda i: (i, 0, 0, 0)),
            pl.BlockSpec((STEP_X, 6, 8, INNER), lambda i: (i, 0, 0, 0)),
        ],
        out_shape=[struct(BOX, 3, 8, INNER), struct(BOX, 6, 8, INNER)],
        name="updated",
    )(masses, planes)


def correct_call(slot_row, updated, apertures, returned):
    return pl.pallas_call(
        correct_kernel,
        grid=(BOX // STEP_X,),
        in_specs=[
            SMEM_SPEC,
            pl.BlockSpec((STEP_X, 3, 8, INNER), lambda i: (i, 0, 0, 0)),
            pl.BlockSpec((STEP_X, 6, 8, INNER), lambda i: (i, 0, 0, 0)),
            ANY_SPEC,
        ],
        out_specs=pl.BlockSpec((3, 8, STEP_X * INNER), lambda i: (0, 0, i)),
        out_shape=struct(3, 8, BOX * INNER),
        scratch_shapes=[
            pltpu.VMEM((8 * RETURN_ROWS, TILE), jnp.float32),
            pltpu.SemaphoreType.DMA((8,)),
        ],
        compiler_params=pltpu.CompilerParams(vmem_limit_bytes=14 << 20),
        name="corrected",
    )(
        slot_row,
        pltpu.with_memory_space_constraint(updated, pltpu.HBM),
        pltpu.with_memory_space_constraint(apertures, pltpu.HBM),
        returned,
    )


HALO = 5
SIDE = 8
EXT = BOX + 2 * HALO
ROWS_Y = BOX + 2 * SIDE
SLOT = 8
GROUP = TILE // SLOT
GROUPS = BOX // GROUP + 2


def loop(start, stop, body, unroll):
    def several(i, carry):
        for j in range(unroll):
            body(start + i * unroll + j)
        return carry

    lax.fori_loop(0, (stop - start) // unroll, several, 0)


STEP_BRICK = 8


def assemble_kernel(table, side, *refs, count):
    boxes = refs[:count]
    brick, first, last, strip, strip_first, strip_last = refs[count:]
    step = pl.program_id(0)
    steps = BOX // STEP_BRICK
    lanes = lane_index()
    lanes_brick = lax.broadcasted_iota(jnp.int32, (BOX, TILE), 1)
    source_lane = jnp.where(side[0] == 0, TILE - SLOT, 0)
    half = step % (GROUP // STEP_BRICK) * STEP_BRICK

    for x in range(STEP_BRICK):
        rows = [boxes[k][0, x * TILES : (x + 1) * TILES, :] for k in range(count)]
        for r in range(PER_TILE):
            value = None
            for k in reversed(range(count)):
                shift = (BOX * (k - r)) % TILE
                piece = pltpu.roll(rows[k], shift, 1) if shift else rows[k]
                value = piece if value is None else jnp.where(lanes < BOX * (k + 1), piece, value)
            brick[pl.ds(x * BOX + r, TILES, stride=PER_TILE), :] = value
    group = step // (GROUP // STEP_BRICK)
    value = jnp.zeros((BOX, TILE), jnp.float32)
    for x in range(STEP_BRICK):
        lane = (half + x) * SLOT
        plane = brick[x * BOX : (x + 1) * BOX, :]
        moved = pltpu.roll(plane, (lane - source_lane + TILE) % TILE, 1)
        value = jnp.where(lanes_brick // SLOT == half + x, moved, value)

    @pl.when(half == 0)
    def _():
        strip[group] = value

    @pl.when(half != 0)
    def _():
        strip[group] = jnp.where(lanes_brick // SLOT >= half, value, strip[group])

    @pl.when(step == 0)
    def _():
        first[...] = brick[0 : HALO * BOX, :]

    @pl.when(step == steps - 1)
    def _():
        last[...] = brick[(STEP_BRICK - HALO) * BOX : STEP_BRICK * BOX, :]
        strip_first[...] = strip[0]
        strip_last[...] = strip[BOX // GROUP - 1]


def solve_kernel(box_of_row, side, *refs, count, lanes_by):
    volume_in, source_in = refs[0:8], refs[8:16]
    pressure, rows = refs[16:18]
    scratch = refs[18:]
    (vol, ax, ay, azu, azl, diag, inv, res, sa, sb, total) = scratch[0:11]
    (hvol, hres, hsa, hsb, htotal, edge_a, edge_b, hcoef, turned, packed, sem) = scratch[11:]
    lane = lane_index()
    at_top = side[0] == 0
    edge_lane = jnp.where(at_top, TILE - 1, 0)
    slot_lane = jnp.where(at_top, 0, SLOT - 1)
    up_lane = jnp.where(at_top, TILE - 1, -1)
    low_lane = jnp.where(at_top, -1, 0)
    open_up = (lane % SLOT == SLOT - 1) & (low_lane == 0)
    open_low = (lane % SLOT == 0) & (up_lane >= 0)
    row_tiles = range(ROWS_Y // 8)

    def base(x):
        return pl.multiple_of(x * ROWS_Y, 8)

    def tile(ref, start, t, offset=0):
        return ref[pl.ds(start + 8 * t + offset, 8), :]

    def put(ref, start, t, value):
        ref[pl.ds(start + 8 * t, 8), :] = value

    def strip_base(g):
        return g * ROWS_Y + 8

    def fill(ext, strips, parts):
        brick, x_lo, x_hi, middle, z_lo, z_hi, y_lo, y_hi = parts

        def rows_of(x):
            ext[pl.ds(base(x), SIDE), :] = y_lo[x]
            ext[pl.ds(base(x) + SIDE + BOX, SIDE), :] = y_hi[x]

        def body(i):
            ext[pl.ds(base(i + HALO) + SIDE, BOX), :] = brick[pl.ds(pl.multiple_of(i * BOX, 8), BOX), :]
            rows_of(i + HALO)

        loop(0, BOX, body, 4)
        for i in range(HALO):
            for x, part in ((i, x_lo), (HALO + BOX + i, x_hi)):
                ext[x * ROWS_Y + SIDE : x * ROWS_Y + SIDE + BOX, :] = part[i * BOX : (i + 1) * BOX, :]
                rows_of(x)
        pieces = [z_lo[...]] + [middle[g] for g in range(GROUPS - 2)] + [z_hi[...]]
        for g, piece in enumerate(pieces):
            start = strip_base(g)
            strips[start : start + SIDE, :] = y_lo[EXT + g]
            strips[start + SIDE : start + SIDE + BOX, :] = piece
            strips[start + SIDE + BOX : start + ROWS_Y, :] = y_hi[EXT + g]

    fill(vol, hvol, volume_in)
    fill(res, hres, source_in)
    guard = jnp.zeros((8, TILE), jnp.float32)
    for ref in (hvol, hsa, hsb):
        ref[0:8, :] = guard
        ref[GROUPS * ROWS_Y + 8 : GROUPS * ROWS_Y + 16, :] = guard
    for ref in (edge_a, edge_b):
        ref[...] = jnp.zeros_like(ref)

    def place(x):
        group = (x + GROUP - HALO) // GROUP
        where = (x + GROUP - HALO) % GROUP * SLOT + slot_lane
        return pl.multiple_of(group * ROWS_Y + 8, 8), where

    def to_edge(edge, start, t, where, value):
        moved = pltpu.roll(value, (where - edge_lane + TILE) % TILE, 1)
        pltpu.store(edge.at[pl.ds(start + 8 * t, 8), :], moved, mask=lane == where)

    def z_sides(value, strips, start, t, where):
        outside = pltpu.roll(tile(strips, start, t), (edge_lane - where + TILE) % TILE, 1)
        up = jnp.where(lane == up_lane, outside, pltpu.roll(value, TILE - 1, 1))
        down = jnp.where(lane == low_lane, outside, pltpu.roll(value, 1, 1))
        return up, down

    def strip_sides(strips, edge, g, t):
        here = tile(strips, strip_base(g), t)
        following = tile(strips, strip_base(min(g + 1, GROUPS - 1)), t)
        previous = tile(strips, strip_base(max(g - 1, 0)), t)
        x_up = pltpu.roll(jnp.where(lane < SLOT, following, here), TILE - SLOT, 1)
        x_down = pltpu.roll(jnp.where(lane >= TILE - SLOT, previous, here), SLOT, 1)
        beyond = tile(edge, strip_base(g), t)
        z_up = jnp.where(open_up, beyond, pltpu.roll(here, TILE - 1, 1))
        z_down = jnp.where(open_low, beyond, pltpu.roll(here, 1, 1))
        y_up = tile(strips, strip_base(g), t, 1)
        y_down = tile(strips, strip_base(g), t, -1)
        return x_up, x_down, y_up, y_down, z_up, z_down

    def volume_edge(x):
        start, where = place(x)
        for t in row_tiles:
            to_edge(edge_a, start, t, where, tile(vol, base(x), t))

    loop(1, EXT - 1, volume_edge, 4)
    center = 0.5 * (UPPER_BOUND + LOWER_BOUND)
    halfwidth = 0.5 * (UPPER_BOUND - LOWER_BOUND)
    spread = center / halfwidth
    damping = 1.0 / spread
    for t in row_tiles:
        for ref in (sa, sb):
            put(ref, 0, t, guard)
            put(ref, (EXT - 1) * ROWS_Y, t, guard)
        put(ax, 0, t, jnp.minimum(tile(vol, 0, t), tile(vol, ROWS_Y, t)))
    put(ay, ROWS_Y - 8, 0, guard)

    def inverse_of(value):
        return jnp.where(value > 0.0, 1.0 / jnp.where(value > 0.0, value, 1.0), 0.0)

    closed_up = (lane == TILE - 1) & (lane != up_lane)
    closed_low = (lane == 0) & (lane != low_lane)

    def prepare(x):
        here = base(x)
        start, where = place(x)
        for t in row_tiles:
            v = tile(vol, here, t)
            upper = jnp.minimum(v, tile(vol, here + ROWS_Y, t))
            lower = jnp.minimum(v, tile(vol, here - ROWS_Y, t))
            z_up, z_down = z_sides(v, hvol, start, t, where)
            z_up = jnp.minimum(v, jnp.where(closed_up, 0.0, z_up))
            z_down = jnp.minimum(v, jnp.where(closed_low, 0.0, z_down))
            y_up = jnp.minimum(v, tile(vol, here, t, 1))
            y_down = jnp.minimum(v, tile(vol, here, t, -1))
            whole = SHIFT_WEIGHT * v + (upper + lower) + (y_up + y_down) + (z_up + z_down)
            scale = inverse_of(whole)
            for ref, value in ((ax, upper), (ay, y_up), (azu, z_up), (azl, z_down), (diag, whole), (inv, scale)):
                put(ref, here, t, value)
            search = (tile(res, here, t) * scale) * (1.0 / center)
            put(sa, here, t, search)
            put(total, here, t, search)
            to_edge(edge_b, start, t, where, search)

    loop(1, EXT - 1, prepare, 2)
    for g in range(GROUPS):
        for t in row_tiles:
            v = tile(hvol, strip_base(g), t)
            parts = [jnp.minimum(v, n) for n in strip_sides(hvol, edge_a, g, t)]
            whole = SHIFT_WEIGHT * v
            for value in parts:
                whole = whole + value
            scale = inverse_of(whole)
            for i, value in enumerate(parts + [whole, scale]):
                hcoef[i, g * ROWS_Y + 8 * t : g * ROWS_Y + 8 * t + 8, :] = value
            search = (tile(hres, strip_base(g), t) * scale) * (1.0 / center)
            put(hsa, strip_base(g), t, search)
            put(htotal, strip_base(g), t, search)

    now, then, hnow, hthen = sa, sb, hsa, hsb
    edge, edge_next = edge_b, edge_a
    for iteration in range(ITERS - 1):
        damping_next = 1.0 / (2.0 * spread - damping)
        keep = damping_next * damping
        push = 2.0 * damping_next / halfwidth
        damping = damping_next

        def iterate(x, now=now, then=then, hnow=hnow, edge_next=edge_next, keep=keep, push=push):
            here = base(x)
            start, where = place(x)
            for t in row_tiles:
                s = tile(now, here, t)
                z_up, z_down = z_sides(s, hnow, start, t, where)
                along_x = tile(ax, here, t) * tile(now, here + ROWS_Y, t)
                along_x = along_x + tile(ax, here - ROWS_Y, t) * tile(now, here - ROWS_Y, t)
                along_y = tile(ay, here, t) * tile(now, here, t, 1)
                along_y = along_y + tile(ay, here, t, -1) * tile(now, here, t, -1)
                along_z = tile(azu, here, t) * z_up + tile(azl, here, t) * z_down
                flow = along_x + along_y + along_z
                residual = tile(res, here, t) - (tile(diag, here, t) * s - flow)
                put(res, here, t, residual)
                search = keep * s + push * (residual * tile(inv, here, t))
                put(then, here, t, search)
                put(total, here, t, tile(total, here, t) + search)
                if edge_next is not None:
                    to_edge(edge_next, start, t, where, search)

        if iteration == ITERS - 2:
            iterate = functools.partial(iterate, edge_next=None)
        loop(1, EXT - 1, iterate, 2)
        for g in range(GROUPS):
            for t in row_tiles:
                rows_here = slice(g * ROWS_Y + 8 * t, g * ROWS_Y + 8 * t + 8)
                s = tile(hnow, strip_base(g), t)
                parts = [hcoef[i, rows_here, :] * v for i, v in enumerate(strip_sides(hnow, edge, g, t))]
                flow = (parts[0] + parts[1]) + (parts[2] + parts[3]) + (parts[4] + parts[5])
                residual = tile(hres, strip_base(g), t) - (hcoef[6, rows_here, :] * s - flow)
                put(hres, strip_base(g), t, residual)
                search = keep * s + push * (residual * hcoef[7, rows_here, :])
                put(hthen, strip_base(g), t, search)
                put(htotal, strip_base(g), t, tile(htotal, strip_base(g), t) + search)
        now, then, hnow, hthen = then, now, hthen, hnow
        edge, edge_next = edge_next, edge

    lanes = lane_index()

    def spread_boxes(pieces, row):
        for k in range(count):
            value = None
            for r in reversed(range(PER_TILE)):
                shift = (BOX * (r - k)) % TILE
                piece = pltpu.roll(pieces[r], shift, 1) if shift else pieces[r]
                value = piece if value is None else jnp.where(lanes < BOX * (r + 1), piece, value)
            packed[pl.ds(pl.multiple_of(k * RETURN_ROWS + row, 8), TILES), :] = value

    def core(i):
        start = (i + HALO - 1) * ROWS_Y + SIDE
        pieces = [total[pl.ds(start + r, TILES, stride=PER_TILE), :] for r in range(PER_TILE)]
        spread_boxes(pieces, i * TILES)

    loop(0, PADDED, core, 2)

    def output(i):
        pressure[i] = total[pl.ds(base(i + HALO) + SIDE, BOX), :]

    loop(0, BOX, output, 4)
    for f, y in enumerate((SIDE - 1, SIDE + BOX)):
        pieces = [
            total[pl.ds((HALO + r) * ROWS_Y + y, TILES, stride=PER_TILE * ROWS_Y), :]
            for r in range(PER_TILE)
        ]
        spread_boxes(pieces, PADDED * TILES + f * TILES)
    z_row = PADDED * TILES + 2 * TILES
    for k in (0, count - 1):
        packed[k * RETURN_ROWS + z_row : k * RETURN_ROWS + z_row + 2 * TILES, :] = jnp.zeros(
            (2 * TILES, TILE), jnp.float32
        )
    for block in range(TILES):
        for i in range(PER_TILE):
            for r in range(PER_TILE):
                start = (HALO + PER_TILE * block + i) * ROWS_Y + SIDE + r
                turned[BOX * r + TILES * i : BOX * r + TILES * (i + 1), :] = total[
                    pl.ds(start, TILES, stride=PER_TILE), :
                ]
        flat = turned[...].T
        for k in range(count):
            low = k * RETURN_ROWS + z_row + block
            if k:
                packed[low : low + 1, :] = flat[BOX * k - 1 : BOX * k, :]
            if k < count - 1:
                packed[low + TILES : low + TILES + 1, :] = flat[BOX * k + BOX : BOX * k + BOX + 1, :]
    half = GROUP // PER_TILE
    row4 = lax.broadcasted_iota(jnp.int32, (half, TILE), 1)
    box = jnp.where(at_top, count - 1, 0)
    target = box * RETURN_ROWS + z_row + jnp.where(at_top, TILES, 0)
    for g in range(1, GROUPS - 1):
        turned[...] = jnp.zeros_like(turned)
        for r in range(PER_TILE):
            turned[BOX * r : BOX * r + TILES, :] = htotal[
                pl.ds(strip_base(g) + SIDE + r, TILES, stride=PER_TILE), :
            ]
        turned[...] = turned[...].T
        value = None
        for i in range(PER_TILE):
            piece = turned[pl.ds(SLOT * i + slot_lane, half, stride=SLOT * PER_TILE), :]
            piece = pltpu.roll(piece, TILES * i, 1) if i else piece
            value = piece if value is None else jnp.where(row4 % BOX // TILES == i, piece, value)
        packed[pl.ds(target + (g - 1) * half, half), :] = value
    copies = [
        pltpu.make_async_copy(
            packed.at[pl.ds(pl.multiple_of(box_of_row[d] * RETURN_ROWS, 8), RETURN_ROWS)],
            rows.at[d],
            sem.at[d],
        )
        for d in range(lanes_by)
    ]
    for copy in copies:
        copy.start()
    for copy in copies:
        copy.wait()


def assemble_call(table, side, recv):
    count = table.shape[0]
    fixed = [
        (HALO * BOX, TILE),
        (HALO * BOX, TILE),
        (BOX // GROUP, BOX, TILE),
        (BOX, TILE),
        (BOX, TILE),
    ]

    def box_spec(k):
        return pl.BlockSpec((1, STEP_BRICK * TILES, TILE), lambda i, table, side: (table[k], i, 0))

    def fixed_spec(shape):
        return pl.BlockSpec(shape, lambda i, table, side: (0,) * len(shape))

    return pl.pallas_call(
        functools.partial(assemble_kernel, count=count),
        grid_spec=pltpu.PrefetchScalarGridSpec(
            num_scalar_prefetch=2,
            grid=(BOX // STEP_BRICK,),
            in_specs=[box_spec(k) for k in range(count)],
            out_specs=[pl.BlockSpec((STEP_BRICK * BOX, TILE), lambda i, table, side: (i, 0))]
            + [fixed_spec(shape) for shape in fixed],
        ),
        out_shape=[struct(BOX * BOX, TILE)] + [struct(*shape) for shape in fixed],
        compiler_params=pltpu.CompilerParams(vmem_limit_bytes=6 << 20),
        name="brick",
    )(table, side, *([recv] * count))


def halo(parts):
    brick, first, last, strip, strip_first, strip_last = parts
    nx, ny = lax.axis_size("bx"), lax.axis_size("by")
    nz = lax.axis_size("bz")
    middle = lax.ppermute(strip, "bz", [(i, nz - 1 - i) for i in range(nz)])
    up = [(i, i + 1) for i in range(nx - 1)]
    down = [(j, i) for i, j in up]
    cross_up = [(i * nz + z, j * nz + nz - 1 - z) for i, j in up for z in range(nz)]
    cross_down = [(i * nz + z, j * nz + nz - 1 - z) for i, j in down for z in range(nz)]
    x_lo = lax.ppermute(last, "bx", up)
    x_hi = lax.ppermute(first, "bx", down)
    z_lo = lax.ppermute(strip_last, ("bx", "bz"), cross_up)
    z_hi = lax.ppermute(strip_first, ("bx", "bz"), cross_down)
    cubes = [v.reshape(-1, BOX, TILE) for v in (x_lo, brick, x_hi, z_lo, middle, z_hi)]

    def edge(start):
        return jnp.concatenate([v[:, start : start + SIDE] for v in cubes], axis=0)

    y_up = [(i, i + 1) for i in range(ny - 1)]
    y_lo = lax.ppermute(edge(BOX - SIDE), "by", y_up)
    y_hi = lax.ppermute(edge(0), "by", [(j, i) for i, j in y_up])
    return brick, x_lo, x_hi, middle, z_lo, z_hi, y_lo, y_hi


def solve_call(box_of_row, side, count, volume, source):
    lanes_by = box_of_row.shape[0]
    wide = pltpu.VMEM((EXT * ROWS_Y, TILE), jnp.float32)
    narrow = pltpu.VMEM((GROUPS * ROWS_Y + 16, TILE), jnp.float32)
    return pl.pallas_call(
        functools.partial(solve_kernel, count=count, lanes_by=lanes_by),
        in_specs=[SMEM_SPEC, SMEM_SPEC] + [VMEM_SPEC] * 16,
        out_specs=[VMEM_SPEC, HBM_SPEC],
        out_shape=[struct(BOX, BOX, count * BOX), struct(lanes_by, RETURN_ROWS, TILE)],
        scratch_shapes=[wide] * 11
        + [narrow] * 7
        + [
            pltpu.VMEM((8, GROUPS * ROWS_Y, TILE), jnp.float32),
            pltpu.VMEM((TILE, TILE), jnp.float32),
            pltpu.VMEM((count * RETURN_ROWS, TILE), jnp.float32),
            pltpu.SemaphoreType.DMA((lanes_by,)),
        ],
        compiler_params=pltpu.CompilerParams(vmem_limit_bytes=26 << 20),
        name="solve",
    )(box_of_row, side, *volume, *source)


def routing(placement, capacity):
    lanes = lax.axis_size("by")
    own_index = lax.axis_index("by")
    table = placement[0, :, 0, :]
    per_brick = table.shape[1]
    entries = lanes * per_brick
    owners = table.reshape(entries)
    onehot = (owners[:, None] == jnp.arange(lanes, dtype=jnp.int32)[None, :]).astype(jnp.int32)
    ranks = jnp.sum((jnp.cumsum(onehot, axis=0) - onehot) * onehot, axis=1)
    matches = (table == own_index).astype(jnp.int32)
    send_slot = jnp.sum(matches * ranks.reshape(lanes, per_brick), axis=1)
    slot_match = (
        (owners == own_index)[:, None]
        & (ranks[:, None] == jnp.arange(capacity, dtype=jnp.int32)[None, :])
    ).astype(jnp.int32)
    row_value = jnp.arange(entries, dtype=jnp.int32) // per_brick
    slot_row = jnp.sum(slot_match * row_value[:, None], axis=0)
    brick_table = lax.dynamic_index_in_dim(table, own_index, 0, keepdims=False)
    all_rows = jnp.arange(lanes, dtype=jnp.int32)
    box_of_row = jnp.sum(
        (brick_table[None, :] == all_rows[:, None]).astype(jnp.int32)
        * jnp.arange(per_brick, dtype=jnp.int32)[None, :],
        axis=1,
    )
    return send_slot, slot_row, brick_table, box_of_row


def exchange(rows):
    return lax.all_to_all(rows, "by", split_axis=0, concat_axis=0, tiled=True)


def local(velocity, fraction, placement):
    send_slot, slot_row, brick_table, box_of_row = routing(placement, velocity.shape[0])
    own = lax.axis_index("by").reshape(1)
    table = placement.reshape(-1)
    volume_rows = volume_call(table, own, fraction, send_slot.shape[0])
    volume_recv = exchange(volume_rows)
    planes, masses, source_rows = flux_call(send_slot, jnp.swapaxes(velocity, 0, 1), fraction)
    source_recv = exchange(source_rows)
    updated, apertures = update_call(masses, planes)
    side = lax.axis_index("bz").reshape(1)
    volume = halo(assemble_call(brick_table, side, volume_recv))
    source_recv, volume = lax.optimization_barrier((source_recv, volume))
    source = halo(assemble_call(brick_table, side, source_recv))
    pressure, rows = solve_call(box_of_row, side, placement.shape[3], volume, source)
    returned = exchange(rows)
    corrected = correct_call(slot_row, updated, apertures, returned)
    return (jnp.swapaxes(corrected, 0, 1), pressure)


def solution(mesh):
    in_specs = (
        P(("bx", "by", "bz"), None, None),
        P(("bx", "by", "bz"), None),
        P("bx", None, "bz", None),
    )
    out_specs = (P(("bx", "by", "bz"), None, None), P("bx", "by", "bz"))
    return jax.shard_map(local, mesh=mesh, in_specs=in_specs, out_specs=out_specs, check_vma=False)
```

```python
import functools

import jax
import jax.numpy as jnp
from jax import lax
from jax.experimental import pallas as pl
from jax.experimental.pallas import tpu as pltpu
from jax.sharding import PartitionSpec as P

BOX = 32
ITERS = 4
PADDED = BOX + 2
PLANE = PADDED * PADDED
TILE = 128
WIDE = 10 * TILE
INNER = BOX * BOX
TILES = INNER // TILE
PER_TILE = TILE // BOX
ROWS = BOX * TILES
PITCH = ROWS + 8
RETURN_ROWS = PADDED * TILES + 4 * TILES
STEP_DT = 0.25
SHIFT_WEIGHT = 0.5
LOWER_BOUND = 0.5 / 6.5
UPPER_BOUND = 2.0

VMEM_SPEC = pl.BlockSpec(memory_space=pltpu.VMEM)
SMEM_SPEC = pl.BlockSpec(memory_space=pltpu.SMEM)
ANY_SPEC = pl.BlockSpec(memory_space=pl.ANY)
HBM_SPEC = pl.BlockSpec(memory_space=pltpu.HBM)


def lane_index():
    return lax.broadcasted_iota(jnp.int32, (8, TILE), 1)


def inside_plane():
    flat = lax.broadcasted_iota(jnp.int32, (8, WIDE), 1)
    row = flat // PADDED
    col = flat % PADDED
    return (row >= 1) & (row <= BOX) & (col >= 1) & (col <= BOX)


def ahead(values, offset):
    return pltpu.roll(values, WIDE - offset, 1)


def behind(values, offset):
    return pltpu.roll(values, offset, 1)


def compact(values, offset, lanes):
    tiles = [values[:, t * TILE : (t + 1) * TILE] for t in range(WIDE // TILE)]
    out = []
    for q in range(TILES):
        pieces = []
        for r in range(PER_TILE):
            start = (q * PER_TILE + r + 1) * PADDED + 1 + offset
            index, lane = divmod(start, TILE)
            shift = (BOX * r - lane) % TILE
            piece = pltpu.roll(tiles[index], shift, 1) if shift else tiles[index]
            if lane + BOX > TILE:
                rest = pltpu.roll(tiles[index + 1], shift, 1) if shift else tiles[index + 1]
                piece = jnp.where(lanes < BOX * r + TILE - lane, piece, rest)
            pieces.append(piece)
        value = pieces[-1]
        for r in reversed(range(PER_TILE - 1)):
            value = jnp.where(lanes < BOX * (r + 1), pieces[r], value)
        out.append(value)
    return out


def aligned_plane(load, x, lanes):
    start = x * (PLANE // TILE) + (x * (PLANE % TILE)) // TILE
    amount = (x * (PLANE % TILE)) % TILE
    block = load(pl.multiple_of(start * TILE, TILE))
    tiles = [
        pltpu.roll(block[:, t * TILE : (t + 1) * TILE], TILE - amount, 1)
        for t in range(WIDE // TILE)
    ]
    keep = lanes < TILE - amount
    return [
        jnp.where(keep, tiles[t], tiles[t + 1]) if t + 1 < len(tiles) else tiles[t]
        for t in range(len(tiles))
    ]


def store_plane(ref, index, tiles):
    for t, tile in enumerate(tiles):
        ref[index + (slice(None), slice(t * TILE, (t + 1) * TILE))] = tile


def last_plane(ref_tail, out_ref, index):
    tail = ref_tail
    start = (PADDED - 1) * PLANE
    first = start // TILE * TILE
    span = PADDED * PLANE - first
    tail_block = jnp.concatenate([tail, jnp.zeros((8, WIDE - span), jnp.float32)], axis=1)
    out_ref[index] = pltpu.roll(tail_block, WIDE - (start - first), 1)


def put_rows(ref, x, tiles):
    for q, tile in enumerate(tiles):
        ref[pl.ds(x * TILES + q, 8, stride=PITCH), :] = tile


def send_rows(slots, rows_ref, out_ref, sem, count):
    copies = [
        pltpu.make_async_copy(
            rows_ref.at[pl.ds(pl.multiple_of(slots[d] * PITCH, 8), ROWS)],
            out_ref.at[d],
            sem.at[d],
        )
        for d in range(count)
    ]
    for copy in copies:
        copy.start()
    for copy in copies:
        copy.wait()


def own_slots(table, own, lanes_by):
    per_brick = table.shape[0] // lanes_by
    count = jnp.int32(0)
    slots = []
    for d in range(lanes_by):
        slot = jnp.int32(0)
        for k in range(per_brick):
            hit = jnp.where(table[d * per_brick + k] == own[0], 1, 0)
            slot = slot + hit * count
            count = count + hit
        slots.append(slot)
    return slots


CHUNK = 8


def fetched_until(x):
    return x * PLANE // TILE * TILE + WIDE


def volume_kernel(table, own, fraction, rows, cells, packed, sem_in, sem, *, lanes_by):
    lanes = lane_index()
    fetches = []
    begin = 0
    for chunk in range(BOX // CHUNK):
        end = fetched_until((chunk + 1) * CHUNK)
        fetches.append(
            pltpu.make_async_copy(
                fraction.at[:, pl.ds(begin, end - begin)],
                cells.at[:, pl.ds(begin, end - begin)],
                sem_in.at[chunk],
            )
        )
        begin = end
    for fetch in fetches:
        fetch.start()
    slots = own_slots(table, own, lanes_by)

    def send(chunk):
        span = CHUNK * TILES
        copies = [
            pltpu.make_async_copy(
                packed.at[pl.ds(pl.multiple_of(slots[d] * PITCH + chunk * span, 8), span)],
                rows.at[d, pl.ds(chunk * span, span)],
                sem.at[chunk, d],
            )
            for d in range(lanes_by)
        ]
        for copy in copies:
            copy.start()
        return copies

    def body(x, carry):
        tiles = aligned_plane(
            lambda s: cells[:, pl.ds(s, WIDE)].astype(jnp.float32) * (1.0 / 256.0), x, lanes
        )
        put_rows(packed, x - 1, compact(jnp.concatenate(tiles, axis=1), 0, lanes))
        return carry

    copies = []
    for chunk in range(BOX // CHUNK):
        fetches[chunk].wait()
        loop(chunk * CHUNK + 1, (chunk + 1) * CHUNK + 1, lambda x: body(x, 0), 4)
        copies += send(chunk)
    for copy in copies:
        copy.wait()


def flux_kernel(slots, velocity, fraction, planes, masses, rows, field, tail, carry_ref, packed, sem, *, lanes_by):
    lanes = lane_index()
    inside = inside_plane()

    def align(x):
        tiles = aligned_plane(
            lambda s: fraction[:, pl.ds(s, WIDE)].astype(jnp.float32) * (1.0 / 256.0), x, lanes
        )
        store_plane(planes, (x,), tiles)
        for c in range(3):
            store_plane(field, (x, c), aligned_plane(lambda s: velocity[c, :, pl.ds(s, WIDE)], x, lanes))

    def align_body(x, carry):
        align(x)
        return carry

    loop(0, PADDED - 1, align, 3)
    start = (PADDED - 1) * PLANE
    first = start // TILE * TILE
    span = PADDED * PLANE - first
    tail[...] = jnp.zeros_like(tail)
    tail[:, 0:span] = fraction[:, first : PADDED * PLANE].astype(jnp.float32) * (1.0 / 256.0)
    planes[PADDED - 1] = ahead(tail[...], start - first)
    for c in range(3):
        tail[:, 0:span] = velocity[c, :, first : PADDED * PLANE]
        field[PADDED - 1, c] = ahead(tail[...], start - first)

    def face(volume, volume_ahead, here, there, heading):
        speed = 0.5 * (here[heading] + there[heading])
        flow = jnp.minimum(volume, volume_ahead) * speed
        upwind = speed > 0.0
        return [flow * jnp.where(upwind, here[c], there[c]) for c in range(3)] + [flow]

    def x_face(x):
        return face(
            planes[x], planes[x + 1], [field[x, c] for c in range(3)], [field[x + 1, c] for c in range(3)], 0
        )

    for c, value in enumerate(x_face(0)):
        carry_ref[c] = value
    for c in range(3):
        masses[0, c] = jnp.zeros((8, WIDE), jnp.float32)
        masses[PADDED - 1, c] = jnp.zeros((8, WIDE), jnp.float32)

    def step(x, carry):
        volume = planes[x]
        here = [field[x, c] for c in range(3)]
        upper = x_face(x)
        total = [upper[c] - carry_ref[c] for c in range(4)]
        for c in range(4):
            carry_ref[c] = upper[c]
        for heading, offset in ((1, PADDED), (2, 1)):
            faces = face(volume, ahead(volume, offset), here, [ahead(v, offset) for v in here], heading)
            total = [total[c] + faces[c] - behind(faces[c], offset) for c in range(4)]
        for c in range(3):
            masses[x, c] = jnp.where(inside, volume * here[c] - STEP_DT * total[c], 0.0)
        put_rows(packed, x - 1, compact(-total[3], 0, lanes))
        return carry

    lax.fori_loop(1, PADDED - 1, step, 0)
    send_rows(slots, packed, rows, sem, lanes_by)


def update_kernel(masses, planes, updated, apertures):
    lanes = lane_index()
    inside = inside_plane()

    def put(ref, index, tiles):
        for q, tile in enumerate(tiles):
            ref[index + (slice(None), slice(q * TILE, (q + 1) * TILE))] = tile

    def neighbours(here, below, above):
        total = here + below + above
        for offset in (PADDED, 1):
            total = total + ahead(here, offset) + behind(here, offset)
        return total

    def step(i, carry):
        x = pl.program_id(0) * STEP_X + i + 1
        volume = planes[x]
        weight = jnp.where(inside, volume, 0.0)
        below = jnp.where(inside & (x > 1), planes[x - 1], 0.0)
        above = jnp.where(inside & (x < BOX), planes[x + 1], 0.0)
        weights = neighbours(weight, below, above)
        inverse = 1.0 / jnp.where(weights > 0.0, weights, 1.0)
        cut = volume < 1.0
        for c in range(3):
            here = masses[x, c]
            spread = neighbours(here, masses[x - 1, c], masses[x + 1, c]) * inverse
            put(updated, (i, c), compact(jnp.where(cut, spread, here), 0, lanes))
        put(apertures, (i, 0), compact(jnp.minimum(volume, planes[x - 1]), 0, lanes))
        put(apertures, (i, 1), compact(jnp.minimum(volume, planes[x + 1]), 0, lanes))
        for axis, offset in ((1, PADDED), (2, 1)):
            aperture = jnp.minimum(volume, ahead(volume, offset))
            put(apertures, (i, 2 * axis), compact(aperture, -offset, lanes))
            put(apertures, (i, 2 * axis + 1), compact(aperture, 0, lanes))
        return carry

    loop(0, STEP_X, lambda i: step(i, 0), 4)


STEP_X = 4


def correct_kernel(rows, updated, apertures, returned, out, boxes, sem):
    step = pl.program_id(0)
    lanes = lane_index()

    @pl.when(step == 0)
    def _():
        copies = [
            pltpu.make_async_copy(
                returned.at[rows[s]], boxes.at[pl.ds(s * RETURN_ROWS, RETURN_ROWS)], sem.at[s]
            )
            for s in range(8)
        ]
        for copy in copies:
            copy.start()
        for copy in copies:
            copy.wait()

    def tile_of(row):
        return boxes[pl.ds(row, 8, stride=RETURN_ROWS), :]

    base = step * STEP_X
    faces = [
        tile_of(PADDED * TILES + f * TILES + step) for f in range(4)
    ]

    for i in range(STEP_X):
        x = base + i
        below = [tile_of(x * TILES + q) for q in range(TILES)]
        here = [tile_of((x + 1) * TILES + q) for q in range(TILES)]
        above = [tile_of((x + 2) * TILES + q) for q in range(TILES)]
        y_low, y_high = [
            pltpu.roll(faces[f], (TILE - BOX * i) % TILE, 1) if i else faces[f] for f in (0, 1)
        ]
        z_low, z_high = faces[2], faces[3]
        quarter = [pltpu.roll(t, BOX, 1) for t in here]
        reverse = [pltpu.roll(t, TILE - BOX, 1) for t in here]
        for q in range(TILES):
            p = here[q]
            before = quarter[q - 1] if q else pltpu.roll(y_low, 0, 1)
            y_behind = jnp.where(lanes < BOX, before, quarter[q])
            after = reverse[q + 1] if q + 1 < TILES else pltpu.roll(y_high, TILE - BOX, 1)
            y_ahead = jnp.where(lanes < TILE - BOX, reverse[q], after)
            z_behind = pltpu.roll(p, 1, 1)
            z_ahead = pltpu.roll(p, TILE - 1, 1)
            low = pltpu.roll(z_low, (TILE - TILES * i - q) % TILE, 1) if i + q else z_low
            high = pltpu.roll(z_high, (BOX - 1 - TILES * i - q) % TILE, 1)
            z_behind = jnp.where(lanes % BOX == 0, low, z_behind)
            z_ahead = jnp.where(lanes % BOX == BOX - 1, high, z_ahead)
            cut = slice(q * TILE, (q + 1) * TILE)
            around = ((below[q], above[q]), (y_behind, y_ahead), (z_behind, z_ahead))
            for c, (lower, upper) in enumerate(around):
                slope = 0.5 * (
                    apertures[i, 2 * c + 1, :, cut] * (upper - p)
                    + apertures[i, 2 * c, :, cut] * (p - lower)
                )
                out[c, :, i * INNER + q * TILE : i * INNER + (q + 1) * TILE] = updated[i, c, :, cut] - slope


def struct(*shape):
    return jax.ShapeDtypeStruct(shape, jnp.float32)


def volume_call(table, own, fraction, lanes_by):
    return pl.pallas_call(
        functools.partial(volume_kernel, lanes_by=lanes_by),
        in_specs=[SMEM_SPEC, SMEM_SPEC, ANY_SPEC],
        out_specs=HBM_SPEC,
        out_shape=struct(lanes_by, ROWS, TILE),
        scratch_shapes=[
            pltpu.VMEM((8, fetched_until(BOX)), jnp.int32),
            pltpu.VMEM((8 * PITCH, TILE), jnp.float32),
            pltpu.SemaphoreType.DMA((BOX // CHUNK,)),
            pltpu.SemaphoreType.DMA((BOX // CHUNK, lanes_by)),
        ],
        name="volume_rows",
    )(table, own, fraction)


def flux_call(send_slot, velocity, fraction):
    lanes_by = send_slot.shape[0]
    return pl.pallas_call(
        functools.partial(flux_kernel, lanes_by=lanes_by),
        in_specs=[SMEM_SPEC, VMEM_SPEC, VMEM_SPEC],
        out_specs=[VMEM_SPEC, VMEM_SPEC, HBM_SPEC],
        out_shape=[
            struct(PADDED, 8, WIDE),
            struct(PADDED, 3, 8, WIDE),
            struct(lanes_by, ROWS, TILE),
        ],
        scratch_shapes=[
            pltpu.VMEM((PADDED, 3, 8, WIDE), jnp.float32),
            pltpu.VMEM((8, WIDE), jnp.float32),
            pltpu.VMEM((4, 8, WIDE), jnp.float32),
            pltpu.VMEM((8 * PITCH, TILE), jnp.float32),
            pltpu.SemaphoreType.DMA((lanes_by,)),
        ],
        name="flux_rows",
    )(send_slot, velocity, fraction)


def update_call(masses, planes):
    return pl.pallas_call(
        update_kernel,
        grid=(BOX // STEP_X,),
        in_specs=[VMEM_SPEC, VMEM_SPEC],
        out_specs=[
            pl.BlockSpec((STEP_X, 3, 8, INNER), lambda i: (i, 0, 0, 0)),
            pl.BlockSpec((STEP_X, 6, 8, INNER), lambda i: (i, 0, 0, 0)),
        ],
        out_shape=[struct(BOX, 3, 8, INNER), struct(BOX, 6, 8, INNER)],
        name="updated",
    )(masses, planes)


def correct_call(slot_row, updated, apertures, returned):
    return pl.pallas_call(
        correct_kernel,
        grid=(BOX // STEP_X,),
        in_specs=[
            SMEM_SPEC,
            pl.BlockSpec((STEP_X, 3, 8, INNER), lambda i: (i, 0, 0, 0)),
            pl.BlockSpec((STEP_X, 6, 8, INNER), lambda i: (i, 0, 0, 0)),
            ANY_SPEC,
        ],
        out_specs=pl.BlockSpec((3, 8, STEP_X * INNER), lambda i: (0, 0, i)),
        out_shape=struct(3, 8, BOX * INNER),
        scratch_shapes=[
            pltpu.VMEM((8 * RETURN_ROWS, TILE), jnp.float32),
            pltpu.SemaphoreType.DMA((8,)),
        ],
        compiler_params=pltpu.CompilerParams(vmem_limit_bytes=14 << 20),
        name="corrected",
    )(
        slot_row,
        pltpu.with_memory_space_constraint(updated, pltpu.HBM),
        pltpu.with_memory_space_constraint(apertures, pltpu.HBM),
        returned,
    )


HALO = 5
SIDE = 8
EXT = BOX + 2 * HALO
ROWS_Y = BOX + 2 * SIDE
SLOT = 8
GROUP = TILE // SLOT
GROUPS = BOX // GROUP + 2


def loop(start, stop, body, unroll):
    def several(i, carry):
        for j in range(unroll):
            body(start + i * unroll + j)
        return carry

    lax.fori_loop(0, (stop - start) // unroll, several, 0)


STEP_BRICK = 8


def assemble_kernel(table, side, *refs, count):
    boxes = refs[:count]
    brick, first, last, strip = refs[count:]
    step = pl.program_id(0)
    steps = BOX // STEP_BRICK
    lanes = lane_index()
    lanes_brick = lax.broadcasted_iota(jnp.int32, (BOX, TILE), 1)
    source_lane = jnp.where(side[0] == 0, TILE - SLOT, 0)
    half = step % (GROUP // STEP_BRICK) * STEP_BRICK

    for x in range(STEP_BRICK):
        rows = [boxes[k][0, x * TILES : (x + 1) * TILES, :] for k in range(count)]
        for r in range(PER_TILE):
            value = None
            for k in reversed(range(count)):
                shift = (BOX * (k - r)) % TILE
                piece = pltpu.roll(rows[k], shift, 1) if shift else rows[k]
                value = piece if value is None else jnp.where(lanes < BOX * (k + 1), piece, value)
            brick[pl.ds(x * BOX + r, TILES, stride=PER_TILE), :] = value
    group = step // (GROUP // STEP_BRICK)
    value = jnp.zeros((BOX, TILE), jnp.float32)
    for x in range(STEP_BRICK):
        lane = (half + x) * SLOT
        plane = brick[x * BOX : (x + 1) * BOX, :]
        moved = pltpu.roll(plane, (lane - source_lane + TILE) % TILE, 1)
        value = jnp.where(lanes_brick // SLOT == half + x, moved, value)

    @pl.when(half == 0)
    def _():
        strip[group] = value

    @pl.when(half != 0)
    def _():
        strip[group] = jnp.where(lanes_brick // SLOT >= half, value, strip[group])

    @pl.when(step == 0)
    def _():
        first[...] = brick[0 : HALO * BOX, :]

    @pl.when(step == steps - 1)
    def _():
        last[...] = brick[(STEP_BRICK - HALO) * BOX : STEP_BRICK * BOX, :]


def solve_kernel(box_of_row, side, *refs, count, lanes_by):
    volume_in, source_in = refs[0:6], refs[6:12]
    pressure, rows = refs[12:14]
    scratch = refs[14:]
    (vol, ax, ay, azu, azl, diag, inv, res, sa, sb, total) = scratch[0:11]
    (hvol, hres, hsa, hsb, htotal, edge_a, edge_b, hcoef, turned, packed, sem) = scratch[11:]
    lane = lane_index()
    at_top = side[0] == 0
    edge_lane = jnp.where(at_top, TILE - 1, 0)
    slot_lane = jnp.where(at_top, 0, SLOT - 1)
    up_lane = jnp.where(at_top, TILE - 1, -1)
    low_lane = jnp.where(at_top, -1, 0)
    open_up = (lane % SLOT == SLOT - 1) & (low_lane == 0)
    open_low = (lane % SLOT == 0) & (up_lane >= 0)
    row_tiles = range(ROWS_Y // 8)

    def base(x):
        return pl.multiple_of(x * ROWS_Y, 8)

    def tile(ref, start, t, offset=0):
        return ref[pl.ds(start + 8 * t + offset, 8), :]

    def put(ref, start, t, value):
        ref[pl.ds(start + 8 * t, 8), :] = value

    def strip_base(g):
        return g * ROWS_Y + 8

    def fill(ext, strips, parts):
        brick, x_lo, x_hi, middle, y_lo, y_hi = parts
        own = HALO + 1 + BOX
        after = own + GROUPS - 2

        def rows_of(x, source):
            ext[pl.ds(base(x), SIDE), :] = y_lo[source]
            ext[pl.ds(base(x) + SIDE + BOX, SIDE), :] = y_hi[source]

        def body(i):
            ext[pl.ds(base(i + HALO) + SIDE, BOX), :] = brick[pl.ds(pl.multiple_of(i * BOX, 8), BOX), :]
            rows_of(i + HALO, i + HALO + 1)

        loop(0, BOX, body, 16)
        for i in range(HALO):
            for x, part, source in ((i, x_lo, i), (HALO + BOX + i, x_hi, after + i)):
                ext[x * ROWS_Y + SIDE : x * ROWS_Y + SIDE + BOX, :] = part[i * BOX : (i + 1) * BOX, :]
                rows_of(x, source)
        outer = slice(HALO * BOX, (HALO + 1) * BOX)
        pieces = [x_lo[outer, :]] + [middle[g] for g in range(GROUPS - 2)] + [x_hi[outer, :]]
        sources = [HALO] + [own + g for g in range(GROUPS - 2)] + [after + HALO]
        for g, (piece, source) in enumerate(zip(pieces, sources)):
            start = strip_base(g)
            strips[start : start + SIDE, :] = y_lo[source]
            strips[start + SIDE : start + SIDE + BOX, :] = piece
            strips[start + SIDE + BOX : start + ROWS_Y, :] = y_hi[source]

    fill(vol, hvol, volume_in)
    fill(res, hres, source_in)
    guard = jnp.zeros((8, TILE), jnp.float32)
    for ref in (hvol, hsa, hsb):
        ref[0:8, :] = guard
        ref[GROUPS * ROWS_Y + 8 : GROUPS * ROWS_Y + 16, :] = guard
    for ref in (edge_a, edge_b):
        ref[...] = jnp.zeros_like(ref)

    def place(x):
        group = (x + GROUP - HALO) // GROUP
        where = (x + GROUP - HALO) % GROUP * SLOT + slot_lane
        return pl.multiple_of(group * ROWS_Y + 8, 8), where

    def to_edge(edge, start, t, where, value):
        moved = pltpu.roll(value, (where - edge_lane + TILE) % TILE, 1)
        pltpu.store(edge.at[pl.ds(start + 8 * t, 8), :], moved, mask=lane == where)

    def z_sides(value, strips, start, t, where):
        outside = pltpu.roll(tile(strips, start, t), (edge_lane - where + TILE) % TILE, 1)
        up = jnp.where(lane == up_lane, outside, pltpu.roll(value, TILE - 1, 1))
        down = jnp.where(lane == low_lane, outside, pltpu.roll(value, 1, 1))
        return up, down

    def strip_sides(strips, edge, g, t):
        here = tile(strips, strip_base(g), t)
        following = tile(strips, strip_base(min(g + 1, GROUPS - 1)), t)
        previous = tile(strips, strip_base(max(g - 1, 0)), t)
        x_up = pltpu.roll(jnp.where(lane < SLOT, following, here), TILE - SLOT, 1)
        x_down = pltpu.roll(jnp.where(lane >= TILE - SLOT, previous, here), SLOT, 1)
        beyond = tile(edge, strip_base(g), t)
        z_up = jnp.where(open_up, beyond, pltpu.roll(here, TILE - 1, 1))
        z_down = jnp.where(open_low, beyond, pltpu.roll(here, 1, 1))
        y_up = tile(strips, strip_base(g), t, 1)
        y_down = tile(strips, strip_base(g), t, -1)
        return x_up, x_down, y_up, y_down, z_up, z_down

    def volume_edge(x):
        start, where = place(x)
        for t in row_tiles:
            to_edge(edge_a, start, t, where, tile(vol, base(x), t))

    loop(1, EXT - 1, volume_edge, 8)
    center = 0.5 * (UPPER_BOUND + LOWER_BOUND)
    halfwidth = 0.5 * (UPPER_BOUND - LOWER_BOUND)
    spread = center / halfwidth
    damping = 1.0 / spread
    for t in row_tiles:
        for ref in (sa, sb):
            put(ref, 0, t, guard)
            put(ref, (EXT - 1) * ROWS_Y, t, guard)
        put(ax, 0, t, jnp.minimum(tile(vol, 0, t), tile(vol, ROWS_Y, t)))
    put(ay, ROWS_Y - 8, 0, guard)

    def inverse_of(value):
        return jnp.where(value > 0.0, 1.0 / jnp.where(value > 0.0, value, 1.0), 0.0)

    closed_up = (lane == TILE - 1) & (lane != up_lane)
    closed_low = (lane == 0) & (lane != low_lane)

    def prepare(x):
        here = base(x)
        start, where = place(x)
        for t in row_tiles:
            v = tile(vol, here, t)
            upper = jnp.minimum(v, tile(vol, here + ROWS_Y, t))
            lower = jnp.minimum(v, tile(vol, here - ROWS_Y, t))
            z_up, z_down = z_sides(v, hvol, start, t, where)
            z_up = jnp.minimum(v, jnp.where(closed_up, 0.0, z_up))
            z_down = jnp.minimum(v, jnp.where(closed_low, 0.0, z_down))
            y_up = jnp.minimum(v, tile(vol, here, t, 1))
            y_down = jnp.minimum(v, tile(vol, here, t, -1))
            whole = SHIFT_WEIGHT * v + (upper + lower) + (y_up + y_down) + (z_up + z_down)
            scale = inverse_of(whole)
            for ref, value in ((ax, upper), (ay, y_up), (azu, z_up), (azl, z_down), (diag, whole), (inv, scale)):
                put(ref, here, t, value)
            search = (tile(res, here, t) * scale) * (1.0 / center)
            put(sa, here, t, search)
            put(total, here, t, search)
            to_edge(edge_b, start, t, where, search)

    loop(1, EXT - 1, prepare, 4)
    for g in range(GROUPS):
        for t in row_tiles:
            v = tile(hvol, strip_base(g), t)
            parts = [jnp.minimum(v, n) for n in strip_sides(hvol, edge_a, g, t)]
            whole = SHIFT_WEIGHT * v
            for value in parts:
                whole = whole + value
            scale = inverse_of(whole)
            for i, value in enumerate(parts + [whole, scale]):
                hcoef[i, g * ROWS_Y + 8 * t : g * ROWS_Y + 8 * t + 8, :] = value
            search = (tile(hres, strip_base(g), t) * scale) * (1.0 / center)
            put(hsa, strip_base(g), t, search)
            put(htotal, strip_base(g), t, search)

    now, then, hnow, hthen = sa, sb, hsa, hsb
    edge, edge_next = edge_b, edge_a
    for iteration in range(ITERS - 1):
        damping_next = 1.0 / (2.0 * spread - damping)
        keep = damping_next * damping
        push = 2.0 * damping_next / halfwidth
        damping = damping_next

        def iterate(x, now=now, then=then, hnow=hnow, edge_next=edge_next, keep=keep, push=push):
            here = base(x)
            start, where = place(x)
            for t in row_tiles:
                s = tile(now, here, t)
                z_up, z_down = z_sides(s, hnow, start, t, where)
                along_x = tile(ax, here, t) * tile(now, here + ROWS_Y, t)
                along_x = along_x + tile(ax, here - ROWS_Y, t) * tile(now, here - ROWS_Y, t)
                along_y = tile(ay, here, t) * tile(now, here, t, 1)
                along_y = along_y + tile(ay, here, t, -1) * tile(now, here, t, -1)
                along_z = tile(azu, here, t) * z_up + tile(azl, here, t) * z_down
                flow = along_x + along_y + along_z
                residual = tile(res, here, t) - (tile(diag, here, t) * s - flow)
                put(res, here, t, residual)
                search = keep * s + push * (residual * tile(inv, here, t))
                put(then, here, t, search)
                put(total, here, t, tile(total, here, t) + search)
                if edge_next is not None:
                    to_edge(edge_next, start, t, where, search)

        if iteration == ITERS - 2:
            iterate = functools.partial(iterate, edge_next=None)
        loop(1, EXT - 1, iterate, 4)
        for g in range(GROUPS):
            for t in row_tiles:
                rows_here = slice(g * ROWS_Y + 8 * t, g * ROWS_Y + 8 * t + 8)
                s = tile(hnow, strip_base(g), t)
                parts = [hcoef[i, rows_here, :] * v for i, v in enumerate(strip_sides(hnow, edge, g, t))]
                flow = (parts[0] + parts[1]) + (parts[2] + parts[3]) + (parts[4] + parts[5])
                residual = tile(hres, strip_base(g), t) - (hcoef[6, rows_here, :] * s - flow)
                put(hres, strip_base(g), t, residual)
                search = keep * s + push * (residual * hcoef[7, rows_here, :])
                put(hthen, strip_base(g), t, search)
                put(htotal, strip_base(g), t, tile(htotal, strip_base(g), t) + search)
        now, then, hnow, hthen = then, now, hthen, hnow
        edge, edge_next = edge_next, edge

    lanes = lane_index()

    def spread_boxes(pieces, row):
        for k in range(count):
            value = None
            for r in reversed(range(PER_TILE)):
                shift = (BOX * (r - k)) % TILE
                piece = pltpu.roll(pieces[r], shift, 1) if shift else pieces[r]
                value = piece if value is None else jnp.where(lanes < BOX * (r + 1), piece, value)
            packed[pl.ds(pl.multiple_of(k * RETURN_ROWS + row, 8), TILES), :] = value

    def core(i):
        start = (i + HALO - 1) * ROWS_Y + SIDE
        pieces = [total[pl.ds(start + r, TILES, stride=PER_TILE), :] for r in range(PER_TILE)]
        spread_boxes(pieces, i * TILES)

    loop(0, PADDED, core, 17)

    def output(i):
        pressure[i] = total[pl.ds(base(i + HALO) + SIDE, BOX), :]

    loop(0, BOX, output, 8)
    for f, y in enumerate((SIDE - 1, SIDE + BOX)):
        pieces = [
            total[pl.ds((HALO + r) * ROWS_Y + y, TILES, stride=PER_TILE * ROWS_Y), :]
            for r in range(PER_TILE)
        ]
        spread_boxes(pieces, PADDED * TILES + f * TILES)
    z_row = PADDED * TILES + 2 * TILES
    for k in (0, count - 1):
        packed[k * RETURN_ROWS + z_row : k * RETURN_ROWS + z_row + 2 * TILES, :] = jnp.zeros(
            (2 * TILES, TILE), jnp.float32
        )
    for block in range(TILES):
        for i in range(PER_TILE):
            for r in range(PER_TILE):
                start = (HALO + PER_TILE * block + i) * ROWS_Y + SIDE + r
                turned[BOX * r + TILES * i : BOX * r + TILES * (i + 1), :] = total[
                    pl.ds(start, TILES, stride=PER_TILE), :
                ]
        flat = turned[...].T
        for k in range(count):
            low = k * RETURN_ROWS + z_row + block
            if k:
                packed[low : low + 1, :] = flat[BOX * k - 1 : BOX * k, :]
            if k < count - 1:
                packed[low + TILES : low + TILES + 1, :] = flat[BOX * k + BOX : BOX * k + BOX + 1, :]
    half = GROUP // PER_TILE
    row4 = lax.broadcasted_iota(jnp.int32, (half, TILE), 1)
    box = jnp.where(at_top, count - 1, 0)
    target = box * RETURN_ROWS + z_row + jnp.where(at_top, TILES, 0)
    for g in range(1, GROUPS - 1):
        turned[...] = jnp.zeros_like(turned)
        for r in range(PER_TILE):
            turned[BOX * r : BOX * r + TILES, :] = htotal[
                pl.ds(strip_base(g) + SIDE + r, TILES, stride=PER_TILE), :
            ]
        turned[...] = turned[...].T
        value = None
        for i in range(PER_TILE):
            piece = turned[pl.ds(SLOT * i + slot_lane, half, stride=SLOT * PER_TILE), :]
            piece = pltpu.roll(piece, TILES * i, 1) if i else piece
            value = piece if value is None else jnp.where(row4 % BOX // TILES == i, piece, value)
        packed[pl.ds(target + (g - 1) * half, half), :] = value
    copies = [
        pltpu.make_async_copy(
            packed.at[pl.ds(pl.multiple_of(box_of_row[d] * RETURN_ROWS, 8), RETURN_ROWS)],
            rows.at[d],
            sem.at[d],
        )
        for d in range(lanes_by)
    ]
    for copy in copies:
        copy.start()
    for copy in copies:
        copy.wait()


def assemble_call(table, side, recv):
    count = table.shape[0]
    fixed = [
        (HALO * BOX, TILE),
        (HALO * BOX, TILE),
        (BOX // GROUP, BOX, TILE),
    ]

    def box_spec(k):
        return pl.BlockSpec((1, STEP_BRICK * TILES, TILE), lambda i, table, side: (table[k], i, 0))

    def fixed_spec(shape):
        return pl.BlockSpec(shape, lambda i, table, side: (0,) * len(shape))

    return pl.pallas_call(
        functools.partial(assemble_kernel, count=count),
        grid_spec=pltpu.PrefetchScalarGridSpec(
            num_scalar_prefetch=2,
            grid=(BOX // STEP_BRICK,),
            in_specs=[box_spec(k) for k in range(count)],
            out_specs=[pl.BlockSpec((STEP_BRICK * BOX, TILE), lambda i, table, side: (i, 0))]
            + [fixed_spec(shape) for shape in fixed],
        ),
        out_shape=[struct(BOX * BOX, TILE)] + [struct(*shape) for shape in fixed],
        compiler_params=pltpu.CompilerParams(vmem_limit_bytes=6 << 20),
        name="brick",
    )(table, side, *([recv] * count))


def halo(parts):
    brick, first, last, strip = parts
    nx, ny = lax.axis_size("bx"), lax.axis_size("by")
    nz = lax.axis_size("bz")
    middle = lax.ppermute(strip, "bz", [(i, nz - 1 - i) for i in range(nz)])
    up = [(i, i + 1) for i in range(nx - 1)]
    down = [(j, i) for i, j in up]
    x_lo = lax.ppermute(jnp.concatenate([last, middle[-1]], axis=0), "bx", up)
    x_hi = lax.ppermute(jnp.concatenate([first, middle[0]], axis=0), "bx", down)
    cubes = [v.reshape(-1, BOX, TILE) for v in (x_lo, brick, middle, x_hi)]

    def edge(start):
        return jnp.concatenate([v[:, start : start + SIDE] for v in cubes], axis=0)

    y_up = [(i, i + 1) for i in range(ny - 1)]
    y_lo = lax.ppermute(edge(BOX - SIDE), "by", y_up)
    y_hi = lax.ppermute(edge(0), "by", [(j, i) for i, j in y_up])
    return brick, x_lo, x_hi, middle, y_lo, y_hi


def solve_call(box_of_row, side, count, volume, source):
    lanes_by = box_of_row.shape[0]
    wide = pltpu.VMEM((EXT * ROWS_Y, TILE), jnp.float32)
    narrow = pltpu.VMEM((GROUPS * ROWS_Y + 16, TILE), jnp.float32)
    return pl.pallas_call(
        functools.partial(solve_kernel, count=count, lanes_by=lanes_by),
        in_specs=[SMEM_SPEC, SMEM_SPEC] + [VMEM_SPEC] * 12,
        out_specs=[VMEM_SPEC, HBM_SPEC],
        out_shape=[struct(BOX, BOX, count * BOX), struct(lanes_by, RETURN_ROWS, TILE)],
        scratch_shapes=[wide] * 11
        + [narrow] * 7
        + [
            pltpu.VMEM((8, GROUPS * ROWS_Y, TILE), jnp.float32),
            pltpu.VMEM((TILE, TILE), jnp.float32),
            pltpu.VMEM((count * RETURN_ROWS, TILE), jnp.float32),
            pltpu.SemaphoreType.DMA((lanes_by,)),
        ],
        compiler_params=pltpu.CompilerParams(vmem_limit_bytes=26 << 20),
        name="solve",
    )(box_of_row, side, *volume, *source)


def routing(placement, capacity):
    lanes = lax.axis_size("by")
    own_index = lax.axis_index("by")
    table = placement[0, :, 0, :]
    per_brick = table.shape[1]
    entries = lanes * per_brick
    owners = table.reshape(entries)
    onehot = (owners[:, None] == jnp.arange(lanes, dtype=jnp.int32)[None, :]).astype(jnp.int32)
    ranks = jnp.sum((jnp.cumsum(onehot, axis=0) - onehot) * onehot, axis=1)
    matches = (table == own_index).astype(jnp.int32)
    send_slot = jnp.sum(matches * ranks.reshape(lanes, per_brick), axis=1)
    slot_match = (
        (owners == own_index)[:, None]
        & (ranks[:, None] == jnp.arange(capacity, dtype=jnp.int32)[None, :])
    ).astype(jnp.int32)
    row_value = jnp.arange(entries, dtype=jnp.int32) // per_brick
    slot_row = jnp.sum(slot_match * row_value[:, None], axis=0)
    brick_table = lax.dynamic_index_in_dim(table, own_index, 0, keepdims=False)
    all_rows = jnp.arange(lanes, dtype=jnp.int32)
    box_of_row = jnp.sum(
        (brick_table[None, :] == all_rows[:, None]).astype(jnp.int32)
        * jnp.arange(per_brick, dtype=jnp.int32)[None, :],
        axis=1,
    )
    return send_slot, slot_row, brick_table, box_of_row


def exchange(rows):
    return lax.all_to_all(rows, "by", split_axis=0, concat_axis=0, tiled=True)


def local(velocity, fraction, placement):
    send_slot, slot_row, brick_table, box_of_row = routing(placement, velocity.shape[0])
    own = lax.axis_index("by").reshape(1)
    table = placement.reshape(-1)
    volume_rows = volume_call(table, own, fraction, send_slot.shape[0])
    volume_recv = exchange(volume_rows)
    planes, masses, source_rows = flux_call(send_slot, jnp.swapaxes(velocity, 0, 1), fraction)
    source_recv = exchange(source_rows)
    updated, apertures = update_call(masses, planes)
    side = lax.axis_index("bz").reshape(1)
    volume = halo(assemble_call(brick_table, side, volume_recv))
    source_recv, volume = lax.optimization_barrier((source_recv, volume))
    source = halo(assemble_call(brick_table, side, source_recv))
    pressure, rows = solve_call(box_of_row, side, placement.shape[3], volume, source)
    returned = exchange(rows)
    corrected = correct_call(slot_row, updated, apertures, returned)
    return (jnp.swapaxes(corrected, 0, 1), pressure)


def solution(mesh):
    in_specs = (
        P(("bx", "by", "bz"), None, None),
        P(("bx", "by", "bz"), None),
        P("bx", None, "bz", None),
    )
    out_specs = (P(("bx", "by", "bz"), None, None), P("bx", "by", "bz"))
    return jax.shard_map(local, mesh=mesh, in_specs=in_specs, out_specs=out_specs, check_vma=False)
```

```python
import functools

import jax
import jax.numpy as jnp
from jax import lax
from jax.experimental import pallas as pl
from jax.experimental.pallas import tpu as pltpu
from jax.sharding import PartitionSpec as P

BOX = 32
ITERS = 4
PADDED = BOX + 2
PLANE = PADDED * PADDED
TILE = 128
WIDE = 10 * TILE
INNER = BOX * BOX
TILES = INNER // TILE
PER_TILE = TILE // BOX
ROWS = BOX * TILES
PITCH = ROWS + 8
RETURN_ROWS = PADDED * TILES + 4 * TILES
STEP_DT = 0.25
SHIFT_WEIGHT = 0.5
LOWER_BOUND = 0.5 / 6.5
UPPER_BOUND = 2.0

VMEM_SPEC = pl.BlockSpec(memory_space=pltpu.VMEM)
SMEM_SPEC = pl.BlockSpec(memory_space=pltpu.SMEM)
ANY_SPEC = pl.BlockSpec(memory_space=pl.ANY)
HBM_SPEC = pl.BlockSpec(memory_space=pltpu.HBM)


def lane_index():
    return lax.broadcasted_iota(jnp.int32, (8, TILE), 1)


def inside_plane():
    flat = lax.broadcasted_iota(jnp.int32, (8, WIDE), 1)
    row = flat // PADDED
    col = flat % PADDED
    return (row >= 1) & (row <= BOX) & (col >= 1) & (col <= BOX)


def ahead(values, offset):
    return pltpu.roll(values, WIDE - offset, 1)


def behind(values, offset):
    return pltpu.roll(values, offset, 1)


def compact(values, offset, lanes):
    tiles = [values[:, t * TILE : (t + 1) * TILE] for t in range(WIDE // TILE)]
    out = []
    for q in range(TILES):
        pieces = []
        for r in range(PER_TILE):
            start = (q * PER_TILE + r + 1) * PADDED + 1 + offset
            index, lane = divmod(start, TILE)
            shift = (BOX * r - lane) % TILE
            piece = pltpu.roll(tiles[index], shift, 1) if shift else tiles[index]
            if lane + BOX > TILE:
                rest = pltpu.roll(tiles[index + 1], shift, 1) if shift else tiles[index + 1]
                piece = jnp.where(lanes < BOX * r + TILE - lane, piece, rest)
            pieces.append(piece)
        value = pieces[-1]
        for r in reversed(range(PER_TILE - 1)):
            value = jnp.where(lanes < BOX * (r + 1), pieces[r], value)
        out.append(value)
    return out


def aligned_plane(load, x, lanes):
    start = x * (PLANE // TILE) + (x * (PLANE % TILE)) // TILE
    amount = (x * (PLANE % TILE)) % TILE
    block = load(pl.multiple_of(start * TILE, TILE))
    tiles = [
        pltpu.roll(block[:, t * TILE : (t + 1) * TILE], TILE - amount, 1)
        for t in range(WIDE // TILE)
    ]
    keep = lanes < TILE - amount
    return [
        jnp.where(keep, tiles[t], tiles[t + 1]) if t + 1 < len(tiles) else tiles[t]
        for t in range(len(tiles))
    ]


def store_plane(ref, index, tiles):
    for t, tile in enumerate(tiles):
        ref[index + (slice(None), slice(t * TILE, (t + 1) * TILE))] = tile


def last_plane(ref_tail, out_ref, index):
    tail = ref_tail
    start = (PADDED - 1) * PLANE
    first = start // TILE * TILE
    span = PADDED * PLANE - first
    tail_block = jnp.concatenate([tail, jnp.zeros((8, WIDE - span), jnp.float32)], axis=1)
    out_ref[index] = pltpu.roll(tail_block, WIDE - (start - first), 1)


def put_rows(ref, x, tiles):
    for q, tile in enumerate(tiles):
        ref[pl.ds(x * TILES + q, 8, stride=PITCH), :] = tile


def send_rows(slots, rows_ref, out_ref, sem, count):
    copies = [
        pltpu.make_async_copy(
            rows_ref.at[pl.ds(pl.multiple_of(slots[d] * PITCH, 8), ROWS)],
            out_ref.at[d],
            sem.at[d],
        )
        for d in range(count)
    ]
    for copy in copies:
        copy.start()
    for copy in copies:
        copy.wait()


def own_slots(table, own, lanes_by):
    per_brick = table.shape[0] // lanes_by
    count = jnp.int32(0)
    slots = []
    for d in range(lanes_by):
        slot = jnp.int32(0)
        for k in range(per_brick):
            hit = jnp.where(table[d * per_brick + k] == own[0], 1, 0)
            slot = slot + hit * count
            count = count + hit
        slots.append(slot)
    return slots


CHUNK = 8


def fetched_until(x):
    return x * PLANE // TILE * TILE + WIDE


def volume_kernel(table, own, fraction, rows, cells, packed, sem_in, sem, *, lanes_by):
    lanes = lane_index()
    fetches = []
    begin = 0
    for chunk in range(BOX // CHUNK):
        end = fetched_until((chunk + 1) * CHUNK)
        fetches.append(
            pltpu.make_async_copy(
                fraction.at[:, pl.ds(begin, end - begin)],
                cells.at[:, pl.ds(begin, end - begin)],
                sem_in.at[chunk],
            )
        )
        begin = end
    for fetch in fetches:
        fetch.start()
    slots = own_slots(table, own, lanes_by)

    def send(chunk):
        span = CHUNK * TILES
        copies = [
            pltpu.make_async_copy(
                packed.at[pl.ds(pl.multiple_of(slots[d] * PITCH + chunk * span, 8), span)],
                rows.at[d, pl.ds(chunk * span, span)],
                sem.at[chunk, d],
            )
            for d in range(lanes_by)
        ]
        for copy in copies:
            copy.start()
        return copies

    def body(x, carry):
        tiles = aligned_plane(
            lambda s: cells[:, pl.ds(s, WIDE)].astype(jnp.float32) * (1.0 / 256.0), x, lanes
        )
        put_rows(packed, x - 1, compact(jnp.concatenate(tiles, axis=1), 0, lanes))
        return carry

    copies = []
    for chunk in range(BOX // CHUNK):
        fetches[chunk].wait()
        loop(chunk * CHUNK + 1, (chunk + 1) * CHUNK + 1, lambda x: body(x, 0), 4)
        copies += send(chunk)
    for copy in copies:
        copy.wait()


def flux_kernel(slots, velocity, fraction, planes, masses, rows, field, tail, carry_ref, packed, sem, *, lanes_by):
    lanes = lane_index()
    inside = inside_plane()

    def align(x):
        tiles = aligned_plane(
            lambda s: fraction[:, pl.ds(s, WIDE)].astype(jnp.float32) * (1.0 / 256.0), x, lanes
        )
        store_plane(planes, (x,), tiles)
        for c in range(3):
            store_plane(field, (x, c), aligned_plane(lambda s: velocity[c, :, pl.ds(s, WIDE)], x, lanes))

    def align_body(x, carry):
        align(x)
        return carry

    loop(0, PADDED - 1, align, 3)
    start = (PADDED - 1) * PLANE
    first = start // TILE * TILE
    span = PADDED * PLANE - first
    tail[...] = jnp.zeros_like(tail)
    tail[:, 0:span] = fraction[:, first : PADDED * PLANE].astype(jnp.float32) * (1.0 / 256.0)
    planes[PADDED - 1] = ahead(tail[...], start - first)
    for c in range(3):
        tail[:, 0:span] = velocity[c, :, first : PADDED * PLANE]
        field[PADDED - 1, c] = ahead(tail[...], start - first)

    def face(volume, volume_ahead, here, there, heading):
        speed = 0.5 * (here[heading] + there[heading])
        flow = jnp.minimum(volume, volume_ahead) * speed
        upwind = speed > 0.0
        return [flow * jnp.where(upwind, here[c], there[c]) for c in range(3)] + [flow]

    def x_face(x):
        return face(
            planes[x], planes[x + 1], [field[x, c] for c in range(3)], [field[x + 1, c] for c in range(3)], 0
        )

    for c, value in enumerate(x_face(0)):
        carry_ref[c] = value
    for c in range(3):
        masses[0, c] = jnp.zeros((8, WIDE), jnp.float32)
        masses[PADDED - 1, c] = jnp.zeros((8, WIDE), jnp.float32)

    def step(x, carry):
        volume = planes[x]
        here = [field[x, c] for c in range(3)]
        upper = x_face(x)
        total = [upper[c] - carry_ref[c] for c in range(4)]
        for c in range(4):
            carry_ref[c] = upper[c]
        for heading, offset in ((1, PADDED), (2, 1)):
            faces = face(volume, ahead(volume, offset), here, [ahead(v, offset) for v in here], heading)
            total = [total[c] + faces[c] - behind(faces[c], offset) for c in range(4)]
        for c in range(3):
            masses[x, c] = jnp.where(inside, volume * here[c] - STEP_DT * total[c], 0.0)
        put_rows(packed, x - 1, compact(-total[3], 0, lanes))
        return carry

    lax.fori_loop(1, PADDED - 1, step, 0)
    send_rows(slots, packed, rows, sem, lanes_by)


def update_kernel(masses, planes, updated, apertures):
    lanes = lane_index()
    inside = inside_plane()

    def put(ref, index, tiles):
        for q, tile in enumerate(tiles):
            ref[index + (slice(None), slice(q * TILE, (q + 1) * TILE))] = tile

    def neighbours(here, below, above):
        total = here + below + above
        for offset in (PADDED, 1):
            total = total + ahead(here, offset) + behind(here, offset)
        return total

    def step(i, carry):
        x = pl.program_id(0) * STEP_X + i + 1
        volume = planes[x]
        weight = jnp.where(inside, volume, 0.0)
        below = jnp.where(inside & (x > 1), planes[x - 1], 0.0)
        above = jnp.where(inside & (x < BOX), planes[x + 1], 0.0)
        weights = neighbours(weight, below, above)
        inverse = 1.0 / jnp.where(weights > 0.0, weights, 1.0)
        cut = volume < 1.0
        for c in range(3):
            here = masses[x, c]
            spread = neighbours(here, masses[x - 1, c], masses[x + 1, c]) * inverse
            put(updated, (i, c), compact(jnp.where(cut, spread, here), 0, lanes))
        put(apertures, (i, 0), compact(jnp.minimum(volume, planes[x - 1]), 0, lanes))
        put(apertures, (i, 1), compact(jnp.minimum(volume, planes[x + 1]), 0, lanes))
        for axis, offset in ((1, PADDED), (2, 1)):
            aperture = jnp.minimum(volume, ahead(volume, offset))
            put(apertures, (i, 2 * axis), compact(aperture, -offset, lanes))
            put(apertures, (i, 2 * axis + 1), compact(aperture, 0, lanes))
        return carry

    loop(0, STEP_X, lambda i: step(i, 0), 4)


STEP_X = 4


def correct_kernel(rows, updated, apertures, returned, out, boxes, sem):
    step = pl.program_id(0)
    lanes = lane_index()

    @pl.when(step == 0)
    def _():
        copies = [
            pltpu.make_async_copy(
                returned.at[rows[s]], boxes.at[pl.ds(s * RETURN_ROWS, RETURN_ROWS)], sem.at[s]
            )
            for s in range(8)
        ]
        for copy in copies:
            copy.start()
        for copy in copies:
            copy.wait()

    def tile_of(row):
        return boxes[pl.ds(row, 8, stride=RETURN_ROWS), :]

    base = step * STEP_X
    faces = [
        tile_of(PADDED * TILES + f * TILES + step) for f in range(4)
    ]

    for i in range(STEP_X):
        x = base + i
        below = [tile_of(x * TILES + q) for q in range(TILES)]
        here = [tile_of((x + 1) * TILES + q) for q in range(TILES)]
        above = [tile_of((x + 2) * TILES + q) for q in range(TILES)]
        y_low, y_high = [
            pltpu.roll(faces[f], (TILE - BOX * i) % TILE, 1) if i else faces[f] for f in (0, 1)
        ]
        z_low, z_high = faces[2], faces[3]
        quarter = [pltpu.roll(t, BOX, 1) for t in here]
        reverse = [pltpu.roll(t, TILE - BOX, 1) for t in here]
        for q in range(TILES):
            p = here[q]
            before = quarter[q - 1] if q else pltpu.roll(y_low, 0, 1)
            y_behind = jnp.where(lanes < BOX, before, quarter[q])
            after = reverse[q + 1] if q + 1 < TILES else pltpu.roll(y_high, TILE - BOX, 1)
            y_ahead = jnp.where(lanes < TILE - BOX, reverse[q], after)
            z_behind = pltpu.roll(p, 1, 1)
            z_ahead = pltpu.roll(p, TILE - 1, 1)
            low = pltpu.roll(z_low, (TILE - TILES * i - q) % TILE, 1) if i + q else z_low
            high = pltpu.roll(z_high, (BOX - 1 - TILES * i - q) % TILE, 1)
            z_behind = jnp.where(lanes % BOX == 0, low, z_behind)
            z_ahead = jnp.where(lanes % BOX == BOX - 1, high, z_ahead)
            cut = slice(q * TILE, (q + 1) * TILE)
            around = ((below[q], above[q]), (y_behind, y_ahead), (z_behind, z_ahead))
            for c, (lower, upper) in enumerate(around):
                slope = 0.5 * (
                    apertures[i, 2 * c + 1, :, cut] * (upper - p)
                    + apertures[i, 2 * c, :, cut] * (p - lower)
                )
                out[c, :, i * INNER + q * TILE : i * INNER + (q + 1) * TILE] = updated[i, c, :, cut] - slope


def struct(*shape):
    return jax.ShapeDtypeStruct(shape, jnp.float32)


def volume_call(table, own, fraction, lanes_by):
    return pl.pallas_call(
        functools.partial(volume_kernel, lanes_by=lanes_by),
        in_specs=[SMEM_SPEC, SMEM_SPEC, ANY_SPEC],
        out_specs=HBM_SPEC,
        out_shape=struct(lanes_by, ROWS, TILE),
        scratch_shapes=[
            pltpu.VMEM((8, fetched_until(BOX)), jnp.int32),
            pltpu.VMEM((8 * PITCH, TILE), jnp.float32),
            pltpu.SemaphoreType.DMA((BOX // CHUNK,)),
            pltpu.SemaphoreType.DMA((BOX // CHUNK, lanes_by)),
        ],
        name="volume_rows",
    )(table, own, fraction)


def flux_call(send_slot, velocity, fraction):
    lanes_by = send_slot.shape[0]
    return pl.pallas_call(
        functools.partial(flux_kernel, lanes_by=lanes_by),
        in_specs=[SMEM_SPEC, VMEM_SPEC, VMEM_SPEC],
        out_specs=[VMEM_SPEC, VMEM_SPEC, HBM_SPEC],
        out_shape=[
            struct(PADDED, 8, WIDE),
            struct(PADDED, 3, 8, WIDE),
            struct(lanes_by, ROWS, TILE),
        ],
        scratch_shapes=[
            pltpu.VMEM((PADDED, 3, 8, WIDE), jnp.float32),
            pltpu.VMEM((8, WIDE), jnp.float32),
            pltpu.VMEM((4, 8, WIDE), jnp.float32),
            pltpu.VMEM((8 * PITCH, TILE), jnp.float32),
            pltpu.SemaphoreType.DMA((lanes_by,)),
        ],
        name="flux_rows",
    )(send_slot, velocity, fraction)


def update_call(masses, planes):
    return pl.pallas_call(
        update_kernel,
        grid=(BOX // STEP_X,),
        in_specs=[VMEM_SPEC, VMEM_SPEC],
        out_specs=[
            pl.BlockSpec((STEP_X, 3, 8, INNER), lambda i: (i, 0, 0, 0)),
            pl.BlockSpec((STEP_X, 6, 8, INNER), lambda i: (i, 0, 0, 0)),
        ],
        out_shape=[struct(BOX, 3, 8, INNER), struct(BOX, 6, 8, INNER)],
        name="updated",
    )(masses, planes)


def correct_call(slot_row, updated, apertures, returned):
    return pl.pallas_call(
        correct_kernel,
        grid=(BOX // STEP_X,),
        in_specs=[
            SMEM_SPEC,
            pl.BlockSpec((STEP_X, 3, 8, INNER), lambda i: (i, 0, 0, 0)),
            pl.BlockSpec((STEP_X, 6, 8, INNER), lambda i: (i, 0, 0, 0)),
            ANY_SPEC,
        ],
        out_specs=pl.BlockSpec((3, 8, STEP_X * INNER), lambda i: (0, 0, i)),
        out_shape=struct(3, 8, BOX * INNER),
        scratch_shapes=[
            pltpu.VMEM((8 * RETURN_ROWS, TILE), jnp.float32),
            pltpu.SemaphoreType.DMA((8,)),
        ],
        compiler_params=pltpu.CompilerParams(vmem_limit_bytes=14 << 20),
        name="corrected",
    )(
        slot_row,
        pltpu.with_memory_space_constraint(updated, pltpu.HBM),
        pltpu.with_memory_space_constraint(apertures, pltpu.HBM),
        returned,
    )


HALO = 5
SIDE = 8
EXT = BOX + 2 * HALO
ROWS_Y = BOX + 2 * SIDE
SLOT = 8
GROUP = TILE // SLOT
GROUPS = BOX // GROUP + 2


def loop(start, stop, body, unroll):
    def several(i, carry):
        for j in range(unroll):
            body(start + i * unroll + j)
        return carry

    lax.fori_loop(0, (stop - start) // unroll, several, 0)


STEP_BRICK = 8


def assemble_kernel(table, side, *refs, count):
    boxes = refs[:count]
    brick, first, last, strip = refs[count:]
    step = pl.program_id(0)
    steps = BOX // STEP_BRICK
    lanes = lane_index()
    lanes_brick = lax.broadcasted_iota(jnp.int32, (BOX, TILE), 1)
    source_lane = jnp.where(side[0] == 0, TILE - SLOT, 0)
    half = step % (GROUP // STEP_BRICK) * STEP_BRICK

    for x in range(STEP_BRICK):
        rows = [boxes[k][0, x * TILES : (x + 1) * TILES, :] for k in range(count)]
        for r in range(PER_TILE):
            value = None
            for k in reversed(range(count)):
                shift = (BOX * (k - r)) % TILE
                piece = pltpu.roll(rows[k], shift, 1) if shift else rows[k]
                value = piece if value is None else jnp.where(lanes < BOX * (k + 1), piece, value)
            brick[pl.ds(x * BOX + r, TILES, stride=PER_TILE), :] = value
    group = step // (GROUP // STEP_BRICK)
    value = jnp.zeros((BOX, TILE), jnp.float32)
    for x in range(STEP_BRICK):
        lane = (half + x) * SLOT
        plane = brick[x * BOX : (x + 1) * BOX, :]
        moved = pltpu.roll(plane, (lane - source_lane + TILE) % TILE, 1)
        value = jnp.where(lanes_brick // SLOT == half + x, moved, value)

    @pl.when(half == 0)
    def _():
        strip[group] = value

    @pl.when(half != 0)
    def _():
        strip[group] = jnp.where(lanes_brick // SLOT >= half, value, strip[group])

    @pl.when(step == 0)
    def _():
        first[...] = brick[0 : HALO * BOX, :]

    @pl.when(step == steps - 1)
    def _():
        last[...] = brick[(STEP_BRICK - HALO) * BOX : STEP_BRICK * BOX, :]


def solve_kernel(box_of_row, side, *refs, count, lanes_by):
    volume_in, source_in = refs[0:6], refs[6:12]
    pressure, rows = refs[12:14]
    scratch = refs[14:]
    (vol, ax, ay, azu, azl, diag, inv, res, sa, sb, total) = scratch[0:11]
    (hvol, hres, hsa, hsb, htotal, edge_a, edge_b, hcoef, turned, packed, sem) = scratch[11:]
    lane = lane_index()
    at_top = side[0] == 0
    edge_lane = jnp.where(at_top, TILE - 1, 0)
    slot_lane = jnp.where(at_top, 0, SLOT - 1)
    up_lane = jnp.where(at_top, TILE - 1, -1)
    low_lane = jnp.where(at_top, -1, 0)
    open_up = (lane % SLOT == SLOT - 1) & (low_lane == 0)
    open_low = (lane % SLOT == 0) & (up_lane >= 0)
    row_tiles = range(ROWS_Y // 8)

    def base(x):
        return pl.multiple_of(x * ROWS_Y, 8)

    def tile(ref, start, t, offset=0):
        return ref[pl.ds(start + 8 * t + offset, 8), :]

    def put(ref, start, t, value):
        ref[pl.ds(start + 8 * t, 8), :] = value

    def strip_base(g):
        return g * ROWS_Y + 8

    def fill(ext, strips, parts, depth):
        brick, x_lo, x_hi, middle, y_lo, y_hi = parts
        own = HALO + 1 + BOX
        after = own + GROUPS - 2

        def rows_of(x, source):
            ext[pl.ds(base(x), SIDE), :] = low_rows(source)
            ext[pl.ds(base(x) + SIDE + BOX, SIDE), :] = high_rows(source)

        rest = jnp.zeros((SIDE - depth, TILE), jnp.float32) if depth < SIDE else None

        def low_rows(source):
            return y_lo[source] if rest is None else jnp.concatenate([rest, y_lo[source]], axis=0)

        def high_rows(source):
            return y_hi[source] if rest is None else jnp.concatenate([y_hi[source], rest], axis=0)

        def body(i):
            ext[pl.ds(base(i + HALO) + SIDE, BOX), :] = brick[pl.ds(pl.multiple_of(i * BOX, 8), BOX), :]
            rows_of(i + HALO, i + HALO + 1)

        loop(0, BOX, body, 16)
        for i in range(HALO):
            for x, part, source in ((i, x_lo, i), (HALO + BOX + i, x_hi, after + i)):
                ext[x * ROWS_Y + SIDE : x * ROWS_Y + SIDE + BOX, :] = part[i * BOX : (i + 1) * BOX, :]
                rows_of(x, source)
        outer = slice(HALO * BOX, (HALO + 1) * BOX)
        pieces = [x_lo[outer, :]] + [middle[g] for g in range(GROUPS - 2)] + [x_hi[outer, :]]
        sources = [HALO] + [own + g for g in range(GROUPS - 2)] + [after + HALO]
        for g, (piece, source) in enumerate(zip(pieces, sources)):
            start = strip_base(g)
            strips[start : start + SIDE, :] = low_rows(source)
            strips[start + SIDE : start + SIDE + BOX, :] = piece
            strips[start + SIDE + BOX : start + ROWS_Y, :] = high_rows(source)

    fill(vol, hvol, volume_in, SIDE)
    fill(res, hres, source_in, ITERS)
    guard = jnp.zeros((8, TILE), jnp.float32)
    for ref in (hvol, hsa, hsb):
        ref[0:8, :] = guard
        ref[GROUPS * ROWS_Y + 8 : GROUPS * ROWS_Y + 16, :] = guard
    for ref in (edge_a, edge_b):
        ref[...] = jnp.zeros_like(ref)

    def place(x):
        group = (x + GROUP - HALO) // GROUP
        where = (x + GROUP - HALO) % GROUP * SLOT + slot_lane
        return pl.multiple_of(group * ROWS_Y + 8, 8), where

    def to_edge(edge, start, t, where, value):
        moved = pltpu.roll(value, (where - edge_lane + TILE) % TILE, 1)
        pltpu.store(edge.at[pl.ds(start + 8 * t, 8), :], moved, mask=lane == where)

    def z_sides(value, strips, start, t, where):
        outside = pltpu.roll(tile(strips, start, t), (edge_lane - where + TILE) % TILE, 1)
        up = jnp.where(lane == up_lane, outside, pltpu.roll(value, TILE - 1, 1))
        down = jnp.where(lane == low_lane, outside, pltpu.roll(value, 1, 1))
        return up, down

    def strip_sides(strips, edge, g, t):
        here = tile(strips, strip_base(g), t)
        following = tile(strips, strip_base(min(g + 1, GROUPS - 1)), t)
        previous = tile(strips, strip_base(max(g - 1, 0)), t)
        x_up = pltpu.roll(jnp.where(lane < SLOT, following, here), TILE - SLOT, 1)
        x_down = pltpu.roll(jnp.where(lane >= TILE - SLOT, previous, here), SLOT, 1)
        beyond = tile(edge, strip_base(g), t)
        z_up = jnp.where(open_up, beyond, pltpu.roll(here, TILE - 1, 1))
        z_down = jnp.where(open_low, beyond, pltpu.roll(here, 1, 1))
        y_up = tile(strips, strip_base(g), t, 1)
        y_down = tile(strips, strip_base(g), t, -1)
        return x_up, x_down, y_up, y_down, z_up, z_down

    def volume_edge(x):
        start, where = place(x)
        for t in row_tiles:
            to_edge(edge_a, start, t, where, tile(vol, base(x), t))

    loop(1, EXT - 1, volume_edge, 8)
    center = 0.5 * (UPPER_BOUND + LOWER_BOUND)
    halfwidth = 0.5 * (UPPER_BOUND - LOWER_BOUND)
    spread = center / halfwidth
    damping = 1.0 / spread
    for t in row_tiles:
        for ref in (sa, sb):
            put(ref, 0, t, guard)
            put(ref, (EXT - 1) * ROWS_Y, t, guard)
        put(ax, 0, t, jnp.minimum(tile(vol, 0, t), tile(vol, ROWS_Y, t)))
    put(ay, ROWS_Y - 8, 0, guard)

    def inverse_of(value):
        return jnp.where(value > 0.0, 1.0 / jnp.where(value > 0.0, value, 1.0), 0.0)

    closed_up = (lane == TILE - 1) & (lane != up_lane)
    closed_low = (lane == 0) & (lane != low_lane)

    def prepare(x):
        here = base(x)
        start, where = place(x)
        for t in row_tiles:
            v = tile(vol, here, t)
            upper = jnp.minimum(v, tile(vol, here + ROWS_Y, t))
            lower = jnp.minimum(v, tile(vol, here - ROWS_Y, t))
            z_up, z_down = z_sides(v, hvol, start, t, where)
            z_up = jnp.minimum(v, jnp.where(closed_up, 0.0, z_up))
            z_down = jnp.minimum(v, jnp.where(closed_low, 0.0, z_down))
            y_up = jnp.minimum(v, tile(vol, here, t, 1))
            y_down = jnp.minimum(v, tile(vol, here, t, -1))
            whole = SHIFT_WEIGHT * v + (upper + lower) + (y_up + y_down) + (z_up + z_down)
            scale = inverse_of(whole)
            for ref, value in ((ax, upper), (ay, y_up), (azu, z_up), (azl, z_down), (diag, whole), (inv, scale)):
                put(ref, here, t, value)
            search = (tile(res, here, t) * scale) * (1.0 / center)
            put(sa, here, t, search)
            put(total, here, t, search)
            to_edge(edge_b, start, t, where, search)

    loop(1, EXT - 1, prepare, 4)
    for g in range(GROUPS):
        for t in row_tiles:
            v = tile(hvol, strip_base(g), t)
            parts = [jnp.minimum(v, n) for n in strip_sides(hvol, edge_a, g, t)]
            whole = SHIFT_WEIGHT * v
            for value in parts:
                whole = whole + value
            scale = inverse_of(whole)
            for i, value in enumerate(parts + [whole, scale]):
                hcoef[i, g * ROWS_Y + 8 * t : g * ROWS_Y + 8 * t + 8, :] = value
            search = (tile(hres, strip_base(g), t) * scale) * (1.0 / center)
            put(hsa, strip_base(g), t, search)
            put(htotal, strip_base(g), t, search)

    now, then, hnow, hthen = sa, sb, hsa, hsb
    edge, edge_next = edge_b, edge_a
    for iteration in range(ITERS - 1):
        damping_next = 1.0 / (2.0 * spread - damping)
        keep = damping_next * damping
        push = 2.0 * damping_next / halfwidth
        damping = damping_next

        def iterate(x, now=now, then=then, hnow=hnow, edge_next=edge_next, keep=keep, push=push):
            here = base(x)
            start, where = place(x)
            for t in row_tiles:
                s = tile(now, here, t)
                z_up, z_down = z_sides(s, hnow, start, t, where)
                along_x = tile(ax, here, t) * tile(now, here + ROWS_Y, t)
                along_x = along_x + tile(ax, here - ROWS_Y, t) * tile(now, here - ROWS_Y, t)
                along_y = tile(ay, here, t) * tile(now, here, t, 1)
                along_y = along_y + tile(ay, here, t, -1) * tile(now, here, t, -1)
                along_z = tile(azu, here, t) * z_up + tile(azl, here, t) * z_down
                flow = along_x + along_y + along_z
                residual = tile(res, here, t) - (tile(diag, here, t) * s - flow)
                put(res, here, t, residual)
                search = keep * s + push * (residual * tile(inv, here, t))
                put(then, here, t, search)
                put(total, here, t, tile(total, here, t) + search)
                if edge_next is not None:
                    to_edge(edge_next, start, t, where, search)

        if iteration == ITERS - 2:
            iterate = functools.partial(iterate, edge_next=None)
        loop(1, EXT - 1, iterate, 4)
        for g in range(GROUPS):
            for t in row_tiles:
                rows_here = slice(g * ROWS_Y + 8 * t, g * ROWS_Y + 8 * t + 8)
                s = tile(hnow, strip_base(g), t)
                parts = [hcoef[i, rows_here, :] * v for i, v in enumerate(strip_sides(hnow, edge, g, t))]
                flow = (parts[0] + parts[1]) + (parts[2] + parts[3]) + (parts[4] + parts[5])
                residual = tile(hres, strip_base(g), t) - (hcoef[6, rows_here, :] * s - flow)
                put(hres, strip_base(g), t, residual)
                search = keep * s + push * (residual * hcoef[7, rows_here, :])
                put(hthen, strip_base(g), t, search)
                put(htotal, strip_base(g), t, tile(htotal, strip_base(g), t) + search)
        now, then, hnow, hthen = then, now, hthen, hnow
        edge, edge_next = edge_next, edge

    lanes = lane_index()

    def spread_boxes(pieces, row):
        for k in range(count):
            value = None
            for r in reversed(range(PER_TILE)):
                shift = (BOX * (r - k)) % TILE
                piece = pltpu.roll(pieces[r], shift, 1) if shift else pieces[r]
                value = piece if value is None else jnp.where(lanes < BOX * (r + 1), piece, value)
            packed[pl.ds(pl.multiple_of(k * RETURN_ROWS + row, 8), TILES), :] = value

    def core(i):
        start = (i + HALO - 1) * ROWS_Y + SIDE
        pieces = [total[pl.ds(start + r, TILES, stride=PER_TILE), :] for r in range(PER_TILE)]
        spread_boxes(pieces, i * TILES)

    loop(0, PADDED, core, 17)

    def output(i):
        pressure[i] = total[pl.ds(base(i + HALO) + SIDE, BOX), :]

    loop(0, BOX, output, 8)
    for f, y in enumerate((SIDE - 1, SIDE + BOX)):
        pieces = [
            total[pl.ds((HALO + r) * ROWS_Y + y, TILES, stride=PER_TILE * ROWS_Y), :]
            for r in range(PER_TILE)
        ]
        spread_boxes(pieces, PADDED * TILES + f * TILES)
    z_row = PADDED * TILES + 2 * TILES
    for k in (0, count - 1):
        packed[k * RETURN_ROWS + z_row : k * RETURN_ROWS + z_row + 2 * TILES, :] = jnp.zeros(
            (2 * TILES, TILE), jnp.float32
        )
    for block in range(TILES):
        for i in range(PER_TILE):
            for r in range(PER_TILE):
                start = (HALO + PER_TILE * block + i) * ROWS_Y + SIDE + r
                turned[BOX * r + TILES * i : BOX * r + TILES * (i + 1), :] = total[
                    pl.ds(start, TILES, stride=PER_TILE), :
                ]
        flat = turned[...].T
        for k in range(count):
            low = k * RETURN_ROWS + z_row + block
            if k:
                packed[low : low + 1, :] = flat[BOX * k - 1 : BOX * k, :]
            if k < count - 1:
                packed[low + TILES : low + TILES + 1, :] = flat[BOX * k + BOX : BOX * k + BOX + 1, :]
    half = GROUP // PER_TILE
    row4 = lax.broadcasted_iota(jnp.int32, (half, TILE), 1)
    box = jnp.where(at_top, count - 1, 0)
    target = box * RETURN_ROWS + z_row + jnp.where(at_top, TILES, 0)
    for g in range(1, GROUPS - 1):
        turned[...] = jnp.zeros_like(turned)
        for r in range(PER_TILE):
            turned[BOX * r : BOX * r + TILES, :] = htotal[
                pl.ds(strip_base(g) + SIDE + r, TILES, stride=PER_TILE), :
            ]
        turned[...] = turned[...].T
        value = None
        for i in range(PER_TILE):
            piece = turned[pl.ds(SLOT * i + slot_lane, half, stride=SLOT * PER_TILE), :]
            piece = pltpu.roll(piece, TILES * i, 1) if i else piece
            value = piece if value is None else jnp.where(row4 % BOX // TILES == i, piece, value)
        packed[pl.ds(target + (g - 1) * half, half), :] = value
    copies = [
        pltpu.make_async_copy(
            packed.at[pl.ds(pl.multiple_of(box_of_row[d] * RETURN_ROWS, 8), RETURN_ROWS)],
            rows.at[d],
            sem.at[d],
        )
        for d in range(lanes_by)
    ]
    for copy in copies:
        copy.start()
    for copy in copies:
        copy.wait()


def assemble_call(table, side, recv):
    count = table.shape[0]
    fixed = [
        (HALO * BOX, TILE),
        (HALO * BOX, TILE),
        (BOX // GROUP, BOX, TILE),
    ]

    def box_spec(k):
        return pl.BlockSpec((1, STEP_BRICK * TILES, TILE), lambda i, table, side: (table[k], i, 0))

    def fixed_spec(shape):
        return pl.BlockSpec(shape, lambda i, table, side: (0,) * len(shape))

    return pl.pallas_call(
        functools.partial(assemble_kernel, count=count),
        grid_spec=pltpu.PrefetchScalarGridSpec(
            num_scalar_prefetch=2,
            grid=(BOX // STEP_BRICK,),
            in_specs=[box_spec(k) for k in range(count)],
            out_specs=[pl.BlockSpec((STEP_BRICK * BOX, TILE), lambda i, table, side: (i, 0))]
            + [fixed_spec(shape) for shape in fixed],
        ),
        out_shape=[struct(BOX * BOX, TILE)] + [struct(*shape) for shape in fixed],
        compiler_params=pltpu.CompilerParams(vmem_limit_bytes=6 << 20),
        name="brick",
    )(table, side, *([recv] * count))


def halo(parts, depth):
    brick, first, last, strip = parts
    nx, ny = lax.axis_size("bx"), lax.axis_size("by")
    nz = lax.axis_size("bz")
    middle = lax.ppermute(strip, "bz", [(i, nz - 1 - i) for i in range(nz)])
    up = [(i, i + 1) for i in range(nx - 1)]
    down = [(j, i) for i, j in up]
    x_lo = lax.ppermute(jnp.concatenate([last, middle[-1]], axis=0), "bx", up)
    x_hi = lax.ppermute(jnp.concatenate([first, middle[0]], axis=0), "bx", down)
    cubes = [v.reshape(-1, BOX, TILE) for v in (x_lo, brick, middle, x_hi)]

    def edge(start):
        return jnp.concatenate([v[:, start : start + depth] for v in cubes], axis=0)

    y_up = [(i, i + 1) for i in range(ny - 1)]
    y_lo = lax.ppermute(edge(BOX - depth), "by", y_up)
    y_hi = lax.ppermute(edge(0), "by", [(j, i) for i, j in y_up])
    return brick, x_lo, x_hi, middle, y_lo, y_hi


def solve_call(box_of_row, side, count, volume, source):
    lanes_by = box_of_row.shape[0]
    wide = pltpu.VMEM((EXT * ROWS_Y, TILE), jnp.float32)
    narrow = pltpu.VMEM((GROUPS * ROWS_Y + 16, TILE), jnp.float32)
    return pl.pallas_call(
        functools.partial(solve_kernel, count=count, lanes_by=lanes_by),
        in_specs=[SMEM_SPEC, SMEM_SPEC] + [VMEM_SPEC] * 12,
        out_specs=[VMEM_SPEC, HBM_SPEC],
        out_shape=[struct(BOX, BOX, count * BOX), struct(lanes_by, RETURN_ROWS, TILE)],
        scratch_shapes=[wide] * 11
        + [narrow] * 7
        + [
            pltpu.VMEM((8, GROUPS * ROWS_Y, TILE), jnp.float32),
            pltpu.VMEM((TILE, TILE), jnp.float32),
            pltpu.VMEM((count * RETURN_ROWS, TILE), jnp.float32),
            pltpu.SemaphoreType.DMA((lanes_by,)),
        ],
        compiler_params=pltpu.CompilerParams(vmem_limit_bytes=26 << 20),
        name="solve",
    )(box_of_row, side, *volume, *source)


def routing(placement, capacity):
    lanes = lax.axis_size("by")
    own_index = lax.axis_index("by")
    table = placement[0, :, 0, :]
    per_brick = table.shape[1]
    entries = lanes * per_brick
    owners = table.reshape(entries)
    onehot = (owners[:, None] == jnp.arange(lanes, dtype=jnp.int32)[None, :]).astype(jnp.int32)
    ranks = jnp.sum((jnp.cumsum(onehot, axis=0) - onehot) * onehot, axis=1)
    matches = (table == own_index).astype(jnp.int32)
    send_slot = jnp.sum(matches * ranks.reshape(lanes, per_brick), axis=1)
    slot_match = (
        (owners == own_index)[:, None]
        & (ranks[:, None] == jnp.arange(capacity, dtype=jnp.int32)[None, :])
    ).astype(jnp.int32)
    row_value = jnp.arange(entries, dtype=jnp.int32) // per_brick
    slot_row = jnp.sum(slot_match * row_value[:, None], axis=0)
    brick_table = lax.dynamic_index_in_dim(table, own_index, 0, keepdims=False)
    all_rows = jnp.arange(lanes, dtype=jnp.int32)
    box_of_row = jnp.sum(
        (brick_table[None, :] == all_rows[:, None]).astype(jnp.int32)
        * jnp.arange(per_brick, dtype=jnp.int32)[None, :],
        axis=1,
    )
    return send_slot, slot_row, brick_table, box_of_row


def exchange(rows):
    return lax.all_to_all(rows, "by", split_axis=0, concat_axis=0, tiled=True)


def local(velocity, fraction, placement):
    send_slot, slot_row, brick_table, box_of_row = routing(placement, velocity.shape[0])
    own = lax.axis_index("by").reshape(1)
    table = placement.reshape(-1)
    volume_rows = volume_call(table, own, fraction, send_slot.shape[0])
    volume_recv = exchange(volume_rows)
    planes, masses, source_rows = flux_call(send_slot, jnp.swapaxes(velocity, 0, 1), fraction)
    source_recv = exchange(source_rows)
    updated, apertures = update_call(masses, planes)
    side = lax.axis_index("bz").reshape(1)
    volume = halo(assemble_call(brick_table, side, volume_recv), SIDE)
    source_recv, volume = lax.optimization_barrier((source_recv, volume))
    source = halo(assemble_call(brick_table, side, source_recv), ITERS)
    pressure, rows = solve_call(box_of_row, side, placement.shape[3], volume, source)
    returned = exchange(rows)
    corrected = correct_call(slot_row, updated, apertures, returned)
    return (jnp.swapaxes(corrected, 0, 1), pressure)


def solution(mesh):
    in_specs = (
        P(("bx", "by", "bz"), None, None),
        P(("bx", "by", "bz"), None),
        P("bx", None, "bz", None),
    )
    out_specs = (P(("bx", "by", "bz"), None, None), P("bx", "by", "bz"))
    return jax.shard_map(local, mesh=mesh, in_specs=in_specs, out_specs=out_specs, check_vma=False)
```

```python
import functools

import jax
import jax.numpy as jnp
from jax import lax
from jax.experimental import pallas as pl
from jax.experimental.pallas import tpu as pltpu
from jax.sharding import PartitionSpec as P

BOX = 32
ITERS = 4
PADDED = BOX + 2
PLANE = PADDED * PADDED
TILE = 128
WIDE = 10 * TILE
INNER = BOX * BOX
TILES = INNER // TILE
PER_TILE = TILE // BOX
ROWS = BOX * TILES
PITCH = ROWS + 8
RETURN_ROWS = PADDED * TILES + 4 * TILES
STEP_DT = 0.25
SHIFT_WEIGHT = 0.5
LOWER_BOUND = 0.5 / 6.5
UPPER_BOUND = 2.0

VMEM_SPEC = pl.BlockSpec(memory_space=pltpu.VMEM)
SMEM_SPEC = pl.BlockSpec(memory_space=pltpu.SMEM)
ANY_SPEC = pl.BlockSpec(memory_space=pl.ANY)
HBM_SPEC = pl.BlockSpec(memory_space=pltpu.HBM)


def lane_index():
    return lax.broadcasted_iota(jnp.int32, (8, TILE), 1)


def inside_plane():
    flat = lax.broadcasted_iota(jnp.int32, (8, WIDE), 1)
    row = flat // PADDED
    col = flat % PADDED
    return (row >= 1) & (row <= BOX) & (col >= 1) & (col <= BOX)


def ahead(values, offset):
    return pltpu.roll(values, WIDE - offset, 1)


def behind(values, offset):
    return pltpu.roll(values, offset, 1)


def compact(values, offset, lanes):
    tiles = [values[:, t * TILE : (t + 1) * TILE] for t in range(WIDE // TILE)]
    out = []
    for q in range(TILES):
        pieces = []
        for r in range(PER_TILE):
            start = (q * PER_TILE + r + 1) * PADDED + 1 + offset
            index, lane = divmod(start, TILE)
            shift = (BOX * r - lane) % TILE
            piece = pltpu.roll(tiles[index], shift, 1) if shift else tiles[index]
            if lane + BOX > TILE:
                rest = pltpu.roll(tiles[index + 1], shift, 1) if shift else tiles[index + 1]
                piece = jnp.where(lanes < BOX * r + TILE - lane, piece, rest)
            pieces.append(piece)
        value = pieces[-1]
        for r in reversed(range(PER_TILE - 1)):
            value = jnp.where(lanes < BOX * (r + 1), pieces[r], value)
        out.append(value)
    return out


def aligned_plane(load, x, lanes):
    start = x * (PLANE // TILE) + (x * (PLANE % TILE)) // TILE
    amount = (x * (PLANE % TILE)) % TILE
    block = load(pl.multiple_of(start * TILE, TILE))
    tiles = [
        pltpu.roll(block[:, t * TILE : (t + 1) * TILE], TILE - amount, 1)
        for t in range(WIDE // TILE)
    ]
    keep = lanes < TILE - amount
    return [
        jnp.where(keep, tiles[t], tiles[t + 1]) if t + 1 < len(tiles) else tiles[t]
        for t in range(len(tiles))
    ]


def store_plane(ref, index, tiles):
    for t, tile in enumerate(tiles):
        ref[index + (slice(None), slice(t * TILE, (t + 1) * TILE))] = tile


def last_plane(ref_tail, out_ref, index):
    tail = ref_tail
    start = (PADDED - 1) * PLANE
    first = start // TILE * TILE
    span = PADDED * PLANE - first
    tail_block = jnp.concatenate([tail, jnp.zeros((8, WIDE - span), jnp.float32)], axis=1)
    out_ref[index] = pltpu.roll(tail_block, WIDE - (start - first), 1)


def put_rows(ref, x, tiles):
    for q, tile in enumerate(tiles):
        ref[pl.ds(x * TILES + q, 8, stride=PITCH), :] = tile


def send_rows(slots, rows_ref, out_ref, sem, count):
    copies = [
        pltpu.make_async_copy(
            rows_ref.at[pl.ds(pl.multiple_of(slots[d] * PITCH, 8), ROWS)],
            out_ref.at[d],
            sem.at[d],
        )
        for d in range(count)
    ]
    for copy in copies:
        copy.start()
    for copy in copies:
        copy.wait()


def own_slots(table, own, lanes_by):
    per_brick = table.shape[0] // lanes_by
    count = jnp.int32(0)
    slots = []
    for d in range(lanes_by):
        slot = jnp.int32(0)
        for k in range(per_brick):
            hit = jnp.where(table[d * per_brick + k] == own[0], 1, 0)
            slot = slot + hit * count
            count = count + hit
        slots.append(slot)
    return slots


CHUNK = 8


def fetched_until(x):
    return x * PLANE // TILE * TILE + WIDE


def volume_kernel(table, own, fraction, rows, cells, packed, sem_in, sem, *, lanes_by):
    lanes = lane_index()
    fetches = []
    begin = 0
    for chunk in range(BOX // CHUNK):
        end = fetched_until((chunk + 1) * CHUNK)
        fetches.append(
            pltpu.make_async_copy(
                fraction.at[:, pl.ds(begin, end - begin)],
                cells.at[:, pl.ds(begin, end - begin)],
                sem_in.at[chunk],
            )
        )
        begin = end
    for fetch in fetches:
        fetch.start()
    slots = own_slots(table, own, lanes_by)

    def send(chunk):
        span = CHUNK * TILES
        copies = [
            pltpu.make_async_copy(
                packed.at[pl.ds(pl.multiple_of(slots[d] * PITCH + chunk * span, 8), span)],
                rows.at[d, pl.ds(chunk * span, span)],
                sem.at[chunk, d],
            )
            for d in range(lanes_by)
        ]
        for copy in copies:
            copy.start()
        return copies

    def body(x, carry):
        tiles = aligned_plane(
            lambda s: cells[:, pl.ds(s, WIDE)].astype(jnp.float32) * (1.0 / 256.0), x, lanes
        )
        put_rows(packed, x - 1, compact(jnp.concatenate(tiles, axis=1), 0, lanes))
        return carry

    copies = []
    for chunk in range(BOX // CHUNK):
        fetches[chunk].wait()
        loop(chunk * CHUNK + 1, (chunk + 1) * CHUNK + 1, lambda x: body(x, 0), 4)
        copies += send(chunk)
    for copy in copies:
        copy.wait()


def flux_kernel(slots, velocity, fraction, planes, masses, rows, field, tail, carry_ref, packed, sem, *, lanes_by):
    lanes = lane_index()
    inside = inside_plane()

    def align(x):
        tiles = aligned_plane(
            lambda s: fraction[:, pl.ds(s, WIDE)].astype(jnp.float32) * (1.0 / 256.0), x, lanes
        )
        store_plane(planes, (x,), tiles)
        for c in range(3):
            store_plane(field, (x, c), aligned_plane(lambda s: velocity[c, :, pl.ds(s, WIDE)], x, lanes))

    def align_body(x, carry):
        align(x)
        return carry

    loop(0, PADDED - 1, align, 3)
    start = (PADDED - 1) * PLANE
    first = start // TILE * TILE
    span = PADDED * PLANE - first
    tail[...] = jnp.zeros_like(tail)
    tail[:, 0:span] = fraction[:, first : PADDED * PLANE].astype(jnp.float32) * (1.0 / 256.0)
    planes[PADDED - 1] = ahead(tail[...], start - first)
    for c in range(3):
        tail[:, 0:span] = velocity[c, :, first : PADDED * PLANE]
        field[PADDED - 1, c] = ahead(tail[...], start - first)

    def face(volume, volume_ahead, here, there, heading):
        speed = 0.5 * (here[heading] + there[heading])
        flow = jnp.minimum(volume, volume_ahead) * speed
        upwind = speed > 0.0
        return [flow * jnp.where(upwind, here[c], there[c]) for c in range(3)] + [flow]

    def x_face(x):
        return face(
            planes[x], planes[x + 1], [field[x, c] for c in range(3)], [field[x + 1, c] for c in range(3)], 0
        )

    for c, value in enumerate(x_face(0)):
        carry_ref[c] = value
    for c in range(3):
        masses[0, c] = jnp.zeros((8, WIDE), jnp.float32)
        masses[PADDED - 1, c] = jnp.zeros((8, WIDE), jnp.float32)

    def step(x, carry):
        volume = planes[x]
        here = [field[x, c] for c in range(3)]
        upper = x_face(x)
        total = [upper[c] - carry_ref[c] for c in range(4)]
        for c in range(4):
            carry_ref[c] = upper[c]
        for heading, offset in ((1, PADDED), (2, 1)):
            faces = face(volume, ahead(volume, offset), here, [ahead(v, offset) for v in here], heading)
            total = [total[c] + faces[c] - behind(faces[c], offset) for c in range(4)]
        for c in range(3):
            masses[x, c] = jnp.where(inside, volume * here[c] - STEP_DT * total[c], 0.0)
        put_rows(packed, x - 1, compact(-total[3], 0, lanes))
        return carry

    lax.fori_loop(1, PADDED - 1, step, 0)
    send_rows(slots, packed, rows, sem, lanes_by)


def update_kernel(masses, planes, updated, apertures):
    lanes = lane_index()
    inside = inside_plane()

    def put(ref, index, tiles):
        for q, tile in enumerate(tiles):
            ref[index + (slice(None), slice(q * TILE, (q + 1) * TILE))] = tile

    def neighbours(here, below, above):
        total = here + below + above
        for offset in (PADDED, 1):
            total = total + ahead(here, offset) + behind(here, offset)
        return total

    def step(i, lower):
        x = pl.program_id(0) * STEP_X + i + 1
        volume = planes[x]
        weight = jnp.where(inside, volume, 0.0)
        below = jnp.where(inside & (x > 1), planes[x - 1], 0.0)
        above = jnp.where(inside & (x < BOX), planes[x + 1], 0.0)
        weights = neighbours(weight, below, above)
        inverse = 1.0 / jnp.where(weights > 0.0, weights, 1.0)
        cut = volume < 1.0
        for c in range(3):
            here = masses[x, c]
            spread = neighbours(here, masses[x - 1, c], masses[x + 1, c]) * inverse
            put(updated, (i, c), compact(jnp.where(cut, spread, here), 0, lanes))
        if lower is None:
            lower = compact(jnp.minimum(volume, planes[x - 1]), 0, lanes)
        upper = compact(jnp.minimum(volume, planes[x + 1]), 0, lanes)
        put(apertures, (i, 0), lower)
        put(apertures, (i, 1), upper)
        for axis, offset in ((1, PADDED), (2, 1)):
            aperture = jnp.minimum(volume, ahead(volume, offset))
            put(apertures, (i, 2 * axis), compact(aperture, -offset, lanes))
            put(apertures, (i, 2 * axis + 1), compact(aperture, 0, lanes))
        return upper

    lower = None
    for i in range(STEP_X):
        lower = step(i, lower)


STEP_X = 4


def correct_kernel(rows, updated, apertures, returned, out, boxes, sem):
    step = pl.program_id(0)
    lanes = lane_index()

    @pl.when(step == 0)
    def _():
        copies = [
            pltpu.make_async_copy(
                returned.at[rows[s]], boxes.at[pl.ds(s * RETURN_ROWS, RETURN_ROWS)], sem.at[s]
            )
            for s in range(8)
        ]
        for copy in copies:
            copy.start()
        for copy in copies:
            copy.wait()

    def tile_of(row):
        return boxes[pl.ds(row, 8, stride=RETURN_ROWS), :]

    base = step * STEP_X
    faces = [
        tile_of(PADDED * TILES + f * TILES + step) for f in range(4)
    ]

    for i in range(STEP_X):
        x = base + i
        below = [tile_of(x * TILES + q) for q in range(TILES)]
        here = [tile_of((x + 1) * TILES + q) for q in range(TILES)]
        above = [tile_of((x + 2) * TILES + q) for q in range(TILES)]
        y_low, y_high = [
            pltpu.roll(faces[f], (TILE - BOX * i) % TILE, 1) if i else faces[f] for f in (0, 1)
        ]
        z_low, z_high = faces[2], faces[3]
        quarter = [pltpu.roll(t, BOX, 1) for t in here]
        reverse = [pltpu.roll(t, TILE - BOX, 1) for t in here]
        for q in range(TILES):
            p = here[q]
            before = quarter[q - 1] if q else pltpu.roll(y_low, 0, 1)
            y_behind = jnp.where(lanes < BOX, before, quarter[q])
            after = reverse[q + 1] if q + 1 < TILES else pltpu.roll(y_high, TILE - BOX, 1)
            y_ahead = jnp.where(lanes < TILE - BOX, reverse[q], after)
            z_behind = pltpu.roll(p, 1, 1)
            z_ahead = pltpu.roll(p, TILE - 1, 1)
            low = pltpu.roll(z_low, (TILE - TILES * i - q) % TILE, 1) if i + q else z_low
            high = pltpu.roll(z_high, (BOX - 1 - TILES * i - q) % TILE, 1)
            z_behind = jnp.where(lanes % BOX == 0, low, z_behind)
            z_ahead = jnp.where(lanes % BOX == BOX - 1, high, z_ahead)
            cut = slice(q * TILE, (q + 1) * TILE)
            around = ((below[q], above[q]), (y_behind, y_ahead), (z_behind, z_ahead))
            for c, (lower, upper) in enumerate(around):
                slope = 0.5 * (
                    apertures[i, 2 * c + 1, :, cut] * (upper - p)
                    + apertures[i, 2 * c, :, cut] * (p - lower)
                )
                out[c, :, i * INNER + q * TILE : i * INNER + (q + 1) * TILE] = updated[i, c, :, cut] - slope


def struct(*shape):
    return jax.ShapeDtypeStruct(shape, jnp.float32)


def volume_call(table, own, fraction, lanes_by):
    return pl.pallas_call(
        functools.partial(volume_kernel, lanes_by=lanes_by),
        in_specs=[SMEM_SPEC, SMEM_SPEC, ANY_SPEC],
        out_specs=HBM_SPEC,
        out_shape=struct(lanes_by, ROWS, TILE),
        scratch_shapes=[
            pltpu.VMEM((8, fetched_until(BOX)), jnp.int32),
            pltpu.VMEM((8 * PITCH, TILE), jnp.float32),
            pltpu.SemaphoreType.DMA((BOX // CHUNK,)),
            pltpu.SemaphoreType.DMA((BOX // CHUNK, lanes_by)),
        ],
        name="volume_rows",
    )(table, own, fraction)


def flux_call(send_slot, velocity, fraction):
    lanes_by = send_slot.shape[0]
    return pl.pallas_call(
        functools.partial(flux_kernel, lanes_by=lanes_by),
        in_specs=[SMEM_SPEC, VMEM_SPEC, VMEM_SPEC],
        out_specs=[VMEM_SPEC, VMEM_SPEC, HBM_SPEC],
        out_shape=[
            struct(PADDED, 8, WIDE),
            struct(PADDED, 3, 8, WIDE),
            struct(lanes_by, ROWS, TILE),
        ],
        scratch_shapes=[
            pltpu.VMEM((PADDED, 3, 8, WIDE), jnp.float32),
            pltpu.VMEM((8, WIDE), jnp.float32),
            pltpu.VMEM((4, 8, WIDE), jnp.float32),
            pltpu.VMEM((8 * PITCH, TILE), jnp.float32),
            pltpu.SemaphoreType.DMA((lanes_by,)),
        ],
        name="flux_rows",
    )(send_slot, velocity, fraction)


def update_call(masses, planes):
    return pl.pallas_call(
        update_kernel,
        grid=(BOX // STEP_X,),
        in_specs=[VMEM_SPEC, VMEM_SPEC],
        out_specs=[
            pl.BlockSpec((STEP_X, 3, 8, INNER), lambda i: (i, 0, 0, 0)),
            pl.BlockSpec((STEP_X, 6, 8, INNER), lambda i: (i, 0, 0, 0)),
        ],
        out_shape=[struct(BOX, 3, 8, INNER), struct(BOX, 6, 8, INNER)],
        name="updated",
    )(masses, planes)


def correct_call(slot_row, updated, apertures, returned):
    return pl.pallas_call(
        correct_kernel,
        grid=(BOX // STEP_X,),
        in_specs=[
            SMEM_SPEC,
            pl.BlockSpec((STEP_X, 3, 8, INNER), lambda i: (i, 0, 0, 0)),
            pl.BlockSpec((STEP_X, 6, 8, INNER), lambda i: (i, 0, 0, 0)),
            ANY_SPEC,
        ],
        out_specs=pl.BlockSpec((3, 8, STEP_X * INNER), lambda i: (0, 0, i)),
        out_shape=struct(3, 8, BOX * INNER),
        scratch_shapes=[
            pltpu.VMEM((8 * RETURN_ROWS, TILE), jnp.float32),
            pltpu.SemaphoreType.DMA((8,)),
        ],
        compiler_params=pltpu.CompilerParams(vmem_limit_bytes=14 << 20),
        name="corrected",
    )(
        slot_row,
        pltpu.with_memory_space_constraint(updated, pltpu.HBM),
        pltpu.with_memory_space_constraint(apertures, pltpu.HBM),
        returned,
    )


HALO = 5
SIDE = 8
EXT = BOX + 2 * HALO
ROWS_Y = BOX + 2 * SIDE
SLOT = 8
GROUP = TILE // SLOT
GROUPS = BOX // GROUP + 2


def loop(start, stop, body, unroll):
    def several(i, carry):
        for j in range(unroll):
            body(start + i * unroll + j)
        return carry

    lax.fori_loop(0, (stop - start) // unroll, several, 0)


STEP_BRICK = 8


def assemble_kernel(table, side, *refs, count):
    boxes = refs[:count]
    brick, first, last, strip = refs[count:]
    step = pl.program_id(0)
    steps = BOX // STEP_BRICK
    lanes = lane_index()
    lanes_brick = lax.broadcasted_iota(jnp.int32, (BOX, TILE), 1)
    source_lane = jnp.where(side[0] == 0, TILE - SLOT, 0)
    half = step % (GROUP // STEP_BRICK) * STEP_BRICK

    for x in range(STEP_BRICK):
        rows = [boxes[k][0, x * TILES : (x + 1) * TILES, :] for k in range(count)]
        for r in range(PER_TILE):
            value = None
            for k in reversed(range(count)):
                shift = (BOX * (k - r)) % TILE
                piece = pltpu.roll(rows[k], shift, 1) if shift else rows[k]
                value = piece if value is None else jnp.where(lanes < BOX * (k + 1), piece, value)
            brick[pl.ds(x * BOX + r, TILES, stride=PER_TILE), :] = value
    group = step // (GROUP // STEP_BRICK)
    value = jnp.zeros((BOX, TILE), jnp.float32)
    for x in range(STEP_BRICK):
        lane = (half + x) * SLOT
        plane = brick[x * BOX : (x + 1) * BOX, :]
        moved = pltpu.roll(plane, (lane - source_lane + TILE) % TILE, 1)
        value = jnp.where(lanes_brick // SLOT == half + x, moved, value)

    @pl.when(half == 0)
    def _():
        strip[group] = value

    @pl.when(half != 0)
    def _():
        strip[group] = jnp.where(lanes_brick // SLOT >= half, value, strip[group])

    @pl.when(step == 0)
    def _():
        first[...] = brick[0 : HALO * BOX, :]

    @pl.when(step == steps - 1)
    def _():
        last[...] = brick[(STEP_BRICK - HALO) * BOX : STEP_BRICK * BOX, :]


def solve_kernel(box_of_row, side, *refs, count, lanes_by):
    volume_in, source_in = refs[0:6], refs[6:12]
    pressure, rows = refs[12:14]
    scratch = refs[14:]
    (vol, ax, ay, azu, azl, diag, inv, res, sa, sb, total) = scratch[0:11]
    (hvol, hres, hsa, hsb, htotal, edge_a, edge_b, hcoef, turned, packed, sem) = scratch[11:]
    lane = lane_index()
    at_top = side[0] == 0
    edge_lane = jnp.where(at_top, TILE - 1, 0)
    slot_lane = jnp.where(at_top, 0, SLOT - 1)
    up_lane = jnp.where(at_top, TILE - 1, -1)
    low_lane = jnp.where(at_top, -1, 0)
    open_up = (lane % SLOT == SLOT - 1) & (low_lane == 0)
    open_low = (lane % SLOT == 0) & (up_lane >= 0)
    row_tiles = range(ROWS_Y // 8)

    def base(x):
        return pl.multiple_of(x * ROWS_Y, 8)

    def tile(ref, start, t, offset=0):
        return ref[pl.ds(start + 8 * t + offset, 8), :]

    def put(ref, start, t, value):
        ref[pl.ds(start + 8 * t, 8), :] = value

    def strip_base(g):
        return g * ROWS_Y + 8

    def fill(ext, strips, parts, depth):
        brick, x_lo, x_hi, middle, y_lo, y_hi = parts
        own = HALO + 1 + BOX
        after = own + GROUPS - 2

        def rows_of(x, source):
            ext[pl.ds(base(x), SIDE), :] = low_rows(source)
            ext[pl.ds(base(x) + SIDE + BOX, SIDE), :] = high_rows(source)

        rest = jnp.zeros((SIDE - depth, TILE), jnp.float32) if depth < SIDE else None

        def low_rows(source):
            return y_lo[source] if rest is None else jnp.concatenate([rest, y_lo[source]], axis=0)

        def high_rows(source):
            return y_hi[source] if rest is None else jnp.concatenate([y_hi[source], rest], axis=0)

        def body(i):
            ext[pl.ds(base(i + HALO) + SIDE, BOX), :] = brick[pl.ds(pl.multiple_of(i * BOX, 8), BOX), :]
            rows_of(i + HALO, i + HALO + 1)

        loop(0, BOX, body, 16)
        for i in range(HALO):
            for x, part, source in ((i, x_lo, i), (HALO + BOX + i, x_hi, after + i)):
                ext[x * ROWS_Y + SIDE : x * ROWS_Y + SIDE + BOX, :] = part[i * BOX : (i + 1) * BOX, :]
                rows_of(x, source)
        outer = slice(HALO * BOX, (HALO + 1) * BOX)
        pieces = [x_lo[outer, :]] + [middle[g] for g in range(GROUPS - 2)] + [x_hi[outer, :]]
        sources = [HALO] + [own + g for g in range(GROUPS - 2)] + [after + HALO]
        for g, (piece, source) in enumerate(zip(pieces, sources)):
            start = strip_base(g)
            strips[start : start + SIDE, :] = low_rows(source)
            strips[start + SIDE : start + SIDE + BOX, :] = piece
            strips[start + SIDE + BOX : start + ROWS_Y, :] = high_rows(source)

    fill(vol, hvol, volume_in, SIDE)
    fill(res, hres, source_in, ITERS)
    guard = jnp.zeros((8, TILE), jnp.float32)
    for ref in (hvol, hsa, hsb):
        ref[0:8, :] = guard
        ref[GROUPS * ROWS_Y + 8 : GROUPS * ROWS_Y + 16, :] = guard
    for ref in (edge_a, edge_b):
        ref[...] = jnp.zeros_like(ref)

    def place(x):
        group = (x + GROUP - HALO) // GROUP
        where = (x + GROUP - HALO) % GROUP * SLOT + slot_lane
        return pl.multiple_of(group * ROWS_Y + 8, 8), where

    def to_edge(edge, start, t, where, value):
        moved = pltpu.roll(value, (where - edge_lane + TILE) % TILE, 1)
        pltpu.store(edge.at[pl.ds(start + 8 * t, 8), :], moved, mask=lane == where)

    def z_sides(value, strips, start, t, where):
        outside = pltpu.roll(tile(strips, start, t), (edge_lane - where + TILE) % TILE, 1)
        up = jnp.where(lane == up_lane, outside, pltpu.roll(value, TILE - 1, 1))
        down = jnp.where(lane == low_lane, outside, pltpu.roll(value, 1, 1))
        return up, down

    def strip_sides(strips, edge, g, t):
        here = tile(strips, strip_base(g), t)
        following = tile(strips, strip_base(min(g + 1, GROUPS - 1)), t)
        previous = tile(strips, strip_base(max(g - 1, 0)), t)
        x_up = pltpu.roll(jnp.where(lane < SLOT, following, here), TILE - SLOT, 1)
        x_down = pltpu.roll(jnp.where(lane >= TILE - SLOT, previous, here), SLOT, 1)
        beyond = tile(edge, strip_base(g), t)
        z_up = jnp.where(open_up, beyond, pltpu.roll(here, TILE - 1, 1))
        z_down = jnp.where(open_low, beyond, pltpu.roll(here, 1, 1))
        y_up = tile(strips, strip_base(g), t, 1)
        y_down = tile(strips, strip_base(g), t, -1)
        return x_up, x_down, y_up, y_down, z_up, z_down

    def volume_edge(x):
        start, where = place(x)
        for t in row_tiles:
            to_edge(edge_a, start, t, where, tile(vol, base(x), t))

    loop(1, EXT - 1, volume_edge, 8)
    center = 0.5 * (UPPER_BOUND + LOWER_BOUND)
    halfwidth = 0.5 * (UPPER_BOUND - LOWER_BOUND)
    spread = center / halfwidth
    damping = 1.0 / spread
    for t in row_tiles:
        for ref in (sa, sb):
            put(ref, 0, t, guard)
            put(ref, (EXT - 1) * ROWS_Y, t, guard)
        put(ax, 0, t, jnp.minimum(tile(vol, 0, t), tile(vol, ROWS_Y, t)))
    put(ay, ROWS_Y - 8, 0, guard)

    def inverse_of(value):
        return jnp.where(value > 0.0, 1.0 / jnp.where(value > 0.0, value, 1.0), 0.0)

    closed_up = (lane == TILE - 1) & (lane != up_lane)
    closed_low = (lane == 0) & (lane != low_lane)

    def prepare(x):
        here = base(x)
        start, where = place(x)
        for t in row_tiles:
            v = tile(vol, here, t)
            upper = jnp.minimum(v, tile(vol, here + ROWS_Y, t))
            lower = jnp.minimum(v, tile(vol, here - ROWS_Y, t))
            z_up, z_down = z_sides(v, hvol, start, t, where)
            z_up = jnp.minimum(v, jnp.where(closed_up, 0.0, z_up))
            z_down = jnp.minimum(v, jnp.where(closed_low, 0.0, z_down))
            y_up = jnp.minimum(v, tile(vol, here, t, 1))
            y_down = jnp.minimum(v, tile(vol, here, t, -1))
            whole = SHIFT_WEIGHT * v + (upper + lower) + (y_up + y_down) + (z_up + z_down)
            scale = inverse_of(whole)
            for ref, value in ((ax, upper), (ay, y_up), (azu, z_up), (azl, z_down), (diag, whole), (inv, scale)):
                put(ref, here, t, value)
            search = (tile(res, here, t) * scale) * (1.0 / center)
            put(sa, here, t, search)
            put(total, here, t, search)
            to_edge(edge_b, start, t, where, search)

    loop(1, EXT - 1, prepare, 4)
    for g in range(GROUPS):
        for t in row_tiles:
            v = tile(hvol, strip_base(g), t)
            parts = [jnp.minimum(v, n) for n in strip_sides(hvol, edge_a, g, t)]
            whole = SHIFT_WEIGHT * v
            for value in parts:
                whole = whole + value
            scale = inverse_of(whole)
            for i, value in enumerate(parts + [whole, scale]):
                hcoef[i, g * ROWS_Y + 8 * t : g * ROWS_Y + 8 * t + 8, :] = value
            search = (tile(hres, strip_base(g), t) * scale) * (1.0 / center)
            put(hsa, strip_base(g), t, search)
            put(htotal, strip_base(g), t, search)

    now, then, hnow, hthen = sa, sb, hsa, hsb
    edge, edge_next = edge_b, edge_a
    for iteration in range(ITERS - 1):
        damping_next = 1.0 / (2.0 * spread - damping)
        keep = damping_next * damping
        push = 2.0 * damping_next / halfwidth
        damping = damping_next

        def iterate(x, now=now, then=then, hnow=hnow, edge_next=edge_next, keep=keep, push=push):
            here = base(x)
            start, where = place(x)
            for t in row_tiles:
                s = tile(now, here, t)
                z_up, z_down = z_sides(s, hnow, start, t, where)
                along_x = tile(ax, here, t) * tile(now, here + ROWS_Y, t)
                along_x = along_x + tile(ax, here - ROWS_Y, t) * tile(now, here - ROWS_Y, t)
                along_y = tile(ay, here, t) * tile(now, here, t, 1)
                along_y = along_y + tile(ay, here, t, -1) * tile(now, here, t, -1)
                along_z = tile(azu, here, t) * z_up + tile(azl, here, t) * z_down
                flow = along_x + along_y + along_z
                residual = tile(res, here, t) - (tile(diag, here, t) * s - flow)
                put(res, here, t, residual)
                search = keep * s + push * (residual * tile(inv, here, t))
                put(then, here, t, search)
                put(total, here, t, tile(total, here, t) + search)
                if edge_next is not None:
                    to_edge(edge_next, start, t, where, search)

        if iteration == ITERS - 2:
            iterate = functools.partial(iterate, edge_next=None)
        loop(1, EXT - 1, iterate, 4)
        for g in range(GROUPS):
            for t in row_tiles:
                rows_here = slice(g * ROWS_Y + 8 * t, g * ROWS_Y + 8 * t + 8)
                s = tile(hnow, strip_base(g), t)
                parts = [hcoef[i, rows_here, :] * v for i, v in enumerate(strip_sides(hnow, edge, g, t))]
                flow = (parts[0] + parts[1]) + (parts[2] + parts[3]) + (parts[4] + parts[5])
                residual = tile(hres, strip_base(g), t) - (hcoef[6, rows_here, :] * s - flow)
                put(hres, strip_base(g), t, residual)
                search = keep * s + push * (residual * hcoef[7, rows_here, :])
                put(hthen, strip_base(g), t, search)
                put(htotal, strip_base(g), t, tile(htotal, strip_base(g), t) + search)
        now, then, hnow, hthen = then, now, hthen, hnow
        edge, edge_next = edge_next, edge

    lanes = lane_index()

    def spread_boxes(pieces, row):
        for k in range(count):
            value = None
            for r in reversed(range(PER_TILE)):
                shift = (BOX * (r - k)) % TILE
                piece = pltpu.roll(pieces[r], shift, 1) if shift else pieces[r]
                value = piece if value is None else jnp.where(lanes < BOX * (r + 1), piece, value)
            packed[pl.ds(pl.multiple_of(k * RETURN_ROWS + row, 8), TILES), :] = value

    def core(i):
        start = (i + HALO - 1) * ROWS_Y + SIDE
        pieces = [total[pl.ds(start + r, TILES, stride=PER_TILE), :] for r in range(PER_TILE)]
        spread_boxes(pieces, i * TILES)

    loop(0, PADDED, core, 17)

    def output(i):
        pressure[i] = total[pl.ds(base(i + HALO) + SIDE, BOX), :]

    loop(0, BOX, output, 8)
    for f, y in enumerate((SIDE - 1, SIDE + BOX)):
        pieces = [
            total[pl.ds((HALO + r) * ROWS_Y + y, TILES, stride=PER_TILE * ROWS_Y), :]
            for r in range(PER_TILE)
        ]
        spread_boxes(pieces, PADDED * TILES + f * TILES)
    z_row = PADDED * TILES + 2 * TILES
    for k in (0, count - 1):
        packed[k * RETURN_ROWS + z_row : k * RETURN_ROWS + z_row + 2 * TILES, :] = jnp.zeros(
            (2 * TILES, TILE), jnp.float32
        )
    for block in range(TILES):
        for i in range(PER_TILE):
            for r in range(PER_TILE):
                start = (HALO + PER_TILE * block + i) * ROWS_Y + SIDE + r
                turned[BOX * r + TILES * i : BOX * r + TILES * (i + 1), :] = total[
                    pl.ds(start, TILES, stride=PER_TILE), :
                ]
        flat = turned[...].T
        for k in range(count):
            low = k * RETURN_ROWS + z_row + block
            if k:
                packed[low : low + 1, :] = flat[BOX * k - 1 : BOX * k, :]
            if k < count - 1:
                packed[low + TILES : low + TILES + 1, :] = flat[BOX * k + BOX : BOX * k + BOX + 1, :]
    half = GROUP // PER_TILE
    row4 = lax.broadcasted_iota(jnp.int32, (half, TILE), 1)
    box = jnp.where(at_top, count - 1, 0)
    target = box * RETURN_ROWS + z_row + jnp.where(at_top, TILES, 0)
    for g in range(1, GROUPS - 1):
        turned[...] = jnp.zeros_like(turned)
        for r in range(PER_TILE):
            turned[BOX * r : BOX * r + TILES, :] = htotal[
                pl.ds(strip_base(g) + SIDE + r, TILES, stride=PER_TILE), :
            ]
        turned[...] = turned[...].T
        value = None
        for i in range(PER_TILE):
            piece = turned[pl.ds(SLOT * i + slot_lane, half, stride=SLOT * PER_TILE), :]
            piece = pltpu.roll(piece, TILES * i, 1) if i else piece
            value = piece if value is None else jnp.where(row4 % BOX // TILES == i, piece, value)
        packed[pl.ds(target + (g - 1) * half, half), :] = value
    copies = [
        pltpu.make_async_copy(
            packed.at[pl.ds(pl.multiple_of(box_of_row[d] * RETURN_ROWS, 8), RETURN_ROWS)],
            rows.at[d],
            sem.at[d],
        )
        for d in range(lanes_by)
    ]
    for copy in copies:
        copy.start()
    for copy in copies:
        copy.wait()


def assemble_call(table, side, recv):
    count = table.shape[0]
    fixed = [
        (HALO * BOX, TILE),
        (HALO * BOX, TILE),
        (BOX // GROUP, BOX, TILE),
    ]

    def box_spec(k):
        return pl.BlockSpec((1, STEP_BRICK * TILES, TILE), lambda i, table, side: (table[k], i, 0))

    def fixed_spec(shape):
        return pl.BlockSpec(shape, lambda i, table, side: (0,) * len(shape))

    return pl.pallas_call(
        functools.partial(assemble_kernel, count=count),
        grid_spec=pltpu.PrefetchScalarGridSpec(
            num_scalar_prefetch=2,
            grid=(BOX // STEP_BRICK,),
            in_specs=[box_spec(k) for k in range(count)],
            out_specs=[pl.BlockSpec((STEP_BRICK * BOX, TILE), lambda i, table, side: (i, 0))]
            + [fixed_spec(shape) for shape in fixed],
        ),
        out_shape=[struct(BOX * BOX, TILE)] + [struct(*shape) for shape in fixed],
        compiler_params=pltpu.CompilerParams(vmem_limit_bytes=6 << 20),
        name="brick",
    )(table, side, *([recv] * count))


def halo(parts, depth):
    brick, first, last, strip = parts
    nx, ny = lax.axis_size("bx"), lax.axis_size("by")
    nz = lax.axis_size("bz")
    middle = lax.ppermute(strip, "bz", [(i, nz - 1 - i) for i in range(nz)])
    up = [(i, i + 1) for i in range(nx - 1)]
    down = [(j, i) for i, j in up]
    x_lo = lax.ppermute(jnp.concatenate([last, middle[-1]], axis=0), "bx", up)
    x_hi = lax.ppermute(jnp.concatenate([first, middle[0]], axis=0), "bx", down)
    cubes = [v.reshape(-1, BOX, TILE) for v in (x_lo, brick, middle, x_hi)]

    def edge(start):
        return jnp.concatenate([v[:, start : start + depth] for v in cubes], axis=0)

    y_up = [(i, i + 1) for i in range(ny - 1)]
    y_lo = lax.ppermute(edge(BOX - depth), "by", y_up)
    y_hi = lax.ppermute(edge(0), "by", [(j, i) for i, j in y_up])
    return brick, x_lo, x_hi, middle, y_lo, y_hi


def solve_call(box_of_row, side, count, volume, source):
    lanes_by = box_of_row.shape[0]
    wide = pltpu.VMEM((EXT * ROWS_Y, TILE), jnp.float32)
    narrow = pltpu.VMEM((GROUPS * ROWS_Y + 16, TILE), jnp.float32)
    return pl.pallas_call(
        functools.partial(solve_kernel, count=count, lanes_by=lanes_by),
        in_specs=[SMEM_SPEC, SMEM_SPEC] + [VMEM_SPEC] * 12,
        out_specs=[VMEM_SPEC, HBM_SPEC],
        out_shape=[struct(BOX, BOX, count * BOX), struct(lanes_by, RETURN_ROWS, TILE)],
        scratch_shapes=[wide] * 11
        + [narrow] * 7
        + [
            pltpu.VMEM((8, GROUPS * ROWS_Y, TILE), jnp.float32),
            pltpu.VMEM((TILE, TILE), jnp.float32),
            pltpu.VMEM((count * RETURN_ROWS, TILE), jnp.float32),
            pltpu.SemaphoreType.DMA((lanes_by,)),
        ],
        compiler_params=pltpu.CompilerParams(vmem_limit_bytes=26 << 20),
        name="solve",
    )(box_of_row, side, *volume, *source)


def routing(placement, capacity):
    lanes = lax.axis_size("by")
    own_index = lax.axis_index("by")
    table = placement[0, :, 0, :]
    per_brick = table.shape[1]
    entries = lanes * per_brick
    owners = table.reshape(entries)
    onehot = (owners[:, None] == jnp.arange(lanes, dtype=jnp.int32)[None, :]).astype(jnp.int32)
    ranks = jnp.sum((jnp.cumsum(onehot, axis=0) - onehot) * onehot, axis=1)
    matches = (table == own_index).astype(jnp.int32)
    send_slot = jnp.sum(matches * ranks.reshape(lanes, per_brick), axis=1)
    slot_match = (
        (owners == own_index)[:, None]
        & (ranks[:, None] == jnp.arange(capacity, dtype=jnp.int32)[None, :])
    ).astype(jnp.int32)
    row_value = jnp.arange(entries, dtype=jnp.int32) // per_brick
    slot_row = jnp.sum(slot_match * row_value[:, None], axis=0)
    brick_table = lax.dynamic_index_in_dim(table, own_index, 0, keepdims=False)
    all_rows = jnp.arange(lanes, dtype=jnp.int32)
    box_of_row = jnp.sum(
        (brick_table[None, :] == all_rows[:, None]).astype(jnp.int32)
        * jnp.arange(per_brick, dtype=jnp.int32)[None, :],
        axis=1,
    )
    return send_slot, slot_row, brick_table, box_of_row


def exchange(rows):
    return lax.all_to_all(rows, "by", split_axis=0, concat_axis=0, tiled=True)


def local(velocity, fraction, placement):
    send_slot, slot_row, brick_table, box_of_row = routing(placement, velocity.shape[0])
    own = lax.axis_index("by").reshape(1)
    table = placement.reshape(-1)
    volume_rows = volume_call(table, own, fraction, send_slot.shape[0])
    volume_recv = exchange(volume_rows)
    planes, masses, source_rows = flux_call(send_slot, jnp.swapaxes(velocity, 0, 1), fraction)
    source_recv = exchange(source_rows)
    updated, apertures = update_call(masses, planes)
    side = lax.axis_index("bz").reshape(1)
    volume = halo(assemble_call(brick_table, side, volume_recv), SIDE)
    source_recv, volume = lax.optimization_barrier((source_recv, volume))
    source = halo(assemble_call(brick_table, side, source_recv), ITERS)
    pressure, rows = solve_call(box_of_row, side, placement.shape[3], volume, source)
    returned = exchange(rows)
    corrected = correct_call(slot_row, updated, apertures, returned)
    return (jnp.swapaxes(corrected, 0, 1), pressure)


def solution(mesh):
    in_specs = (
        P(("bx", "by", "bz"), None, None),
        P(("bx", "by", "bz"), None),
        P("bx", None, "bz", None),
    )
    out_specs = (P(("bx", "by", "bz"), None, None), P("bx", "by", "bz"))
    return jax.shard_map(local, mesh=mesh, in_specs=in_specs, out_specs=out_specs, check_vma=False)
```
